32 devices in a mesh: table: 4 (over y, x), ctx: 8 (over z, core).
Axes of the slice: x: 2, y: 2, z: 4, core: 2. Of those that a mesh axis runs over, the one named last changes fastest.
Arguments:
- item_local: int32 [4, 2048], P('table', 'ctx'), may hold values from 0 to 511
- item_owner: int32 [4, 2048, 1], P('table', 'ctx'), may hold values from 0 to 3; in each aligned block of 256 rows (0 to 255, 256 to 511, ..., all dimensions but the last counted through in order) at most 128 rows name the same one
- hist_len: int32 [4], P('table'), may hold values from 512 to 2048, as said below
- table: bfloat16 [2048, 512], P('table'), may hold values from -6 to 6
- gain: float32 [512], replicated, may hold values from 0.1 to 1.9
- w_query: bfloat16 [512, 512], replicated, may hold values from -0.25 to 0.25
- w_key: bfloat16 [512, 512], replicated, may hold values from -0.25 to 0.25
- w_value: bfloat16 [512, 512], replicated, may hold values from -0.25 to 0.25
- w_out: bfloat16 [512, 512], replicated, may hold values from -0.25 to 0.25
- rate: float32 [8], replicated, may hold values from 0.0009765625 to 0.05
- d_out: bfloat16 [4, 2048, 512], P('table', 'ctx'), may hold values from -6 to 6
Outputs:
- output: bfloat16 [4, 2048, 512], P('table', 'ctx')
- table_grad: bfloat16 [2048, 512], P('table')
The draws below stay inside these ranges and needn't reach their ends.
Inputs may be any that keep to these rules, and one draw needn't show every extreme that they name: `item_owner`: among the 256 positions of one device at most 128 name the same owner, and some device's positions reach 128. `hist_len`: each length is a multiple of 64; some user's history fills all 2048 positions.
All inputs are finite; a program needn't handle non-finite values.
Results may differ from the reference program's by a relative error of at most 0.009.
Values may be sent and summed in bfloat16 or wider, within the bound.
No kernel may reach another device: no remote copies, remote signals or barrier semaphores. Data moves between devices by JAX's collectives and lax.ppermute only.
A program may use at most 64 MiB of HBM per device.

```python
import math
import jax
import jax.numpy as jnp
import numpy as np
from jax import lax

H = 8
D = 512
ROWS_DEV = 512
POS_DEV = 256
BLK = 64
USERS = 4
LEN = 2048
CAP = 128
VOCAB = 2048
N_TABLE = 4


def draw_hist_len(key, part):
    first_key = jax.random.fold_in(key, 11)
    second_key = jax.random.fold_in(key, 23)
    blocks = LEN // BLK
    counts = jax.random.randint(first_key, (USERS,), blocks // 4, blocks + 1)
    longest = jax.random.randint(second_key, (), 0, USERS)
    counts = jnp.where(jnp.arange(USERS, dtype=jnp.int32) == longest, blocks, counts)
    return (counts * BLK).astype(jnp.int32)


def place_ends(drawn, key, smallest, top_value):
    dims = drawn.shape
    place = [jax.random.randint(jax.random.fold_in(key, axis), (), 0, dims[axis]) for axis in range(len(dims))]
    drawn = drawn.at[tuple(place)].set(smallest)
    longest = dims.index(max(dims))
    place[longest] = (place[longest] + 1) % dims[longest]
    return drawn.at[tuple(place)].set(top_value)


def shard_levels(key, extent, cuts, least, high):
    loudness, own = 1.0, jax.random.fold_in(key, 6)
    for dim, parts in cuts:
        heights = jnp.exp(jax.random.uniform(jax.random.fold_in(own, dim), (parts,), jnp.float32, least / len(cuts), high / len(cuts)))
        loudness = loudness * jnp.repeat(heights, extent[dim] // parts).reshape([-1 if axis == dim else 1 for axis in range(len(extent))])
    return loudness


def rank_bounds(number_of, lean):
    portions = [(1 << 20) // math.isqrt(grade ** lean) + 1 for grade in range(1, number_of + 1)]
    scale = 1 + sum(portions) // (1 << 30)
    return np.cumsum(np.array([max(1, weight // scale) for weight in portions]))


def ranked(own_key, extent, number_of, lean):
    table = rank_bounds(number_of, lean)
    lot = jax.random.randint(jax.random.fold_in(own_key, 1), extent, 0, int(table[number_of - 1]))
    standing = jnp.searchsorted(jnp.asarray(table, jnp.int32), lot, side="right")
    return jax.random.permutation(jax.random.fold_in(own_key, 2), number_of)[standing].astype(jnp.int32)


def assign_block(own_key, own, number, rows, amount, top, bound, slope):
    sequence = jax.random.permutation(own_key, amount)
    heavy_load, ordinary = load_shares(amount, rows * top, bound, slope, True), load_shares(amount, rows * top, bound, slope, False)
    places = jnp.arange(amount)

    def named(sizes, rotation):
        used = int((sizes > 0).sum())
        fixed = max(1, used // 4)
        shifted = fixed + (places - fixed + rotation * (used - fixed)) % max(1, amount - fixed)
        return jnp.zeros((amount,), jnp.int32).at[sequence[jnp.where(places < fixed, places, shifted)]].set(jnp.asarray(sizes, jnp.int32))

    sizes = jnp.where(number % 4 == 0, named(heavy_load, number // 4), named(ordinary, number - number // 4 - 1))
    mixed = jax.random.permutation(jax.random.fold_in(own, 3), amount)
    donor, taker = mixed[0:amount // 2 * 2:2], mixed[1:amount // 2 * 2:2]
    margin = jnp.minimum(sizes[donor] - 1, bound - sizes[taker]) // 2
    margin = jnp.where((donor == sequence[0]) | (taker == sequence[0]) | (sizes[taker] == 0), 0, jnp.maximum(margin, 0))
    shifted = jax.random.randint(jax.random.fold_in(own, 4), (amount // 2,), 0, 1 << 20) % (margin + 1)
    sizes = sizes.at[donor].add(-shifted).at[taker].add(shifted)
    labels = jnp.searchsorted(jnp.cumsum(sizes), jnp.arange(rows * top), side="right").astype(jnp.int32)
    table = labels.reshape(top, rows).T
    table = table[jax.random.permutation(jax.random.fold_in(own, 1), rows)]
    rotation = jax.random.randint(jax.random.fold_in(own, 2), (rows, 1), 0, top)
    return jnp.take_along_axis(table, (jnp.arange(top)[None, :] + rotation) % top, axis=1)


def load_shares(amount, total, most, slope, full):
    weights = [(1 << 20) // math.isqrt(grade ** slope) + 1 for grade in range(1, amount + 1)]
    largest = most if full else min(most, max(-(-total // amount), total * weights[0] // sum(weights)))
    least = 1 if total - largest >= amount - 1 else 0
    holding, rest = [largest] + [least] * (amount - 1), total - largest - least * (amount - 1)
    while rest > 0:
        free = [i for i in range(1, amount) if holding[i] < largest] or [i for i in range(1, amount) if holding[i] < most]
        pool, remaining = sum([weights[i] for i in free]), rest
        for i in free:
            extra = min(most - holding[i], max(1, remaining * weights[i] // pool), rest)
            holding[i] = holding[i] + extra
            rest = rest - extra
    return np.array(holding)


def centred(rng, shape, scale, limit, pieces=(), kind=jnp.bfloat16):
    array = jax.random.normal(rng, shape, jnp.float32) * scale
    if len(pieces) > 0:
        array = shard_levels(rng, shape, pieces, -0.22, 0.18) * array
    return jnp.clip(array, min=-limit, max=limit).astype(kind)


def setup_inputs(seed: int = 0) -> dict:
    keys = jax.random.split(jax.random.key(seed), 12)
    item_local = place_ends(ranked(keys[0], (USERS, LEN), ROWS_DEV, 2), jax.random.fold_in(keys[0], 3), 0, ROWS_DEV - 1).astype(jnp.int32)
    item_owner_keys = jax.random.split(jax.random.fold_in(keys[1], 1), USERS * LEN // POS_DEV)
    item_owner_turns = jax.random.permutation(jax.random.fold_in(keys[1], 3), USERS * LEN // POS_DEV)
    item_owner = jax.vmap(lambda own, number: assign_block(jax.random.fold_in(keys[1], 2), own, number, POS_DEV, N_TABLE, 1, CAP, 2))(item_owner_keys, item_owner_turns).reshape((USERS, LEN, 1))
    hist_len = draw_hist_len(jax.random.fold_in(keys[11], 71), 0)
    table = centred(keys[3], (VOCAB, D), 1.0, 6.0, ((0, 4),))
    gain = jnp.clip(1.0 + 0.18 * jax.random.normal(keys[4], (D,), jnp.float32), 0.1, 1.9)
    w_query = centred(keys[5], (D, D), D ** -0.5, 0.25)
    w_key = centred(keys[6], (D, D), D ** -0.5, 0.25)
    w_value = centred(keys[7], (D, D), D ** -0.5, 0.25)
    w_out = centred(keys[8], (D, D), D ** -0.5, 0.25)
    rate = jnp.clip(jnp.exp(jax.random.uniform(keys[9], (H,), jnp.float32, math.log(0.0009765625), math.log(0.05))), 0.0009765625, 0.05)
    d_out = centred(keys[10], (USERS, LEN, D), 1.0, 6.0, ((0, 4), (1, 8)))
    return dict(item_local=item_local, item_owner=item_owner, hist_len=hist_len, table=table, gain=gain, w_query=w_query, w_key=w_key, w_value=w_value, w_out=w_out, rate=rate, d_out=d_out)


EPS = 1e-06
HIGHEST = lax.Precision.HIGHEST

def inv_rms(tensor):
    return lax.rsqrt(lax.optimization_barrier(jnp.mean(tensor * tensor, axis=-1, keepdims=True)) + EPS)

def norm_back(tensor, factor, upstream, scale):
    return scale * factor * (upstream - tensor * factor * factor * lax.optimization_barrier(jnp.mean(tensor * upstream, axis=-1, keepdims=True)))

def precise(form, left, right):
    return jnp.einsum(form, left, right, precision=HIGHEST)

def back_dot(upstream, matrix):
    return lax.dot_general(upstream, matrix, (((1,), (1,)), ((), ())), preferred_element_type=jnp.float32)

def decay_tables(rate, length):
    position = jnp.arange(length, dtype=jnp.float32)
    distance = position[:, None] - position[None, :]
    within = jnp.where(distance[None] >= 0.0, jnp.exp(-rate[:, None, None] * jnp.maximum(distance, 0.0)[None]), 0.0)
    entering = jnp.exp(-rate[None, :] * (position[:, None] + 1.0))
    leaving = jnp.exp(-rate[None, :] * (length - 1.0 - position[:, None]))
    return (within, entering, leaving)

def attention_pass(queries, keys_unit, values_in, grad_out, state_in, adjoint_in, within, entering, leaving):
    scores = precise('thd,shd->hts', queries, keys_unit) * within
    attended = precise('hts,shd->thd', scores, values_in) + entering[:, :, None] * precise('thi,hij->thj', queries, state_in)
    pair_grads = precise('thd,shd->hts', grad_out, values_in) * within
    grad_queries = precise('hts,shd->thd', pair_grads, keys_unit) + entering[:, :, None] * precise('thj,hij->thi', grad_out, state_in)
    grad_keys = precise('hts,thd->shd', pair_grads, queries) + leaving[:, :, None] * precise('shj,hij->shi', values_in, adjoint_in)
    grad_values = precise('hts,thd->shd', scores, grad_out) + leaving[:, :, None] * precise('shi,hij->shj', keys_unit, adjoint_in)
    return (attended, grad_queries, grad_keys, grad_values)

def group_states(queries, keys_unit, values_in, grad_out, entering, leaving):
    carried = precise('shi,shj->hij', keys_unit * leaving[:, :, None], values_in)
    adjoint = precise('thi,thj->hij', queries * entering[:, :, None], grad_out)
    return (carried, adjoint)

def block_sums(ids_block, grads_block):
    count = ids_block.shape[0]
    order = jnp.arange(count, dtype=jnp.int32)
    same = ids_block[:, None] == ids_block[None, :]
    earlier = jnp.any(same & (order[None, :] < order[:, None]), axis=1)
    summed = jnp.dot(same.astype(jnp.float32), grads_block, precision=HIGHEST)
    return jnp.where(earlier[:, None], jnp.zeros_like(summed), summed)

def reference(item_local, item_owner, hist_len, table, gain, w_query, w_key, w_value, w_out, rate, d_out):
    width = table.shape[1]
    heads = rate.shape[0]
    head_size = width // heads
    blocks = LEN // POS_DEV
    key_scale = 1.0 / math.sqrt(head_size)
    row_ids = (item_owner[:, :, 0] * ROWS_DEV + item_local).astype(jnp.int32)
    within, entering, leaving = decay_tables(rate, POS_DEV)
    block_decay = jnp.exp(-rate * POS_DEV)

    def user_pass(row_user, length_user, grad_user):
        embedded = jnp.take(table, row_user, axis=0)
        validity = (jnp.arange(LEN, dtype=jnp.int32) < length_user).astype(jnp.float32)[:, None]
        mask_heads = validity[:, :, None]
        inputs_f = embedded.astype(jnp.float32)
        rstd = inv_rms(inputs_f)
        normed = (inputs_f * rstd * gain).astype(jnp.bfloat16)
        query_raw = jnp.dot(normed, w_query, preferred_element_type=jnp.float32).reshape(LEN, heads, head_size)
        key_raw = jnp.dot(normed, w_key, preferred_element_type=jnp.float32).reshape(LEN, heads, head_size)
        value_raw = jnp.dot(normed, w_value, preferred_element_type=jnp.float32).reshape(LEN, heads, head_size)
        query_rms = inv_rms(query_raw)
        key_rms = inv_rms(key_raw)
        queries = query_raw * query_rms / head_size
        keys_unit = key_raw * key_rms * key_scale * mask_heads
        values_in = value_raw * mask_heads
        grad_masked = grad_user * validity.astype(jnp.bfloat16)
        grad_out = back_dot(grad_masked, w_out).reshape(LEN, heads, head_size)
        shape_blocks = (blocks, POS_DEV, heads, head_size)
        query_blocks = queries.reshape(shape_blocks)
        key_blocks = keys_unit.reshape(shape_blocks)
        value_blocks = values_in.reshape(shape_blocks)
        grad_blocks = grad_out.reshape(shape_blocks)
        carried, adjoint = jax.vmap(lambda a, b, c, e: group_states(a, b, c, e, entering, leaving))(query_blocks, key_blocks, value_blocks, grad_blocks)
        zero_state = jnp.zeros((heads, head_size, head_size), jnp.float32)

        def step_forward(state_now, piece):
            return (block_decay[:, None, None] * state_now + piece, state_now)

        def step_reverse(state_now, piece):
            return (piece + block_decay[:, None, None] * state_now, state_now)
        _, state_in = lax.scan(step_forward, zero_state, carried)
        _, adjoint_in = lax.scan(step_reverse, zero_state, adjoint, reverse=True)
        attended, grad_queries, grad_keys, grad_values = lax.map(lambda pack: attention_pass(pack[0], pack[1], pack[2], pack[3], pack[4], pack[5], within, entering, leaving), (query_blocks, key_blocks, value_blocks, grad_blocks, state_in, adjoint_in))
        shape_whole = (LEN, heads, head_size)
        attended_b = attended.reshape(LEN, width).astype(jnp.bfloat16)
        output = (inputs_f + jnp.dot(attended_b, w_out, preferred_element_type=jnp.float32)).astype(jnp.bfloat16)
        d_query = norm_back(query_raw, query_rms, grad_queries.reshape(shape_whole), 1.0 / head_size).reshape(LEN, width).astype(jnp.bfloat16)
        d_key = (mask_heads * norm_back(key_raw, key_rms, grad_keys.reshape(shape_whole), key_scale)).reshape(LEN, width).astype(jnp.bfloat16)
        d_value = (mask_heads * grad_values.reshape(shape_whole)).reshape(LEN, width).astype(jnp.bfloat16)
        d_normed = back_dot(d_query, w_query) + back_dot(d_key, w_key) + back_dot(d_value, w_value)
        row_grad = grad_masked.astype(jnp.float32) + norm_back(inputs_f, rstd, d_normed * gain, 1.0)
        block_grad = lax.map(lambda pack: block_sums(pack[0], pack[1]), (row_user.reshape(blocks, POS_DEV), row_grad.reshape(blocks, POS_DEV, width)))
        return (output, block_grad.reshape(LEN, width))

    def per_user(totals, pack):
        output, block_grad = user_pass(pack[0], pack[1], pack[2])
        totals = totals.at[pack[0]].add(block_grad)
        return (totals, output)
    totals, outputs = lax.scan(per_user, jnp.zeros((VOCAB, table.shape[1]), jnp.float32), (row_ids, hist_len, d_out))
    return (outputs, totals.astype(jnp.bfloat16))
```

```python
import functools
import math

import jax
import jax.numpy as jnp
from jax import lax
from jax.experimental import pallas as pl
from jax.experimental.pallas import tpu as pltpu
from jax.sharding import PartitionSpec as P

EPS = 1e-06
F32 = jnp.float32
BF16 = jnp.bfloat16
MIB = 1 << 20


def dot(left, right, ways=(1, 0)):
    return lax.dot_general(
        left, right, (((ways[0],), (ways[1],)), ((), ())), preferred_element_type=F32
    )


def dot_nt(left, right):
    return dot(left, right, (1, 1))


def dot_tn(left, right):
    return dot(left, right, (0, 0))


def call(body, info, operands, specs, outs, flops, name):
    whole = [
        pl.BlockSpec(x.shape, functools.partial(lambda n, i, s: (0,) * n, x.ndim))
        if spec is None
        else spec
        for x, spec in zip(operands, specs)
    ]
    moved = sum(math.prod(x.shape) * x.dtype.itemsize for x in (*operands, *outs))
    return pl.pallas_call(
        body,
        grid_spec=pltpu.PrefetchScalarGridSpec(
            num_scalar_prefetch=1,
            grid=(1,),
            in_specs=whole,
            out_specs=[
                pl.BlockSpec(o.shape, functools.partial(lambda n, i, s: (0,) * n, len(o.shape)))
                for o in outs
            ],
        ),
        out_shape=outs,
        compiler_params=pltpu.CompilerParams(vmem_limit_bytes=56 * MIB),
        cost_estimate=pl.CostEstimate(flops=flops, bytes_accessed=moved, transcendentals=0),
        name=name,
    )(info, *operands)


def iota(shape, dim):
    return lax.broadcasted_iota(jnp.int32, shape, dim)


def head_of(shape, dim, size):
    return iota(shape, dim) // size


def valid_col(info, offset, length):
    position = offset + iota((length, 1), 0)
    return (position < info[3]).astype(F32)


def decay(rate, offset, length, chip):
    centre = (chip - 1) / 2.0
    moment = (offset + iota((length, rate.shape[1]), 0)).astype(F32) - centre
    return jnp.exp(-rate * moment), jnp.exp(rate * moment)


def prepare(length, tables, rows, cap, info, d_own, d_oth, w_out, ids_col, ids_row, g, dest, meta):
    mine, core, z = info[0], info[1], info[2]
    for j, d_ref in enumerate((d_own, d_oth)):
        side = core if j == 0 else 1 - core
        valid = valid_col(info, (2 * z + side) * length, length)
        g[j] = (dot_nt(d_ref[...], w_out[...]) * valid).astype(BF16)
        column = ids_col[j]
        row = ids_row[j : j + 1, :]
        owner_row = row // rows
        local_row = row - owner_row * rows
        order = iota((length, length), 0) < iota((length, length), 1)
        same = jnp.where((column // rows == owner_row) & order, 1.0, 0.0)
        slot = jnp.sum(same, axis=0, keepdims=True).astype(jnp.int32)
        where_to = (owner_row ^ mine) * cap + slot
        dest[j : j + 1, :] = where_to
        high = local_row // 32
        pick = iota((16, length), 0)
        coded = jnp.where(
            pick == 0, high + 1, jnp.where(pick == 1, local_row - high * 32, 0)
        )
        coded = coded.astype(F32).astype(BF16)
        for m in range(tables):
            hit = iota((cap, length), 0) + m * cap == where_to
            hit = jnp.where(hit, 1.0, 0.0).astype(BF16)
            meta[m, j] = dot_nt(coded, hit).astype(BF16)


def project(
    length, tables, rows, size, chips, info, ids_col, gain, w_q, w_k, w_v, g, rate, table, *refs
):
    parts, outs = refs[: 2 * (tables - 1)], refs[2 * (tables - 1) :]
    emb, q_raw, k_raw, v_out = outs[:4]
    sends = outs[4:]
    mine, core, z = info[0], info[1], info[2]
    half = w_q.shape[1]
    part = rows // 2
    blocks = [(table, mine * rows)]
    for m in range(1, tables):
        blocks.append((parts[m - 1], (mine ^ m) * rows + core * part))
        blocks.append((parts[tables - 1 + m - 1], (mine ^ m) * rows + (1 - core) * part))
    mean_of = jnp.where(
        head_of((half, half), 0, size) == head_of((half, half), 1, size), 1.0 / size, 0.0
    ).astype(BF16)
    carried = jnp.zeros((half, half), F32)
    adjoint = jnp.zeros((half, half), F32)
    for j in range(2):
        side = core if j == 0 else 1 - core
        column = ids_col[j]
        x = jnp.zeros((length, table.shape[1]), F32)
        for ref, base in blocks:
            count = ref.shape[0]
            hit = column - base == iota((length, count), 1)
            x = x + dot(jnp.where(hit, 1.0, 0.0).astype(BF16), ref[...])
        emb[j] = x.astype(BF16)
        rstd = lax.rsqrt(jnp.mean(x * x, axis=1, keepdims=True) + EPS)
        normed = (x * rstd * gain[...]).astype(BF16)
        valid = valid_col(info, (2 * z + side) * length, length)
        qr = dot(normed, w_q[...])
        kr = dot(normed, w_k[...])
        v = (dot(normed, w_v[...]) * valid).astype(BF16)
        q_raw[j] = qr.astype(BF16)
        k_raw[j] = kr.astype(BF16)
        v_out[j] = v
        falling, rising = decay(rate[...], side * length, length, 2 * length)
        q_rms = lax.rsqrt(dot((qr * qr).astype(BF16), mean_of) + EPS)
        k_rms = lax.rsqrt(dot((kr * kr).astype(BF16), mean_of) + EPS)
        qa = (qr * q_rms * falling / size).astype(BF16)
        kb = (kr * k_rms * rising * (valid / math.sqrt(size))).astype(BF16)
        carried = carried + dot_tn(kb, v)
        adjoint = adjoint + dot_tn(qa, g[j])
    lane_head = head_of((size, half), 1, size)

    def packed(full):
        return sum(
            jnp.where(lane_head == h, full[h * size : (h + 1) * size, :], 0.0)
            for h in range(half // size)
        )

    carried, adjoint = packed(carried), packed(adjoint)
    for bit, ref in enumerate(sends):
        low = ((z >> bit) & 1) == 0
        ref[...] = jnp.where(low, carried, adjoint).astype(BF16)


def scaled_inputs(length, size, info, j, rate, mean_of, q_raw, k_raw, v, g):
    core, z = info[1], info[2]
    side = core if j == 0 else 1 - core
    valid = valid_col(info, (2 * z + side) * length, length)
    falling, rising = decay(rate[...], side * length, length, 2 * length)
    qr = q_raw[j].astype(F32)
    kr = k_raw[j].astype(F32)
    q_rms = lax.rsqrt(dot((qr * qr).astype(BF16), mean_of) + EPS)
    k_rms = lax.rsqrt(dot((kr * kr).astype(BF16), mean_of) + EPS)
    qn = qr * q_rms
    kn = kr * k_rms * valid
    q = qn / size
    k = kn / math.sqrt(size)
    qa = (q * falling).astype(BF16)
    kb = (k * rising).astype(BF16)
    ga = (g[j].astype(F32) * falling).astype(BF16)
    vb = (v[j].astype(F32) * rising).astype(BF16)
    return qn, kn, q_rms, k_rms, q, k, qa, kb, ga, vb, valid


def attend(length, size, info, rate, q_raw, k_raw, v_in, g_in, att, gq, gk, gv):
    core = info[1]
    half = q_raw.shape[2]
    same_head = head_of((half, half), 0, size) == head_of((half, half), 1, size)
    mean_of = jnp.where(same_head, 1.0 / size, 0.0).astype(BF16)
    lane_head = head_of((length, half), 1, size)
    causal = iota((length, length), 0) >= iota((length, length), 1)
    anti = iota((length, length), 0) <= iota((length, length), 1)
    kept, states = [], []
    for j in range(2):
        _, _, _, _, q, k, qa, kb, ga, vb, _ = scaled_inputs(
            length, size, info, j, rate, mean_of, q_raw, k_raw, v_in, g_in
        )
        v, g = v_in[j], g_in[j]
        q, k = q.astype(BF16), k.astype(BF16)
        kept.append((qa, kb, ga, vb))
        states.append(
            (
                jnp.where(same_head, dot_tn(kb, v), 0.0),
                jnp.where(same_head, dot_tn(qa, g), 0.0),
            )
        )
        zero = jnp.zeros_like(v)
        sums = [jnp.zeros((length, half), F32) for _ in range(4)]
        for h in range(half // size):
            mine = lane_head == h

            def only(tensor):
                return jnp.where(mine, tensor, zero)

            def pairs(left, right, mask):
                return jnp.where(mask, dot_nt(only(left), right), 0.0).astype(BF16)

            sums[0] += dot(pairs(qa, kb, causal), only(v))
            sums[1] += dot(pairs(ga, vb, causal), only(k))
            sums[2] += dot(pairs(vb, ga, anti), only(q))
            sums[3] += dot(pairs(kb, qa, anti), only(g))
        kept[j] += (sums,)
    for j in range(2):
        qa, kb, ga, vb, sums = kept[j]
        later = (core if j == 0 else 1 - core).astype(F32)
        state = (states[1 - j][0] * later).astype(BF16)
        back = (states[1 - j][1] * (1.0 - later)).astype(BF16)
        att[j] = (sums[0] + dot(qa, state)).astype(BF16)
        gq[j] = (sums[1] + dot_nt(ga, state)).astype(BF16)
        gk[j] = (sums[2] + dot_nt(vb, back)).astype(BF16)
        gv[j] = (sums[3] + dot(kb, back)).astype(BF16)


def finish(
    length, size, chips, info, rate, q_raw, k_raw, v_in, g_in, att, gq, gk, gv,
    emb, gain, w_q, w_k, w_v, d_own, d_oth, *refs
):
    came, (att_own, att_oth, row_keep, row_send) = refs[: chips - 1], refs[chips - 1 :]
    core, z = info[1], info[2]
    half = q_raw.shape[2]
    same_head = head_of((half, half), 0, size) == head_of((half, half), 1, size)
    mean_of = jnp.where(same_head, 1.0 / size, 0.0).astype(BF16)
    state = jnp.zeros((size, half), F32)
    back = jnp.zeros((size, half), F32)
    for m in range(1, chips):
        peer = z ^ m
        apart = jnp.abs(peer - z).astype(F32) * (2.0 * length)
        piece = came[m - 1][...].astype(F32) * jnp.exp(-rate[...] * apart)
        before = peer < z
        state = state + jnp.where(before, piece, 0.0)
        back = back + jnp.where(before, 0.0, piece)

    def spread(packed):
        return jnp.where(same_head, jnp.concatenate([packed] * (half // size), 0), 0.0).astype(BF16)

    state, back = spread(state), spread(back)
    keep_at = pl.multiple_of(core * half, half)
    send_at = pl.multiple_of((1 - core) * half, half)
    for j, d_ref in enumerate((d_own, d_oth)):
        qn, kn, q_rms, k_rms, _, _, qa, kb, ga, vb, valid = scaled_inputs(
            length, size, info, j, rate, mean_of, q_raw, k_raw, v_in, g_in
        )
        attended = (att[j].astype(F32) + dot(qa, state)).astype(BF16)
        (att_own if j == 0 else att_oth)[...] = attended
        grad_q = gq[j].astype(F32) + dot_nt(ga, state)
        grad_k = gk[j].astype(F32) + dot_nt(vb, back)
        grad_v = gv[j].astype(F32) + dot(kb, back)
        d_q = q_rms / size * (grad_q - qn * dot((qn * grad_q).astype(BF16), mean_of))
        d_k = k_rms * (valid / math.sqrt(size)) * (
            grad_k - kn * dot((kn * grad_k).astype(BF16), mean_of)
        )
        d_q, d_k, d_v = d_q.astype(BF16), d_k.astype(BF16), (grad_v * valid).astype(BF16)
        x = emb[j].astype(F32)
        rstd = lax.rsqrt(jnp.mean(x * x, axis=1, keepdims=True) + EPS)
        scaled = []
        total = jnp.zeros((length, 1), F32)
        for at in (keep_at, send_at):
            rows = pl.ds(at, half)
            d_normed = dot_nt(d_q, w_q[rows, :]) + dot_nt(d_k, w_k[rows, :]) + dot_nt(d_v, w_v[rows, :])
            d_normed = d_normed * gain[:, rows]
            part = emb[j, :, rows].astype(F32)
            scaled.append((d_normed, part))
            total = total + jnp.sum(d_normed * part, axis=1, keepdims=True)
        pull = total * (rstd * rstd / (2 * half))
        kept = rstd * (scaled[0][0] - scaled[0][1] * pull)
        row_keep[j] = kept + d_ref[:, pl.ds(keep_at, half)].astype(F32) * valid
        row_send[1 - j] = (rstd * (scaled[1][0] - scaled[1][1] * pull)).astype(BF16)


def compact(length, tables, cap, info, row_keep, row_came, dest, meta, *outs):
    for j in range(2):
        grads = (row_keep[j] + row_came[j].astype(F32)).astype(BF16)
        where_to = dest[j : j + 1, :]
        for m in range(tables):
            hit = iota((cap, length), 0) + m * cap == where_to
            hit = jnp.where(hit, 1.0, 0.0).astype(BF16)
            outs[m][j * cap : (j + 1) * cap, :] = dot(hit, grads).astype(BF16)
    for m in range(tables):
        for j in range(2):
            base = 2 * cap + 16 * j
            outs[m][base : base + 16, :] = jnp.zeros((16, outs[m].shape[1]), BF16)
            outs[m][base : base + 16, 0:cap] = meta[m, j]


def result(info, emb, att_own, att_came, w_out, out):
    core = info[1]
    half = att_own.shape[1]
    own = pl.ds(pl.multiple_of(core * half, half), half)
    other = pl.ds(pl.multiple_of((1 - core) * half, half), half)
    total = dot(att_own[...], w_out[own, :]) + dot(att_came[...], w_out[other, :])
    out[...] = (emb[0].astype(F32) + total).astype(BF16)


def owner_sum(tables, rows, cap, chips, info, *refs):
    came, outs, acc = refs[:tables], refs[tables : tables + chips], refs[tables + chips]
    z = info[2]
    total = None
    for m in range(tables):
        for j in range(2):
            base = 2 * cap + 16 * j
            coded = came[m][base : base + 16, 0:cap].astype(F32)
            number = ((coded[0:1, :] - 1.0) * 32.0 + coded[1:2, :]).astype(jnp.int32)
            hit = jnp.where(iota((rows, cap), 0) == number, 1.0, 0.0).astype(BF16)
            part = dot(hit, came[m][j * cap : (j + 1) * cap, :])
            total = part if total is None else total + part
    acc[...] = total
    share = rows // chips
    for m in range(chips):
        at = pl.multiple_of((z ^ m) * share, share)
        outs[m][...] = acc[pl.ds(at, share), :].astype(BF16)


def add_up(chips, info, *refs):
    total = refs[0][...].astype(F32)
    for m in range(1, chips):
        total = total + refs[m][...].astype(F32)
    refs[chips][...] = total.astype(BF16)


def assemble(chips, share, half, info, *refs):
    own, other, out, sem = refs[:chips], refs[chips : 2 * chips], refs[2 * chips], refs[2 * chips + 1]
    core, z = info[1], info[2]
    copies = []
    for m in range(chips):
        rows = pl.ds(pl.multiple_of((z ^ m) * share, share), share)
        for n, (ref, side) in enumerate(((own[m], core), (other[m], 1 - core))):
            columns = pl.ds(pl.multiple_of(side * half, half), half)
            copies.append(
                pltpu.make_async_copy(ref, out.at[rows, columns], sem.at[2 * m + n])
            )
    for copy in copies:
        copy.start()
    for copy in copies:
        copy.wait()


def local(
    item_local, item_owner, hist_len, table, gain, w_query, w_key, w_value, w_out, rate, d_out
):
    tables = lax.axis_size("table")
    count = lax.axis_size("ctx")
    length = item_local.shape[1]
    rows, width = table.shape
    heads = rate.shape[0]
    size = width // heads
    half = width // 2
    chips = count // 2
    cap = 2 * length // tables
    mine = lax.axis_index("table")
    block = lax.axis_index("ctx")
    core = block % 2
    z = block // 2

    def over_table(x, m):
        return lax.ppermute(x, "table", [(i, i ^ m) for i in range(tables)])

    def over_z(x, m):
        return lax.ppermute(x, "ctx", [(i, i ^ (2 * m)) for i in range(count)])

    def swap(x):
        return lax.ppermute(x, "ctx", [(i, i ^ 1) for i in range(count)])

    def array(shape, dtype):
        return jax.ShapeDtypeStruct(shape, dtype)

    info = jnp.stack([mine, core, z, hist_len[0]]).astype(jnp.int32)
    part = rows // 2
    part_own = lax.dynamic_slice(table, (core * part, 0), (part, width))
    parts = [over_table(part_own, m) for m in range(1, tables)]
    parts_other = [swap(p) for p in parts]

    ids = item_owner[:, :, 0] * rows + item_local
    ids_row = jnp.concatenate([ids, swap(ids)], 0)
    ids_col = ids_row[:, :, None]
    d_own = d_out[0]
    d_oth = swap(d_own)
    gain_row = gain[None, :]
    rate_row = lax.dynamic_slice(jnp.repeat(rate, size), (core * half,), (half,))[None, :]

    column_half = pl.BlockSpec((width, half), lambda i, s: (0, s[1]))
    row_half = pl.BlockSpec((half, width), lambda i, s: (s[1], 0))

    g, dest, meta = call(
        functools.partial(prepare, length, tables, rows, cap),
        info,
        (d_own, d_oth, w_out, ids_col, ids_row),
        (None, None, row_half, None, None),
        [
            array((2, length, half), BF16),
            array((2, length), jnp.int32),
            array((tables, 2, 16, cap), BF16),
        ],
        4 * length * width * half,
        "prepare",
    )
    bits = max(chips - 1, 1).bit_length() if chips > 1 else 0
    emb, q_raw, k_raw, v, *sends = call(
        functools.partial(project, length, tables, rows, size, chips),
        info,
        (ids_col, gain_row, w_query, w_key, w_value, g, rate_row, table, *parts, *parts_other),
        (None, None, column_half, column_half, column_half) + (None,) * (3 + 2 * (tables - 1)),
        [array((2, length, width), BF16)]
        + [array((2, length, half), BF16)] * 3
        + [array((size, half), BF16)] * bits,
        4 * length * tables * rows * width,
        "project",
    )
    came = [over_z(sends[m.bit_length() - 1], m) for m in range(1, chips)]
    att, gq, gk, gv = call(
        functools.partial(attend, length, size),
        info,
        (rate_row, q_raw, k_raw, v, g),
        (None,) * 5,
        [array((2, length, half), BF16)] * 4,
        32 * length * length * half,
        "attend",
    )
    att_own, att_oth, row_keep, row_send = call(
        functools.partial(finish, length, size, chips),
        info,
        (rate_row, q_raw, k_raw, v, g, att, gq, gk, gv, emb, gain_row, w_query, w_key, w_value,
         d_own, d_oth, *came),
        (None,) * 11 + (column_half,) * 3 + (None,) * (2 + chips - 1),
        [array((length, half), BF16)] * 2
        + [array((2, length, half), F32), array((2, length, half), BF16)],
        12 * length * width * half,
        "finish",
    )
    row_came = swap(row_send)
    att_came = swap(att_oth)
    outgoing = call(
        functools.partial(compact, length, tables, cap),
        info,
        (row_keep, row_came, dest, meta),
        (None,) * 4,
        [array((2 * cap + 32, half), BF16)] * tables,
        4 * length * 2 * length * half,
        "compact",
    )
    arrived = [outgoing[0]] + [over_table(outgoing[m], m) for m in range(1, tables)]
    (output,) = call(
        result,
        info,
        (emb, att_own, att_came, w_out),
        (pl.BlockSpec((1, length, width), lambda i, s: (0, 0, 0)), None, None, None),
        [array((length, width), BF16)],
        2 * length * width * width,
        "result",
    )
    share = rows // chips
    everything = pl.pallas_call(
        functools.partial(owner_sum, tables, rows, cap, chips),
        grid_spec=pltpu.PrefetchScalarGridSpec(
            num_scalar_prefetch=1,
            grid=(1,),
            in_specs=[pl.BlockSpec(x.shape, lambda i, s: (0, 0)) for x in arrived],
            out_specs=[pl.BlockSpec((share, half), lambda i, s: (0, 0))] * chips,
            scratch_shapes=[pltpu.VMEM((rows, half), F32)],
        ),
        out_shape=[array((share, half), BF16)] * chips,
        compiler_params=pltpu.CompilerParams(vmem_limit_bytes=56 * MIB),
        cost_estimate=pl.CostEstimate(
            flops=4 * rows * length * tables * half, bytes_accessed=MIB, transcendentals=0
        ),
        name="owner_sum",
    )(info, *arrived)
    pieces = [everything[0]] + [over_z(everything[m], m) for m in range(1, chips)]
    (summed,) = call(
        functools.partial(add_up, chips),
        info,
        pieces,
        (None,) * chips,
        [array((share, half), BF16)],
        chips * share * half,
        "add_up",
    )
    own = [summed] + [over_z(summed, m) for m in range(1, chips)]
    other = [swap(x) for x in own]
    table_grad = pl.pallas_call(
        functools.partial(assemble, chips, share, half),
        grid_spec=pltpu.PrefetchScalarGridSpec(
            num_scalar_prefetch=1,
            grid=(1,),
            in_specs=[pl.BlockSpec(memory_space=pl.ANY)] * (2 * chips),
            out_specs=pl.BlockSpec(memory_space=pl.ANY),
            scratch_shapes=[pltpu.SemaphoreType.DMA((2 * chips,))],
        ),
        out_shape=array((rows, width), BF16),
        name="assemble",
    )(info, *own, *other)
    return (output[None], table_grad)


def solution(mesh):
    return jax.shard_map(
        local,
        mesh=mesh,
        in_specs=(
            P("table", "ctx"),
            P("table", "ctx", None),
            P("table"),
            P("table", None),
            P(),
            P(),
            P(),
            P(),
            P(),
            P(),
            P("table", "ctx", None),
        ),
        out_specs=(P("table", "ctx", None), P("table", None)),
        check_vma=False,
    )
```

```python
import functools
import math

import jax
import jax.numpy as jnp
from jax import lax
from jax.experimental import pallas as pl
from jax.experimental.pallas import tpu as pltpu
from jax.sharding import PartitionSpec as P

EPS = 1e-06
F32 = jnp.float32
BF16 = jnp.bfloat16
MIB = 1 << 20


def dot(left, right, ways=(1, 0)):
    return lax.dot_general(
        left, right, (((ways[0],), (ways[1],)), ((), ())), preferred_element_type=F32
    )


def dot_nt(left, right):
    return dot(left, right, (1, 1))


def dot_tn(left, right):
    return dot(left, right, (0, 0))


def call(body, info, operands, outs, flops, name, final=False, scratch=()):
    moved = sum(math.prod(x.shape) * x.dtype.itemsize for x in (*operands, *outs))
    here = pl.BlockSpec(memory_space=pltpu.VMEM)
    operands = [pltpu.with_memory_space_constraint(x, pltpu.VMEM) for x in operands]
    return pl.pallas_call(
        body,
        in_specs=[pl.BlockSpec(memory_space=pltpu.SMEM)] + [here] * len(operands),
        out_specs=[here] * len(outs),
        out_shape=outs if final else [pltpu.VMEM(o.shape, o.dtype) for o in outs],
        scratch_shapes=scratch,
        compiler_params=pltpu.CompilerParams(vmem_limit_bytes=32 * MIB),
        cost_estimate=pl.CostEstimate(flops=flops, bytes_accessed=moved, transcendentals=0),
        name=name,
    )(info, *operands)


def iota(shape, dim):
    return lax.broadcasted_iota(jnp.int32, shape, dim)


def head_of(shape, dim, size):
    return iota(shape, dim) // size


def valid_col(info, offset, length):
    position = offset + iota((length, 1), 0)
    return (position < info[3]).astype(F32)


def decay(rate, offset, length, chip):
    centre = (chip - 1) / 2.0
    moment = (offset + iota((length, rate.shape[1]), 0)).astype(F32) - centre
    return jnp.exp(-rate * moment), jnp.exp(rate * moment)


def prepare(length, tables, rows, cap, info, d_own, d_oth, w_out, ids_col, ids_row, g, dest, meta):
    mine, core, z = info[0], info[1], info[2]
    for j, d_ref in enumerate((d_own, d_oth)):
        side = core if j == 0 else 1 - core
        valid = valid_col(info, (2 * z + side) * length, length)
        own_rows = pl.ds(pl.multiple_of(core * g.shape[2], g.shape[2]), g.shape[2])
        g[j] = (dot_nt(d_ref[...], w_out[own_rows, :]) * valid).astype(BF16)
        column = ids_col[j]
        row = ids_row[j : j + 1, :]
        owner_row = row // rows
        local_row = row - owner_row * rows
        order = iota((length, length), 0) < iota((length, length), 1)
        same = jnp.where((column // rows == owner_row) & order, 1.0, 0.0)
        slot = jnp.sum(same, axis=0, keepdims=True).astype(jnp.int32)
        where_to = (owner_row ^ mine) * cap + slot
        dest[j : j + 1, :] = where_to
        high = local_row // 32
        pick = iota((16, length), 0)
        coded = jnp.where(
            pick == 0, high + 1, jnp.where(pick == 1, local_row - high * 32, 0)
        )
        coded = coded.astype(F32).astype(BF16)
        for m in range(tables):
            hit = iota((cap, length), 0) + m * cap == where_to
            hit = jnp.where(hit, 1.0, 0.0).astype(BF16)
            meta[m, j] = dot_nt(coded, hit).astype(BF16)


def project(
    length, tables, rows, size, chips, info, ids_col, gain, w_q, w_k, w_v, g, rate, table, *refs
):
    parts, outs = refs[: 2 * (tables - 1)], refs[2 * (tables - 1) :]
    emb, q_raw, k_raw, v_out = outs[:4]
    sends = outs[4:]
    mine, core, z = info[0], info[1], info[2]
    half = w_q.shape[1] // 2
    part = rows // 2
    mine_at = pl.ds(pl.multiple_of(core * half, half), half)
    blocks = [(table, mine * rows)]
    for m in range(1, tables):
        blocks.append((parts[m - 1], (mine ^ m) * rows + core * part))
        blocks.append((parts[tables - 1 + m - 1], (mine ^ m) * rows + (1 - core) * part))
    mean_of = jnp.where(
        head_of((half, half), 0, size) == head_of((half, half), 1, size), 1.0 / size, 0.0
    ).astype(BF16)
    carried = jnp.zeros((half, half), F32)
    adjoint = jnp.zeros((half, half), F32)
    for j in range(2):
        side = core if j == 0 else 1 - core
        column = ids_col[j]
        x = jnp.zeros((length, table.shape[1]), F32)
        for ref, base in blocks:
            count = ref.shape[0]
            hit = column - base == iota((length, count), 1)
            x = x + dot(jnp.where(hit, 1.0, 0.0).astype(BF16), ref[...])
        emb[j] = x.astype(BF16)
        rstd = lax.rsqrt(jnp.mean(x * x, axis=1, keepdims=True) + EPS)
        normed = (x * rstd * gain[...]).astype(BF16)
        valid = valid_col(info, (2 * z + side) * length, length)
        qr = dot(normed, w_q[:, mine_at])
        kr = dot(normed, w_k[:, mine_at])
        v = (dot(normed, w_v[:, mine_at]) * valid).astype(BF16)
        q_raw[j] = qr.astype(BF16)
        k_raw[j] = kr.astype(BF16)
        v_out[j] = v
        falling, rising = decay(rate[...], side * length, length, 2 * length)
        q_rms = lax.rsqrt(dot((qr * qr).astype(BF16), mean_of) + EPS)
        k_rms = lax.rsqrt(dot((kr * kr).astype(BF16), mean_of) + EPS)
        qa = (qr * q_rms * falling / size).astype(BF16)
        kb = (kr * k_rms * rising * (valid / math.sqrt(size))).astype(BF16)
        carried = carried + dot_tn(kb, v)
        adjoint = adjoint + dot_tn(qa, g[j])
    lane_head = head_of((size, half), 1, size)

    def packed(full):
        return sum(
            jnp.where(lane_head == h, full[h * size : (h + 1) * size, :], 0.0)
            for h in range(half // size)
        )

    carried, adjoint = packed(carried), packed(adjoint)
    for bit, ref in enumerate(sends):
        low = ((z >> bit) & 1) == 0
        ref[...] = jnp.where(low, carried, adjoint).astype(BF16)


def scaled_inputs(length, size, info, j, rate, mean_of, q_raw, k_raw, v, g):
    core, z = info[1], info[2]
    side = core if j == 0 else 1 - core
    valid = valid_col(info, (2 * z + side) * length, length)
    falling, rising = decay(rate[...], side * length, length, 2 * length)
    qr = q_raw[j].astype(F32)
    kr = k_raw[j].astype(F32)
    q_rms = lax.rsqrt(dot((qr * qr).astype(BF16), mean_of) + EPS)
    k_rms = lax.rsqrt(dot((kr * kr).astype(BF16), mean_of) + EPS)
    qn = qr * q_rms
    kn = kr * k_rms * valid
    q = qn / size
    k = kn / math.sqrt(size)
    qa = (q * falling).astype(BF16)
    kb = (k * rising).astype(BF16)
    ga = (g[j].astype(F32) * falling).astype(BF16)
    vb = (v[j].astype(F32) * rising).astype(BF16)
    return qn, kn, q_rms, k_rms, q, k, qa, kb, ga, vb, valid


def attend(length, size, info, rate, q_raw, k_raw, v_in, g_in, att, gq, gk, gv):
    core = info[1]
    half = q_raw.shape[2]
    same_head = head_of((half, half), 0, size) == head_of((half, half), 1, size)
    mean_of = jnp.where(same_head, 1.0 / size, 0.0).astype(BF16)
    lane_head = head_of((length, half), 1, size)
    causal = iota((length, length), 0) >= iota((length, length), 1)
    anti = iota((length, length), 0) <= iota((length, length), 1)
    kept, states = [], []
    for j in range(2):
        _, _, _, _, q, k, qa, kb, ga, vb, _ = scaled_inputs(
            length, size, info, j, rate, mean_of, q_raw, k_raw, v_in, g_in
        )
        v, g = v_in[j], g_in[j]
        q, k = q.astype(BF16), k.astype(BF16)
        kept.append((qa, kb, ga, vb))
        states.append(
            (
                jnp.where(same_head, dot_tn(kb, v), 0.0),
                jnp.where(same_head, dot_tn(qa, g), 0.0),
            )
        )
        zero = jnp.zeros_like(v)
        sums = [jnp.zeros((length, half), F32) for _ in range(4)]
        for h in range(half // size):
            mine = lane_head == h

            def only(tensor):
                return jnp.where(mine, tensor, zero)

            def pairs(left, right, mask):
                return jnp.where(mask, dot_nt(only(left), right), 0.0).astype(BF16)

            sums[0] += dot(pairs(qa, kb, causal), only(v))
            sums[1] += dot(pairs(ga, vb, causal), only(k))
            sums[2] += dot(pairs(vb, ga, anti), only(q))
            sums[3] += dot(pairs(kb, qa, anti), only(g))
        kept[j] += (sums,)
    for j in range(2):
        qa, kb, ga, vb, sums = kept[j]
        later = (core if j == 0 else 1 - core).astype(F32)
        state = (states[1 - j][0] * later).astype(BF16)
        back = (states[1 - j][1] * (1.0 - later)).astype(BF16)
        att[j] = (sums[0] + dot(qa, state)).astype(BF16)
        gq[j] = (sums[1] + dot_nt(ga, state)).astype(BF16)
        gk[j] = (sums[2] + dot_nt(vb, back)).astype(BF16)
        gv[j] = (sums[3] + dot(kb, back)).astype(BF16)


def finish(
    length, size, chips, info, rate, q_raw, k_raw, v_in, g_in, att, gq, gk, gv,
    emb, gain, w_q, w_k, w_v, d_own, d_oth, *refs
):
    came, (att_own, att_oth, row_keep, row_send) = refs[: chips - 1], refs[chips - 1 :]
    core, z = info[1], info[2]
    half = q_raw.shape[2]
    same_head = head_of((half, half), 0, size) == head_of((half, half), 1, size)
    mean_of = jnp.where(same_head, 1.0 / size, 0.0).astype(BF16)
    state = jnp.zeros((size, half), F32)
    back = jnp.zeros((size, half), F32)
    for m in range(1, chips):
        peer = z ^ m
        apart = jnp.abs(peer - z).astype(F32) * (2.0 * length)
        piece = came[m - 1][...].astype(F32) * jnp.exp(-rate[...] * apart)
        before = peer < z
        state = state + jnp.where(before, piece, 0.0)
        back = back + jnp.where(before, 0.0, piece)

    def spread(packed):
        return jnp.where(same_head, jnp.concatenate([packed] * (half // size), 0), 0.0).astype(BF16)

    state, back = spread(state), spread(back)
    keep_at = pl.multiple_of(core * half, half)
    mine_at = pl.ds(keep_at, half)
    send_at = pl.multiple_of((1 - core) * half, half)
    for j, d_ref in enumerate((d_own, d_oth)):
        qn, kn, q_rms, k_rms, _, _, qa, kb, ga, vb, valid = scaled_inputs(
            length, size, info, j, rate, mean_of, q_raw, k_raw, v_in, g_in
        )
        attended = (att[j].astype(F32) + dot(qa, state)).astype(BF16)
        (att_own if j == 0 else att_oth)[...] = attended
        grad_q = gq[j].astype(F32) + dot_nt(ga, state)
        grad_k = gk[j].astype(F32) + dot_nt(vb, back)
        grad_v = gv[j].astype(F32) + dot(kb, back)
        d_q = q_rms / size * (grad_q - qn * dot((qn * grad_q).astype(BF16), mean_of))
        d_k = k_rms * (valid / math.sqrt(size)) * (
            grad_k - kn * dot((kn * grad_k).astype(BF16), mean_of)
        )
        d_q, d_k, d_v = d_q.astype(BF16), d_k.astype(BF16), (grad_v * valid).astype(BF16)
        x = emb[j].astype(F32)
        rstd = lax.rsqrt(jnp.mean(x * x, axis=1, keepdims=True) + EPS)
        scaled = []
        total = jnp.zeros((length, 1), F32)
        for at in (keep_at, send_at):
            rows = pl.ds(at, half)
            d_normed = (
                dot_nt(d_q, w_q[rows, mine_at])
                + dot_nt(d_k, w_k[rows, mine_at])
                + dot_nt(d_v, w_v[rows, mine_at])
            )
            d_normed = d_normed * gain[:, rows]
            part = emb[j, :, rows].astype(F32)
            scaled.append((d_normed, part))
            total = total + jnp.sum(d_normed * part, axis=1, keepdims=True)
        pull = total * (rstd * rstd / (2 * half))
        kept = rstd * (scaled[0][0] - scaled[0][1] * pull)
        row_keep[j] = kept + d_ref[:, pl.ds(keep_at, half)].astype(F32) * valid
        row_send[1 - j] = (rstd * (scaled[1][0] - scaled[1][1] * pull)).astype(BF16)


def compact(length, tables, cap, info, row_keep, row_came, dest, meta, *outs):
    for j in range(2):
        grads = (row_keep[j] + row_came[j].astype(F32)).astype(BF16)
        where_to = dest[j : j + 1, :]
        for m in range(tables):
            hit = iota((cap, length), 0) + m * cap == where_to
            hit = jnp.where(hit, 1.0, 0.0).astype(BF16)
            outs[m][j * cap : (j + 1) * cap, :] = dot(hit, grads).astype(BF16)
    for m in range(tables):
        for j in range(2):
            base = 2 * cap + 16 * j
            outs[m][base : base + 16, :] = jnp.zeros((16, outs[m].shape[1]), BF16)
            outs[m][base : base + 16, 0:cap] = meta[m, j]


def result(info, emb, att_own, att_came, w_out, out):
    core = info[1]
    half = att_own.shape[1]
    own = pl.ds(pl.multiple_of(core * half, half), half)
    other = pl.ds(pl.multiple_of((1 - core) * half, half), half)
    total = dot(att_own[...], w_out[own, :]) + dot(att_came[...], w_out[other, :])
    out[...] = (emb[0].astype(F32) + total).astype(BF16)


def owner_sum(tables, rows, cap, chips, info, *refs):
    came, outs, acc = refs[:tables], refs[tables : tables + chips], refs[tables + chips]
    z = info[2]
    total = None
    for m in range(tables):
        for j in range(2):
            base = 2 * cap + 16 * j
            coded = came[m][base : base + 16, 0:cap].astype(F32)
            number = ((coded[0:1, :] - 1.0) * 32.0 + coded[1:2, :]).astype(jnp.int32)
            hit = jnp.where(iota((rows, cap), 0) == number, 1.0, 0.0).astype(BF16)
            part = dot(hit, came[m][j * cap : (j + 1) * cap, :])
            total = part if total is None else total + part
    acc[...] = total
    share = rows // chips
    for m in range(chips):
        at = pl.multiple_of((z ^ m) * share, share)
        outs[m][...] = acc[pl.ds(at, share), :].astype(BF16)


def add_up(chips, info, *refs):
    total = refs[0][...].astype(F32)
    for m in range(1, chips):
        total = total + refs[m][...].astype(F32)
    refs[chips][...] = total.astype(BF16)


def assemble(chips, share, half, info, *refs):
    own, other, out = refs[:chips], refs[chips : 2 * chips], refs[2 * chips]
    core, z = info[1], info[2]
    for m in range(chips):
        rows = pl.ds(pl.multiple_of((z ^ m) * share, share), share)
        for ref, side in ((own[m], core), (other[m], 1 - core)):
            out[rows, pl.ds(pl.multiple_of(side * half, half), half)] = ref[...]


def local(
    item_local, item_owner, hist_len, table, gain, w_query, w_key, w_value, w_out, rate, d_out
):
    tables = lax.axis_size("table")
    count = lax.axis_size("ctx")
    length = item_local.shape[1]
    rows, width = table.shape
    heads = rate.shape[0]
    size = width // heads
    half = width // 2
    chips = count // 2
    cap = 2 * length // tables
    mine = lax.axis_index("table")
    block = lax.axis_index("ctx")
    core = block % 2
    z = block // 2

    def over_table(x, m):
        return lax.ppermute(x, "table", [(i, i ^ m) for i in range(tables)])

    def over_z(x, m):
        return lax.ppermute(x, "ctx", [(i, i ^ (2 * m)) for i in range(count)])

    def swap(x):
        return lax.ppermute(x, "ctx", [(i, i ^ 1) for i in range(count)])

    def array(shape, dtype):
        return jax.ShapeDtypeStruct(shape, dtype)

    info = jnp.stack([mine, core, z, hist_len[0]]).astype(jnp.int32)
    part = rows // 2
    part_own = lax.dynamic_slice(table, (core * part, 0), (part, width))
    parts = [over_table(part_own, m) for m in range(1, tables)]

    ids = item_owner[:, :, 0] * rows + item_local
    ids_row = jnp.concatenate([ids, swap(ids)], 0)
    ids_col = ids_row[:, :, None]
    d_own = d_out[0]
    d_oth = swap(d_own)
    gain_row = gain[None, :]
    rate_row = lax.dynamic_slice(jnp.repeat(rate, size), (core * half,), (half,))[None, :]

    g, dest, meta = call(
        functools.partial(prepare, length, tables, rows, cap),
        info,
        (d_own, d_oth, w_out, ids_col, ids_row),
        [
            array((2, length, half), BF16),
            array((2, length), jnp.int32),
            array((tables, 2, 16, cap), BF16),
        ],
        4 * length * width * half,
        "prepare",
    )
    parts_other = [swap(lax.optimization_barrier((p, dest))[0]) for p in parts]
    bits = max(chips - 1, 1).bit_length() if chips > 1 else 0
    emb, q_raw, k_raw, v, *sends = call(
        functools.partial(project, length, tables, rows, size, chips),
        info,
        (ids_col, gain_row, w_query, w_key, w_value, g, rate_row, table, *parts, *parts_other),
        [array((2, length, width), BF16)]
        + [array((2, length, half), BF16)] * 3
        + [array((size, half), BF16)] * bits,
        4 * length * tables * rows * width,
        "project",
    )
    came = [over_z(sends[m.bit_length() - 1], m) for m in range(1, chips)]
    att, gq, gk, gv = call(
        functools.partial(attend, length, size),
        info,
        (rate_row, q_raw, k_raw, v, g),
        [array((2, length, half), BF16)] * 4,
        32 * length * length * half,
        "attend",
    )
    att_own, att_oth, row_keep, row_send = call(
        functools.partial(finish, length, size, chips),
        info,
        (rate_row, q_raw, k_raw, v, g, att, gq, gk, gv, emb, gain_row, w_query, w_key, w_value,
         d_own, d_oth, *came),
        [array((length, half), BF16)] * 2
        + [array((2, length, half), F32), array((2, length, half), BF16)],
        12 * length * width * half,
        "finish",
    )
    row_came = swap(row_send)
    att_came = swap(att_oth)
    outgoing = call(
        functools.partial(compact, length, tables, cap),
        info,
        (row_keep, row_came, dest, meta),
        [array((2 * cap + 32, half), BF16)] * tables,
        4 * length * 2 * length * half,
        "compact",
    )
    arrived = [outgoing[0]] + [over_table(outgoing[m], m) for m in range(1, tables)]
    (output,) = call(
        result,
        info,
        (emb, att_own, att_came, w_out),
        [array((length, width), BF16)],
        2 * length * width * width,
        "result",
        True,
    )
    share = rows // chips
    everything = call(
        functools.partial(owner_sum, tables, rows, cap, chips),
        info,
        arrived,
        [array((share, half), BF16)] * chips,
        4 * rows * length * tables * half,
        "owner_sum",
        False,
        [pltpu.VMEM((rows, half), F32)],
    )
    pieces = [everything[0]] + [over_z(everything[m], m) for m in range(1, chips)]
    (summed,) = call(
        functools.partial(add_up, chips),
        info,
        pieces,
        [array((share, half), BF16)],
        chips * share * half,
        "add_up",
    )
    own = [summed] + [over_z(summed, m) for m in range(1, chips)]
    other = [swap(x) for x in own]
    (table_grad,) = call(
        functools.partial(assemble, chips, share, half),
        info,
        [*own, *other],
        [array((rows, width), BF16)],
        rows * width,
        "assemble",
        True,
    )
    return (output[None], table_grad)


def solution(mesh):
    return jax.shard_map(
        local,
        mesh=mesh,
        in_specs=(
            P("table", "ctx"),
            P("table", "ctx", None),
            P("table"),
            P("table", None),
            P(),
            P(),
            P(),
            P(),
            P(),
            P(),
            P("table", "ctx", None),
        ),
        out_specs=(P("table", "ctx", None), P("table", None)),
        check_vma=False,
    )
```

```python
import functools
import math

import jax
import jax.numpy as jnp
from jax import lax
from jax.experimental import pallas as pl
from jax.experimental.pallas import tpu as pltpu
from jax.sharding import PartitionSpec as P

EPS = 1e-06
F32 = jnp.float32
BF16 = jnp.bfloat16
MIB = 1 << 20


def dot(left, right, ways=(1, 0)):
    return lax.dot_general(
        left, right, (((ways[0],), (ways[1],)), ((), ())), preferred_element_type=F32
    )


def dot_nt(left, right):
    return dot(left, right, (1, 1))


def dot_tn(left, right):
    return dot(left, right, (0, 0))


def call(body, info, operands, outs, flops, name, final=False, scratch=()):
    scalars = info if isinstance(info, tuple) else (info,)
    moved = sum(math.prod(x.shape) * x.dtype.itemsize for x in (*operands, *outs))
    here = pl.BlockSpec(memory_space=pltpu.VMEM)
    operands = [pltpu.with_memory_space_constraint(x, pltpu.VMEM) for x in operands]
    return pl.pallas_call(
        body,
        in_specs=[pl.BlockSpec(memory_space=pltpu.SMEM)] * len(scalars) + [here] * len(operands),
        out_specs=[here] * len(outs),
        out_shape=outs if final else [pltpu.VMEM(o.shape, o.dtype) for o in outs],
        scratch_shapes=scratch,
        compiler_params=pltpu.CompilerParams(vmem_limit_bytes=32 * MIB),
        cost_estimate=pl.CostEstimate(flops=flops, bytes_accessed=moved, transcendentals=0),
        name=name,
    )(*scalars, *operands)


def iota(shape, dim):
    return lax.broadcasted_iota(jnp.int32, shape, dim)


def head_of(shape, dim, size):
    return iota(shape, dim) // size


def valid_col(info, offset, length):
    position = offset + iota((length, 1), 0)
    return (position < info[3]).astype(F32)


def decay(rate, offset, length, chip):
    centre = (chip - 1) / 2.0
    moment = (offset + iota((length, rate.shape[1]), 0)).astype(F32) - centre
    return jnp.exp(-rate * moment), jnp.exp(rate * moment)


def pick(part, table, out):
    at = pl.multiple_of((lax.axis_index("ctx") & 1) * part, part)
    pltpu.sync_copy(table.at[pl.ds(at, part), :], out)


def prepare(
    length, tables, rows, cap, size, info, rate, d_own, d_oth, w_out, ids_col, ids_row, table, gain,
    g, dest, meta, emb, rate_row, gain_row,
):
    mine, core, z = info[0], info[1], info[2]
    half = g.shape[2]
    gain_row[...] = gain[...]
    head = head_of((1, half), 1, size) + core * (half // size)
    rates = jnp.zeros((1, half), F32)
    for h in range(rate.shape[0]):
        rates = jnp.where(head == h, rate[h], rates)
    rate_row[...] = rates
    numbers = []
    for j, d_ref in enumerate((d_own, d_oth)):
        side = core if j == 0 else 1 - core
        valid = valid_col(info, (2 * z + side) * length, length)
        own_rows = pl.ds(pl.multiple_of(core * g.shape[2], g.shape[2]), g.shape[2])
        g[j] = (dot_nt(d_ref[...], w_out[own_rows, :]) * valid).astype(BF16)
        column = ids_col[j]
        row = ids_row[j : j + 1, :]
        owner_row = row // rows
        local_row = row - owner_row * rows
        order = iota((length, length), 0) < iota((length, length), 1)
        same = jnp.where((column // rows == owner_row) & order, 1.0, 0.0)
        slot = jnp.sum(same, axis=0, keepdims=True).astype(jnp.int32)
        where_to = (owner_row ^ mine) * cap + slot
        dest[j : j + 1, :] = where_to
        hit = jnp.where(column - mine * rows == iota((length, rows), 1), 1.0, 0.0).astype(BF16)
        emb[j] = dot(hit, table[...]).astype(BF16)
        high = local_row // 32
        line = iota((16, length), 0) - 2 * j
        coded = jnp.where(line == 0, high + 1, jnp.where(line == 1, local_row - high * 32, 0))
        numbers.append((coded.astype(F32).astype(BF16), where_to))
    for m in range(tables):
        total = jnp.zeros((16, cap), F32)
        for coded, where_to in numbers:
            hit = iota((cap, length), 0) + m * cap == where_to
            total = total + dot_nt(coded, jnp.where(hit, 1.0, 0.0).astype(BF16))
        meta[m] = total.astype(BF16)


def project(
    length, tables, rows, size, chips, info, ids_col, gain, w_q, w_k, w_v, g, rate, emb_own, *refs
):
    parts, outs = refs[: 2 * (tables - 1)], refs[2 * (tables - 1) :]
    emb, q_raw, k_raw, v_out = outs[:4]
    sends = outs[4:]
    mine, core, z = info[0], info[1], info[2]
    half = w_q.shape[1] // 2
    part = rows // 2
    mine_at = pl.ds(pl.multiple_of(core * half, half), half)
    blocks = []
    for m in range(1, tables):
        blocks.append((parts[m - 1], (mine ^ m) * rows + core * part))
        blocks.append((parts[tables - 1 + m - 1], (mine ^ m) * rows + (1 - core) * part))
    mean_of = jnp.where(
        head_of((half, half), 0, size) == head_of((half, half), 1, size), 1.0 / size, 0.0
    ).astype(BF16)
    carried = jnp.zeros((half, half), F32)
    adjoint = jnp.zeros((half, half), F32)
    for j in range(2):
        side = core if j == 0 else 1 - core
        column = ids_col[j]
        x = emb_own[j].astype(F32)
        for ref, base in blocks:
            count = ref.shape[0]
            hit = column - base == iota((length, count), 1)
            x = x + dot(jnp.where(hit, 1.0, 0.0).astype(BF16), ref[...])
        emb[j] = x.astype(BF16)
        rstd = lax.rsqrt(jnp.mean(x * x, axis=1, keepdims=True) + EPS)
        normed = (x * rstd * gain[...]).astype(BF16)
        valid = valid_col(info, (2 * z + side) * length, length)
        qr = dot(normed, w_q[:, mine_at])
        kr = dot(normed, w_k[:, mine_at])
        v = (dot(normed, w_v[:, mine_at]) * valid).astype(BF16)
        q_raw[j] = qr.astype(BF16)
        k_raw[j] = kr.astype(BF16)
        v_out[j] = v
        falling, rising = decay(rate[...], side * length, length, 2 * length)
        q_rms = lax.rsqrt(dot((qr * qr).astype(BF16), mean_of) + EPS)
        k_rms = lax.rsqrt(dot((kr * kr).astype(BF16), mean_of) + EPS)
        qa = (qr * q_rms * falling / size).astype(BF16)
        kb = (kr * k_rms * rising * (valid / math.sqrt(size))).astype(BF16)
        carried = carried + dot_tn(kb, v)
        adjoint = adjoint + dot_tn(qa, g[j])
    lane_head = head_of((size, half), 1, size)

    def packed(full):
        return sum(
            jnp.where(lane_head == h, full[h * size : (h + 1) * size, :], 0.0)
            for h in range(half // size)
        )

    carried, adjoint = packed(carried), packed(adjoint)
    for bit, ref in enumerate(sends):
        low = ((z >> bit) & 1) == 0
        ref[...] = jnp.where(low, carried, adjoint).astype(BF16)


def scaled_inputs(length, size, info, j, rate, mean_of, q_raw, k_raw, v, g):
    core, z = info[1], info[2]
    side = core if j == 0 else 1 - core
    valid = valid_col(info, (2 * z + side) * length, length)
    falling, rising = decay(rate[...], side * length, length, 2 * length)
    qr = q_raw[j].astype(F32)
    kr = k_raw[j].astype(F32)
    q_rms = lax.rsqrt(dot((qr * qr).astype(BF16), mean_of) + EPS)
    k_rms = lax.rsqrt(dot((kr * kr).astype(BF16), mean_of) + EPS)
    qn = qr * q_rms
    kn = kr * k_rms * valid
    q = qn / size
    k = kn / math.sqrt(size)
    qa = (q * falling).astype(BF16)
    kb = (k * rising).astype(BF16)
    ga = (g[j].astype(F32) * falling).astype(BF16)
    vb = (v[j].astype(F32) * rising).astype(BF16)
    return qn, kn, q_rms, k_rms, q, k, qa, kb, ga, vb, valid


def attend(length, size, info, rate, q_raw, k_raw, v_in, g_in, att, gq, gk, gv):
    core = info[1]
    half = q_raw.shape[2]
    same_head = head_of((half, half), 0, size) == head_of((half, half), 1, size)
    mean_of = jnp.where(same_head, 1.0 / size, 0.0).astype(BF16)
    lane_head = head_of((length, half), 1, size)
    causal = iota((length, length), 0) >= iota((length, length), 1)
    anti = iota((length, length), 0) <= iota((length, length), 1)
    kept, states = [], []
    for j in range(2):
        _, _, _, _, q, k, qa, kb, ga, vb, _ = scaled_inputs(
            length, size, info, j, rate, mean_of, q_raw, k_raw, v_in, g_in
        )
        v, g = v_in[j], g_in[j]
        q, k = q.astype(BF16), k.astype(BF16)
        kept.append((qa, kb, ga, vb))
        states.append(
            (
                jnp.where(same_head, dot_tn(kb, v), 0.0),
                jnp.where(same_head, dot_tn(qa, g), 0.0),
            )
        )
        zero = jnp.zeros_like(v)
        sums = [jnp.zeros((length, half), F32) for _ in range(4)]
        for h in range(half // size):
            mine = lane_head == h

            def only(tensor):
                return jnp.where(mine, tensor, zero)

            def pairs(left, right, mask):
                return jnp.where(mask, dot_nt(only(left), right), 0.0).astype(BF16)

            sums[0] += dot(pairs(qa, kb, causal), only(v))
            sums[1] += dot(pairs(ga, vb, causal), only(k))
            sums[2] += dot(pairs(vb, ga, anti), only(q))
            sums[3] += dot(pairs(kb, qa, anti), only(g))
        kept[j] += (sums,)
    for j in range(2):
        qa, kb, ga, vb, sums = kept[j]
        later = (core if j == 0 else 1 - core).astype(F32)
        state = (states[1 - j][0] * later).astype(BF16)
        back = (states[1 - j][1] * (1.0 - later)).astype(BF16)
        att[j] = (sums[0] + dot(qa, state)).astype(BF16)
        gq[j] = (sums[1] + dot_nt(ga, state)).astype(BF16)
        gk[j] = (sums[2] + dot_nt(vb, back)).astype(BF16)
        gv[j] = (sums[3] + dot(kb, back)).astype(BF16)


def finish(
    length, size, chips, info, rate, q_raw, k_raw, v_in, g_in, att, gq, gk, gv,
    emb, gain, w_q, w_k, w_v, d_own, d_oth, *refs
):
    came, (att_own, att_oth, row_keep, row_send) = refs[: chips - 1], refs[chips - 1 :]
    core, z = info[1], info[2]
    half = q_raw.shape[2]
    same_head = head_of((half, half), 0, size) == head_of((half, half), 1, size)
    mean_of = jnp.where(same_head, 1.0 / size, 0.0).astype(BF16)
    state = jnp.zeros((size, half), F32)
    back = jnp.zeros((size, half), F32)
    for m in range(1, chips):
        peer = z ^ m
        apart = jnp.abs(peer - z).astype(F32) * (2.0 * length)
        piece = came[m - 1][...].astype(F32) * jnp.exp(-rate[...] * apart)
        before = peer < z
        state = state + jnp.where(before, piece, 0.0)
        back = back + jnp.where(before, 0.0, piece)

    def spread(packed):
        return jnp.where(same_head, jnp.concatenate([packed] * (half // size), 0), 0.0).astype(BF16)

    state, back = spread(state), spread(back)
    keep_at = pl.multiple_of(core * half, half)
    mine_at = pl.ds(keep_at, half)
    send_at = pl.multiple_of((1 - core) * half, half)
    for j, d_ref in enumerate((d_own, d_oth)):
        qn, kn, q_rms, k_rms, _, _, qa, kb, ga, vb, valid = scaled_inputs(
            length, size, info, j, rate, mean_of, q_raw, k_raw, v_in, g_in
        )
        attended = (att[j].astype(F32) + dot(qa, state)).astype(BF16)
        (att_own if j == 0 else att_oth)[...] = attended
        grad_q = gq[j].astype(F32) + dot_nt(ga, state)
        grad_k = gk[j].astype(F32) + dot_nt(vb, back)
        grad_v = gv[j].astype(F32) + dot(kb, back)
        d_q = q_rms / size * (grad_q - qn * dot((qn * grad_q).astype(BF16), mean_of))
        d_k = k_rms * (valid / math.sqrt(size)) * (
            grad_k - kn * dot((kn * grad_k).astype(BF16), mean_of)
        )
        d_q, d_k, d_v = d_q.astype(BF16), d_k.astype(BF16), (grad_v * valid).astype(BF16)
        x = emb[j].astype(F32)
        rstd = lax.rsqrt(jnp.mean(x * x, axis=1, keepdims=True) + EPS)
        scaled = []
        total = jnp.zeros((length, 1), F32)
        for at in (keep_at, send_at):
            rows = pl.ds(at, half)
            d_normed = (
                dot_nt(d_q, w_q[rows, mine_at])
                + dot_nt(d_k, w_k[rows, mine_at])
                + dot_nt(d_v, w_v[rows, mine_at])
            )
            d_normed = d_normed * gain[:, rows]
            part = emb[j, :, rows].astype(F32)
            scaled.append((d_normed, part))
            total = total + jnp.sum(d_normed * part, axis=1, keepdims=True)
        pull = total * (rstd * rstd / (2 * half))
        kept = rstd * (scaled[0][0] - scaled[0][1] * pull)
        row_keep[j] = kept + d_ref[:, pl.ds(keep_at, half)].astype(F32) * valid
        row_send[1 - j] = (rstd * (scaled[1][0] - scaled[1][1] * pull)).astype(BF16)


def compact(length, tables, cap, info, row_keep, row_came, dest, meta, *outs):
    for j in range(2):
        grads = (row_keep[j] + row_came[j].astype(F32)).astype(BF16)
        where_to = dest[j : j + 1, :]
        for m in range(tables):
            hit = iota((cap, length), 0) + m * cap == where_to
            hit = jnp.where(hit, 1.0, 0.0).astype(BF16)
            outs[m][j * cap : (j + 1) * cap, :] = dot(hit, grads).astype(BF16)
    for m in range(tables):
        outs[m][2 * cap : 2 * cap + 16, :] = jnp.zeros((16, outs[m].shape[1]), BF16)
        outs[m][2 * cap : 2 * cap + 16, 0:cap] = meta[m]


def result(info, emb, att_own, att_came, w_out, out):
    core = info[1]
    half = att_own.shape[1]
    own = pl.ds(pl.multiple_of(core * half, half), half)
    other = pl.ds(pl.multiple_of((1 - core) * half, half), half)
    total = dot(att_own[...], w_out[own, :]) + dot(att_came[...], w_out[other, :])
    out[...] = (emb[0].astype(F32) + total).astype(BF16)


def owner_sum(tables, rows, cap, chips, info, *refs):
    came, outs, acc = refs[:tables], refs[tables : tables + chips], refs[tables + chips]
    z = info[2]
    total = None
    for m in range(tables):
        coded = came[m][2 * cap : 2 * cap + 16, 0:cap].astype(F32)
        for j in range(2):
            high, low = coded[2 * j : 2 * j + 1, :], coded[2 * j + 1 : 2 * j + 2, :]
            number = ((high - 1.0) * 32.0 + low).astype(jnp.int32)
            hit = jnp.where(iota((rows, cap), 0) == number, 1.0, 0.0).astype(BF16)
            part = dot(hit, came[m][j * cap : (j + 1) * cap, :])
            total = part if total is None else total + part
    acc[...] = total
    share = rows // chips
    for m in range(chips):
        at = pl.multiple_of((z ^ m) * share, share)
        outs[m][...] = acc[pl.ds(at, share), :].astype(BF16)


def add_up(chips, info, *refs):
    total = refs[0][...].astype(F32)
    for m in range(1, chips):
        total = total + refs[m][...].astype(F32)
    refs[chips][...] = total.astype(BF16)


def assemble(chips, share, half, info, *refs):
    own, other, out = refs[:chips], refs[chips : 2 * chips], refs[2 * chips]
    core, z = info[1], info[2]
    for m in range(chips):
        rows = pl.ds(pl.multiple_of((z ^ m) * share, share), share)
        for ref, side in ((own[m], core), (other[m], 1 - core)):
            out[rows, pl.ds(pl.multiple_of(side * half, half), half)] = ref[...]


def local(
    item_local, item_owner, hist_len, table, gain, w_query, w_key, w_value, w_out, rate, d_out
):
    tables = lax.axis_size("table")
    count = lax.axis_size("ctx")
    length = item_local.shape[1]
    rows, width = table.shape
    heads = rate.shape[0]
    size = width // heads
    half = width // 2
    chips = count // 2
    cap = 2 * length // tables
    mine = lax.axis_index("table")
    block = lax.axis_index("ctx")
    core = block % 2
    z = block // 2

    def over_table(x, m):
        return lax.ppermute(x, "table", [(i, i ^ m) for i in range(tables)])

    def over_z(x, m):
        return lax.ppermute(x, "ctx", [(i, i ^ (2 * m)) for i in range(count)])

    def swap(x):
        return lax.ppermute(x, "ctx", [(i, i ^ 1) for i in range(count)])

    def array(shape, dtype):
        return jax.ShapeDtypeStruct(shape, dtype)

    info = jnp.stack([mine, core, z, hist_len[0]]).astype(jnp.int32)
    part = rows // 2
    part_own = pl.pallas_call(
        functools.partial(pick, part),
        in_specs=[pl.BlockSpec(memory_space=pl.ANY)],
        out_specs=pl.BlockSpec(memory_space=pltpu.VMEM),
        out_shape=pltpu.VMEM((part, width), BF16),
        name="pick",
    )(table)
    parts = [over_table(part_own, m) for m in range(1, tables)]

    ids = item_owner[:, :, 0] * rows + item_local
    ids_row = jnp.concatenate([ids, swap(ids)], 0)
    ids_col = ids_row[:, :, None]
    d_own = d_out[0]
    d_oth = swap(d_own)
    g, dest, meta, emb_own, rate_row, gain_row = call(
        functools.partial(prepare, length, tables, rows, cap, size),
        (info, rate),
        (d_own, d_oth, w_out, ids_col, ids_row, table, gain[None, :]),
        [
            array((2, length, half), BF16),
            array((2, length), jnp.int32),
            array((tables, 16, cap), BF16),
            array((2, length, width), BF16),
            array((1, half), F32),
            array((1, width), F32),
        ],
        4 * length * width * half,
        "prepare",
    )
    parts_other = [swap(p) for p in parts[:-1]] + [swap(lax.optimization_barrier((parts[-1], dest))[0])]
    bits = max(chips - 1, 1).bit_length() if chips > 1 else 0
    emb, q_raw, k_raw, v, *sends = call(
        functools.partial(project, length, tables, rows, size, chips),
        info,
        (ids_col, gain_row, w_query, w_key, w_value, g, rate_row, emb_own, *parts, *parts_other),
        [array((2, length, width), BF16)]
        + [array((2, length, half), BF16)] * 3
        + [array((size, half), BF16)] * bits,
        4 * length * tables * rows * width,
        "project",
    )
    came = [over_z(sends[m.bit_length() - 1], m) for m in range(1, chips)]
    att, gq, gk, gv = call(
        functools.partial(attend, length, size),
        info,
        (rate_row, q_raw, k_raw, v, g),
        [array((2, length, half), BF16)] * 4,
        32 * length * length * half,
        "attend",
    )
    att_own, att_oth, row_keep, row_send = call(
        functools.partial(finish, length, size, chips),
        info,
        (rate_row, q_raw, k_raw, v, g, att, gq, gk, gv, emb, gain_row, w_query, w_key, w_value,
         d_own, d_oth, *came),
        [array((length, half), BF16)] * 2
        + [array((2, length, half), F32), array((2, length, half), BF16)],
        12 * length * width * half,
        "finish",
    )
    row_came = swap(row_send)
    att_came = swap(att_oth)
    outgoing = call(
        functools.partial(compact, length, tables, cap),
        info,
        (row_keep, row_came, dest, meta),
        [array((2 * cap + 16, half), BF16)] * tables,
        4 * length * 2 * length * half,
        "compact",
    )
    outgoing, att_came = lax.optimization_barrier((outgoing, att_came))
    arrived = [outgoing[0]] + [over_table(outgoing[m], m) for m in range(1, tables)]
    (output,) = call(
        result,
        info,
        (emb, att_own, att_came, w_out),
        [array((length, width), BF16)],
        2 * length * width * width,
        "result",
        True,
    )
    arrived, output = lax.optimization_barrier((arrived, output))
    share = rows // chips
    everything = call(
        functools.partial(owner_sum, tables, rows, cap, chips),
        info,
        arrived,
        [array((share, half), BF16)] * chips,
        4 * rows * length * tables * half,
        "owner_sum",
        False,
        [pltpu.VMEM((rows, half), F32)],
    )
    pieces = [everything[0]] + [over_z(everything[m], m) for m in range(1, chips)]
    (summed,) = call(
        functools.partial(add_up, chips),
        info,
        pieces,
        [array((share, half), BF16)],
        chips * share * half,
        "add_up",
    )
    own = [summed] + [over_z(summed, m) for m in range(1, chips)]
    other = [swap(x) for x in own]
    (table_grad,) = call(
        functools.partial(assemble, chips, share, half),
        info,
        [*own, *other],
        [array((rows, width), BF16)],
        rows * width,
        "assemble",
        True,
    )
    return (output[None], table_grad)


def solution(mesh):
    return jax.shard_map(
        local,
        mesh=mesh,
        in_specs=(
            P("table", "ctx"),
            P("table", "ctx", None),
            P("table"),
            P("table", None),
            P(),
            P(),
            P(),
            P(),
            P(),
            P(),
            P("table", "ctx", None),
        ),
        out_specs=(P("table", "ctx", None), P("table", None)),
        check_vma=False,
    )
```

```python
import functools
import math

import jax
import jax.numpy as jnp
from jax import lax
from jax.experimental import pallas as pl
from jax.experimental.pallas import tpu as pltpu
from jax.sharding import PartitionSpec as P

EPS = 1e-06
F32 = jnp.float32
BF16 = jnp.bfloat16
MIB = 1 << 20


def dot(left, right, ways=(1, 0)):
    return lax.dot_general(
        left, right, (((ways[0],), (ways[1],)), ((), ())), preferred_element_type=F32
    )


def dot_nt(left, right):
    return dot(left, right, (1, 1))


def dot_tn(left, right):
    return dot(left, right, (0, 0))


def call(body, info, operands, outs, flops, name, final=None, scratch=(), away=()):
    moved = sum(math.prod(x.shape) * x.dtype.itemsize for x in (*operands, *outs))
    here = pl.BlockSpec(memory_space=pltpu.VMEM)
    operands = [pltpu.with_memory_space_constraint(x, pltpu.VMEM) for x in operands]
    return pl.pallas_call(
        body,
        in_specs=[pl.BlockSpec(memory_space=pltpu.SMEM)]
        + [here] * len(operands)
        + [pl.BlockSpec(memory_space=pl.ANY)] * len(away),
        out_specs=[pl.BlockSpec(memory_space=final) if final else here] * len(outs),
        out_shape=outs if final else [pltpu.VMEM(o.shape, o.dtype) for o in outs],
        scratch_shapes=scratch,
        compiler_params=pltpu.CompilerParams(vmem_limit_bytes=32 * MIB),
        cost_estimate=pl.CostEstimate(flops=flops, bytes_accessed=moved, transcendentals=0),
        name=name,
    )(info, *operands, *away)


def iota(shape, dim):
    return lax.broadcasted_iota(jnp.int32, shape, dim)


def head_of(shape, dim, size):
    return iota(shape, dim) // size


def valid_col(info, offset, length):
    position = offset + iota((length, 1), 0)
    return (position < info[3]).astype(F32)


def decay(rate, offset, length, chip):
    centre = (chip - 1) / 2.0
    moment = (offset + iota((length, rate.shape[1]), 0)).astype(F32) - centre
    return jnp.exp(-rate * moment), jnp.exp(rate * moment)


def pick(part, table, first, second, sems):
    core = lax.axis_index("ctx") & 1
    copies = []
    for n, (side, out) in enumerate(((core, first), (1 - core, second))):
        at = pl.multiple_of(side * part, part)
        copies.append(pltpu.make_async_copy(table.at[pl.ds(at, part), :], out, sems.at[n]))
    for copy in copies:
        copy.start()
    for copy in copies:
        copy.wait()


def held_rows(where_from, refs, info, rows):
    mine, core = info[0], info[1]
    for ref, (masks, sides) in zip(refs, where_from):
        owner = mine ^ jnp.where(core == 0, masks[0], masks[1])
        yield ref, owner * rows + jnp.where(core == 0, sides[0], sides[1]) * (rows // 2)


def chosen_rows(x, column, blocks):
    for ref, base in blocks:
        hit = column - base == iota((column.shape[0], ref.shape[0]), 1)
        x = x + dot(jnp.where(hit, 1.0, 0.0).astype(BF16), ref[...])
    return x


def prepare(
    length, tables, rows, cap, size, where_from, info, d_oth, ids_col, ids_row, *refs
):
    parts = refs[: len(where_from)]
    (rate, w_out, d_own, gain,
    g, ga, dest, meta, emb, falling, rising, rate_row, gain_row, w_here, d_here, rates, sems) = refs[len(where_from) :]
    pairs = ((rate, rates), (d_own, d_here), (w_out, w_here), (gain, gain_row))
    copies = [pltpu.make_async_copy(a, b, sems.at[n]) for n, (a, b) in enumerate(pairs)]
    for copy in copies:
        copy.start()
    mine, core, z = info[0], info[1], info[2]
    half = g.shape[2]
    blocks = list(held_rows(where_from, parts, info, rows))
    numbers = []
    for j in range(2):
        column = ids_col[j]
        row = ids_row[j : j + 1, :]
        owner_row = row // rows
        local_row = row - owner_row * rows
        order = iota((length, length), 0) < iota((length, length), 1)
        same = jnp.where((column // rows == owner_row) & order, 1.0, 0.0)
        slot = jnp.sum(same, axis=0, keepdims=True).astype(jnp.int32)
        where_to = (owner_row ^ mine) * cap + slot
        dest[j : j + 1, :] = where_to
        x = chosen_rows(jnp.zeros((length, emb.shape[2]), F32), column, blocks)
        emb[j] = x.astype(BF16)
        high = local_row // 32
        line = iota((16, length), 0) - 2 * j
        coded = jnp.where(line == 0, high + 1, jnp.where(line == 1, local_row - high * 32, 0))
        numbers.append((coded.astype(F32).astype(BF16), where_to))
    for m in range(tables):
        total = jnp.zeros((16, cap), F32)
        for coded, where_to in numbers:
            hit = iota((cap, length), 0) + m * cap == where_to
            total = total + dot_nt(coded, jnp.where(hit, 1.0, 0.0).astype(BF16))
        meta[m] = total.astype(BF16)
    for copy in copies:
        copy.wait()
    head = head_of((1, half), 1, size) + core * (half // size)
    chosen = jnp.zeros((1, half), F32)
    for h in range(rates.shape[1]):
        chosen = jnp.where(head == h, rates[0:1, h : h + 1], chosen)
    rate_row[...] = chosen
    own_rows = pl.ds(pl.multiple_of(core * half, half), half)
    for j, d_ref in enumerate((d_here, d_oth)):
        side = core if j == 0 else 1 - core
        valid = valid_col(info, (2 * z + side) * length, length)
        down, up = decay(chosen, side * length, length, 2 * length)
        falling[j], rising[j] = down, up
        grads = (dot_nt(d_ref[...], w_here[own_rows, :]) * valid).astype(BF16)
        g[j] = grads
        ga[j] = (grads.astype(F32) * down).astype(BF16)


def same_heads(half, size):
    return head_of((half, half), 0, size) == head_of((half, half), 1, size)


def project(
    length, where_from, rows, size, chips, info, ids_col, gain, w_q, w_k, w_v, g, falling, rising, emb_own, *refs
):
    parts, outs = refs[: len(where_from)], refs[len(where_from) :]
    emb, v_out, qa_out, kb_out, vb_out, qn_out, kn_out, qs_out, ks_out, rstd_out, states = outs[:11]
    sends = outs[11:]
    mine, core, z = info[0], info[1], info[2]
    half = w_q.shape[1] // 2
    mine_at = pl.ds(pl.multiple_of(core * half, half), half)
    blocks = list(held_rows(where_from, parts, info, rows))
    same_head = same_heads(half, size)
    mean_of = jnp.where(same_head, 1.0 / size, 0.0).astype(BF16)
    totals = [0.0, 0.0]
    for j in range(2):
        side = core if j == 0 else 1 - core
        column = ids_col[j]
        x = chosen_rows(emb_own[j].astype(F32), column, blocks)
        emb[j] = x.astype(BF16)
        rstd = lax.rsqrt(jnp.mean(x * x, axis=1, keepdims=True) + EPS)
        rstd_out[j] = rstd
        normed = (x * rstd * gain[...]).astype(BF16)
        valid = valid_col(info, (2 * z + side) * length, length)
        qr = dot(normed, w_q[:, mine_at])
        kr = dot(normed, w_k[:, mine_at])
        v = dot(normed, w_v[:, mine_at]) * valid
        q_rms = lax.rsqrt(dot((qr * qr).astype(BF16), mean_of) + EPS)
        k_rms = lax.rsqrt(dot((kr * kr).astype(BF16), mean_of) + EPS)
        qn = qr * q_rms
        kn = kr * k_rms * valid
        qa = (qn * falling[j] / size).astype(BF16)
        kb = (kn * rising[j] / math.sqrt(size)).astype(BF16)
        vb_out[j] = (v * rising[j]).astype(BF16)
        v = v.astype(BF16)
        v_out[j] = v
        qa_out[j] = qa
        kb_out[j] = kb
        qn_out[j] = qn.astype(BF16)
        kn_out[j] = kn.astype(BF16)
        qs_out[j] = q_rms / size
        ks_out[j] = k_rms * (valid / math.sqrt(size))
        for n, full in enumerate((dot_tn(kb, v), dot_tn(qa, g[j]))):
            full = jnp.where(same_head, full, 0.0)
            states[n, j] = full.astype(BF16)
            totals[n] = totals[n] + full

    def packed(full):
        return sum(full[h * size : (h + 1) * size, :] for h in range(half // size))

    carried, adjoint = packed(totals[0]), packed(totals[1])
    for bit, ref in enumerate(sends):
        low = ((z >> bit) & 1) == 0
        ref[...] = jnp.where(low, carried, adjoint).astype(BF16)


class Pairs:
    def __init__(self, length, half, size):
        self.length, self.count = length, half // size
        self.lane_head = head_of((length, half), 1, size)
        self.lanes = [
            jnp.where(self.lane_head == h, 1.0, 0.0).astype(BF16) for h in range(self.count)
        ]
        ahead = iota((length, length), 0) - iota((length, length), 1)
        self.causal = jnp.where(ahead >= 0, 1.0, 0.0).astype(BF16)
        self.anti = jnp.where(ahead <= 0, 1.0, 0.0).astype(BF16)

    def __call__(self, left, right, mask, value):
        length = self.length
        every = jnp.concatenate([left * only for only in self.lanes], 0)
        scores = dot_nt(every, right).astype(BF16)
        scores = [scores[h * length : (h + 1) * length] * mask for h in range(self.count)]
        whole = dot(jnp.concatenate(scores, 0), value)
        total = whole[:length]
        for h in range(1, self.count):
            total = jnp.where(self.lane_head == h, whole[h * length : (h + 1) * length], total)
        return total


def attend(length, size, info, qa_in, kb_in, v_in, vb_in, g_in, ga_in, states, gq, gk, gv):
    core = info[1]
    pairs = Pairs(length, qa_in.shape[2], size)
    for j in range(2):
        qa, kb, v, vb, g, ga = qa_in[j], kb_in[j], v_in[j], vb_in[j], g_in[j], ga_in[j]
        later = (core if j == 0 else 1 - core).astype(F32)
        grad_q = pairs(ga, v, pairs.causal, kb) + later * dot_nt(ga, states[0, 1 - j])
        grad_k = pairs(vb, g, pairs.anti, qa) + (1.0 - later) * dot_nt(vb, states[1, 1 - j])
        grad_v = pairs(kb, qa, pairs.anti, g) + (1.0 - later) * dot(kb, states[1, 1 - j])
        gq[j], gk[j], gv[j] = grad_q.astype(BF16), grad_k.astype(BF16), grad_v.astype(BF16)


def finish(
    length, size, chips, info, rate, kb, vb, ga, qn_in, kn_in, qs, ks, rstd_in, gq, gk, gv,
    emb, gain, w_q, w_k, w_v, d_own, d_oth, *refs
):
    came, (before_out, row_keep, row_send) = refs[: chips - 1], refs[chips - 1 :]
    core, z = info[1], info[2]
    half = kb.shape[2]
    same_head = same_heads(half, size)
    mean_of = jnp.where(same_head, 1.0 / size, 0.0).astype(BF16)
    state = jnp.zeros((size, half), F32)
    back = jnp.zeros((size, half), F32)
    for m in range(1, chips):
        peer = z ^ m
        apart = jnp.abs(peer - z).astype(F32) * (2.0 * length)
        piece = came[m - 1][...].astype(F32) * jnp.exp(-rate[...] * apart)
        before = peer < z
        state = state + jnp.where(before, piece, 0.0)
        back = back + jnp.where(before, 0.0, piece)

    def spread(packed):
        return jnp.where(same_head, jnp.concatenate([packed] * (half // size), 0), 0.0).astype(BF16)

    state, back = spread(state), spread(back)
    before_out[...] = state
    keep_at = pl.multiple_of(core * half, half)
    mine_at = pl.ds(keep_at, half)
    send_at = pl.multiple_of((1 - core) * half, half)
    for j, d_ref in enumerate((d_own, d_oth)):
        side = core if j == 0 else 1 - core
        valid = valid_col(info, (2 * z + side) * length, length)
        grad_q = gq[j].astype(F32) + dot_nt(ga[j], state)
        grad_k = gk[j].astype(F32) + dot_nt(vb[j], back)
        grad_v = gv[j].astype(F32) + dot(kb[j], back)
        qn, kn = qn_in[j].astype(F32), kn_in[j].astype(F32)
        d_q = qs[j] * (grad_q - qn * dot((qn * grad_q).astype(BF16), mean_of))
        d_k = ks[j] * (grad_k - kn * dot((kn * grad_k).astype(BF16), mean_of))
        d_q, d_k, d_v = d_q.astype(BF16), d_k.astype(BF16), (grad_v * valid).astype(BF16)
        rstd = rstd_in[j]
        scaled = []
        total = jnp.zeros((length, 1), F32)
        for at in (keep_at, send_at):
            rows = pl.ds(at, half)
            d_normed = (
                dot_nt(d_q, w_q[rows, mine_at])
                + dot_nt(d_k, w_k[rows, mine_at])
                + dot_nt(d_v, w_v[rows, mine_at])
            )
            d_normed = d_normed * gain[:, rows]
            part = emb[j, :, rows].astype(F32)
            scaled.append((d_normed, part))
            total = total + jnp.sum(d_normed * part, axis=1, keepdims=True)
        pull = total * (rstd * rstd / (2 * half))
        kept = rstd * (scaled[0][0] - scaled[0][1] * pull)
        row_keep[j] = kept + d_ref[:, pl.ds(keep_at, half)].astype(F32) * valid
        row_send[1 - j] = (rstd * (scaled[1][0] - scaled[1][1] * pull)).astype(BF16)


def outward(length, size, info, qa_in, kb_in, v_in, states, before, att_own, att_oth):
    core = info[1]
    pairs = Pairs(length, qa_in.shape[2], size)
    for j, out in enumerate((att_own, att_oth)):
        qa = qa_in[j]
        later = (core if j == 0 else 1 - core).astype(F32)
        whole = pairs(qa, kb_in[j], pairs.causal, v_in[j]) + dot(qa, before[...])
        out[...] = (whole + later * dot(qa, states[0, 1 - j])).astype(BF16)


def compact(length, tables, cap, info, row_keep, row_came, dest, meta, *outs):
    for j in range(2):
        grads = (row_keep[j] + row_came[j].astype(F32)).astype(BF16)
        where_to = dest[j : j + 1, :]
        for m in range(tables):
            hit = iota((cap, length), 0) + m * cap == where_to
            hit = jnp.where(hit, 1.0, 0.0).astype(BF16)
            outs[m][j * cap : (j + 1) * cap, :] = dot(hit, grads).astype(BF16)
    for m in range(tables):
        outs[m][2 * cap : 2 * cap + 16, :] = jnp.zeros((16, outs[m].shape[1]), BF16)
        outs[m][2 * cap : 2 * cap + 16, 0:cap] = meta[m]


def result(info, emb, att_own, att_came, w_out, out):
    core = info[1]
    half = att_own.shape[1]
    own = pl.ds(pl.multiple_of(core * half, half), half)
    other = pl.ds(pl.multiple_of((1 - core) * half, half), half)
    total = dot(att_own[...], w_out[own, :]) + dot(att_came[...], w_out[other, :])
    out[...] = (emb[0].astype(F32) + total).astype(BF16)


def row_sums(rows, cap, refs):
    total = None
    for ref in refs:
        coded = ref[2 * cap : 2 * cap + 16, 0:cap].astype(F32)
        hits = []
        for j in range(2):
            high, low = coded[2 * j : 2 * j + 1, :], coded[2 * j + 1 : 2 * j + 2, :]
            number = ((high - 1.0) * 32.0 + low).astype(jnp.int32)
            hits.append(jnp.where(iota((rows, cap), 0) == number, 1.0, 0.0).astype(BF16))
        if cap % 128 == 0:
            parts = [dot(jnp.concatenate(hits, 1), ref[: 2 * cap, :])]
        else:
            parts = [dot(hit, ref[j * cap : (j + 1) * cap, :]) for j, hit in enumerate(hits)]
        for part in parts:
            total = part if total is None else total + part
    return total


def early_sum(rows, cap, info, *refs):
    refs[-1][...] = row_sums(rows, cap, refs[:-1])


def owner_sum(rows, cap, chips, count, info, early, *refs):
    came, outs, acc = refs[:count], refs[count : count + chips], refs[count + chips]
    z = info[2]
    acc[...] = early[...] + row_sums(rows, cap, came)
    share = rows // chips
    for m in range(chips):
        at = pl.multiple_of((z ^ m) * share, share)
        outs[m][...] = acc[pl.ds(at, share), :].astype(BF16)


def add_up(chips, info, *refs):
    total = refs[0][...].astype(F32)
    for m in range(1, chips):
        total = total + refs[m][...].astype(F32)
    refs[chips][...] = total.astype(BF16)


def assemble(chips, share, half, info, *refs):
    own, other, (out, held, sems) = refs[:chips], refs[chips : 2 * chips], refs[2 * chips :]
    core, z = info[1], info[2]
    copies = []
    for m in range(chips):
        rows = pl.ds(pl.multiple_of((z ^ m) * share, share), share)
        for ref, side in ((own[m], core), (other[m], 1 - core)):
            held[m, :, pl.ds(pl.multiple_of(side * half, half), half)] = ref[...]
        copies.append(pltpu.make_async_copy(held.at[m], out.at[rows, :], sems.at[m]))
        copies[-1].start()
    for copy in copies:
        copy.wait()


def local(
    item_local, item_owner, hist_len, table, gain, w_query, w_key, w_value, w_out, rate, d_out
):
    tables = lax.axis_size("table")
    count = lax.axis_size("ctx")
    length = item_local.shape[1]
    rows, width = table.shape
    heads = rate.shape[0]
    size = width // heads
    half = width // 2
    chips = count // 2
    cap = 2 * length // tables
    mine = lax.axis_index("table")
    block = lax.axis_index("ctx")
    core = block % 2
    z = block // 2

    def over_table(x, m):
        return lax.ppermute(x, "table", [(i, i ^ m) for i in range(tables)])

    def over_z(x, m):
        return lax.ppermute(x, "ctx", [(i, i ^ (2 * m)) for i in range(count)])

    def swap(x):
        return lax.ppermute(x, "ctx", [(i, i ^ 1) for i in range(count)])

    def array(shape, dtype):
        return jax.ShapeDtypeStruct(shape, dtype)

    info = jnp.stack([mine, core, z, hist_len[0]]).astype(jnp.int32)
    part = rows // 2
    first, second = pl.pallas_call(
        functools.partial(pick, part),
        in_specs=[pl.BlockSpec(memory_space=pl.ANY)],
        out_specs=[pl.BlockSpec(memory_space=pltpu.VMEM)] * 2,
        out_shape=[pltpu.VMEM((part, width), BF16)] * 2,
        scratch_shapes=[pltpu.SemaphoreType.DMA((2,))],
        name="pick",
    )(table)

    def from_mask(x, masks):
        return lax.ppermute(
            x,
            ("table", "ctx"),
            [
                (t * count + c, (t ^ masks[c % 2]) * count + c)
                for t in range(tables)
                for c in range(count)
            ],
        )

    ids = item_owner[:, :, 0] * rows + item_local
    ids_row = jnp.concatenate([ids, swap(ids)], 0)
    ids_col = ids_row[:, :, None]
    if tables == 4:
        near = from_mask(first, (1, 2))
        rest = from_mask(second, (1, 2))
        far = from_mask(lax.optimization_barrier((near, ids_row))[0], (2, 1))
        fetched = [(near, (1, 2), (0, 1)), (rest, (1, 2), (1, 0)), (far, (3, 3), (0, 1))]
        early = fetched[:2]
    else:
        fetched = [(over_table(first, m), (m, m), (0, 1)) for m in range(1, tables)]
        early = []
    late = fetched[len(early) :]
    early = [(first, (0, 0), (0, 1)), (second, (0, 0), (1, 0)), *early]

    d_own = d_out[0]
    d_oth = swap(d_own)
    g, ga, dest, meta, emb_own, falling, rising, rate_row, gain_row, w_here, d_here = call(
        functools.partial(prepare, length, tables, rows, cap, size, [x[1:] for x in early]),
        info,
        (d_oth, ids_col, ids_row, *[x[0] for x in early]),
        [
            array((2, length, half), BF16),
            array((2, length, half), BF16),
            array((2, length), jnp.int32),
            array((tables, 16, cap), BF16),
            array((2, length, width), BF16),
            array((2, length, half), F32),
            array((2, length, half), F32),
            array((1, half), F32),
            array((1, width), F32),
            array((width, width), BF16),
            array((length, width), BF16),
        ],
        4 * length * width * half,
        "prepare",
        away=(rate[None, :], w_out, d_own, gain[None, :]),
        scratch=[pltpu.VMEM((1, heads), F32), pltpu.SemaphoreType.DMA((4,))],
    )
    others = [swap(x) for x, _, _ in fetched[:-1]]
    others.append(swap(lax.optimization_barrier((fetched[-1][0], dest))[0]))
    late += [(x, m[::-1], h[::-1]) for x, (_, m, h) in zip(others, fetched)]
    bits = max(chips - 1, 1).bit_length() if chips > 1 else 0
    emb, v, qa, kb, vb, qn, kn, qs, ks, rstd, states, *sends = call(
        functools.partial(project, length, [x[1:] for x in late], rows, size, chips),
        info,
        (ids_col, gain_row, w_query, w_key, w_value, g, falling, rising, emb_own, *[x[0] for x in late]),
        [array((2, length, width), BF16)]
        + [array((2, length, half), BF16)] * 6
        + [array((2, length, half), F32)] * 2
        + [array((2, length, 1), F32), array((2, 2, half, half), BF16)]
        + [array((size, half), BF16)] * bits,
        4 * length * tables * rows * width,
        "project",
    )
    came = [over_z(sends[m.bit_length() - 1], m) for m in range(1, chips)]
    gq, gk, gv = call(
        functools.partial(attend, length, size),
        info,
        (qa, kb, v, vb, g, ga, states),
        [array((2, length, half), BF16)] * 3,
        24 * length * length * half,
        "attend",
    )
    before, row_keep, row_send = call(
        functools.partial(finish, length, size, chips),
        info,
        (rate_row, kb, vb, ga, qn, kn, qs, ks, rstd, gq, gk, gv, emb, gain_row, w_query, w_key, w_value,
         d_here, d_oth, *came),
        [
            array((half, half), BF16),
            array((2, length, half), F32),
            array((2, length, half), BF16),
        ],
        12 * length * width * half,
        "finish",
    )
    row_came = swap(row_send)
    outgoing = call(
        functools.partial(compact, length, tables, cap),
        info,
        (row_keep, row_came, dest, meta),
        [array((2 * cap + 16, half), BF16)] * tables,
        4 * length * 2 * length * half,
        "compact",
    )
    arrived = [over_table(outgoing[m], m) for m in range(1, tables)]
    arrived[0], before = lax.optimization_barrier((arrived[0], before))
    (early,) = call(
        functools.partial(early_sum, rows, cap),
        info,
        (outgoing[0], arrived[0]),
        [array((rows, half), F32)],
        8 * rows * length * half,
        "early_sum",
    )
    att_own, att_oth = call(
        functools.partial(outward, length, size),
        info,
        (qa, kb, v, states, before),
        [array((length, half), BF16)] * 2,
        8 * length * length * half,
        "outward",
    )
    share = rows // chips
    early, att_oth = lax.optimization_barrier((early, att_oth))
    att_came = swap(att_oth)
    everything = call(
        functools.partial(owner_sum, rows, cap, chips, tables - 2),
        info,
        (early, *arrived[1:]),
        [array((share, half), BF16)] * chips,
        8 * rows * length * (tables - 2) * half,
        "owner_sum",
        None,
        [pltpu.VMEM((rows, half), F32)],
    )
    pieces = [over_z(everything[m], m) for m in reversed(range(1, chips))]
    if pieces:
        pieces[0], att_came = lax.optimization_barrier((pieces[0], att_came))
    (output,) = call(
        result,
        info,
        (emb, att_own, att_came, w_here),
        [array((length, width), BF16)],
        2 * length * width * width,
        "result",
        pltpu.VMEM,
    )
    pieces, output = lax.optimization_barrier((pieces, output))
    pieces = [everything[0]] + pieces
    (summed,) = call(
        functools.partial(add_up, chips),
        info,
        pieces,
        [array((share, half), BF16)],
        chips * share * half,
        "add_up",
    )
    own = [summed] + [over_z(summed, m) for m in range(1, chips)]
    other = [swap(x) for x in own]
    (table_grad,) = call(
        functools.partial(assemble, chips, share, half),
        info,
        [*own, *other],
        [array((rows, width), BF16)],
        rows * width,
        "assemble",
        pl.ANY,
        [pltpu.VMEM((chips, share, width), BF16), pltpu.SemaphoreType.DMA((chips,))],
    )
    return (output[None], table_grad)


def solution(mesh):
    return jax.shard_map(
        local,
        mesh=mesh,
        in_specs=(
            P("table", "ctx"),
            P("table", "ctx", None),
            P("table"),
            P("table", None),
            P(),
            P(),
            P(),
            P(),
            P(),
            P(),
            P("table", "ctx", None),
        ),
        out_specs=(P("table", "ctx", None), P("table", None)),
        check_vma=False,
    )
```

```python
import functools
import math

import jax
import jax.numpy as jnp
from jax import lax
from jax.experimental import pallas as pl
from jax.experimental.pallas import tpu as pltpu
from jax.sharding import PartitionSpec as P

EPS = 1e-06
F32 = jnp.float32
BF16 = jnp.bfloat16
MIB = 1 << 20


def dot(left, right, ways=(1, 0)):
    return lax.dot_general(
        left, right, (((ways[0],), (ways[1],)), ((), ())), preferred_element_type=F32
    )


def dot_nt(left, right):
    return dot(left, right, (1, 1))


def dot_tn(left, right):
    return dot(left, right, (0, 0))


def call(body, info, operands, outs, flops, name, final=None, scratch=(), away=()):
    moved = sum(math.prod(x.shape) * x.dtype.itemsize for x in (*operands, *outs))
    here = pl.BlockSpec(memory_space=pltpu.VMEM)
    operands = [pltpu.with_memory_space_constraint(x, pltpu.VMEM) for x in operands]
    return pl.pallas_call(
        body,
        in_specs=[pl.BlockSpec(memory_space=pltpu.SMEM)]
        + [here] * len(operands)
        + [pl.BlockSpec(memory_space=pl.ANY)] * len(away),
        out_specs=[pl.BlockSpec(memory_space=final) if final else here] * len(outs),
        out_shape=outs if final else [pltpu.VMEM(o.shape, o.dtype) for o in outs],
        scratch_shapes=scratch,
        compiler_params=pltpu.CompilerParams(vmem_limit_bytes=32 * MIB),
        cost_estimate=pl.CostEstimate(flops=flops, bytes_accessed=moved, transcendentals=0),
        name=name,
    )(info, *operands, *away)


def iota(shape, dim):
    return lax.broadcasted_iota(jnp.int32, shape, dim)


def head_of(shape, dim, size):
    return iota(shape, dim) // size


def valid_col(info, offset, length):
    position = offset + iota((length, 1), 0)
    return (position < info[3]).astype(F32)


def decay(rate, offset, length, chip):
    centre = (chip - 1) / 2.0
    moment = (offset + iota((length, rate.shape[1]), 0)).astype(F32) - centre
    return jnp.exp(-rate * moment), jnp.exp(rate * moment)


def pick(part, table, first, second, sems):
    core = lax.axis_index("ctx") & 1
    copies = []
    for n, (side, out) in enumerate(((core, first), (1 - core, second))):
        at = pl.multiple_of(side * part, part)
        copies.append(pltpu.make_async_copy(table.at[pl.ds(at, part), :], out, sems.at[n]))
    for copy in copies:
        copy.start()
    for copy in copies:
        copy.wait()


def held_rows(where_from, refs, info, rows):
    mine, core = info[0], info[1]
    for ref, (masks, sides) in zip(refs, where_from):
        owner = mine ^ jnp.where(core == 0, masks[0], masks[1])
        yield ref, owner * rows + jnp.where(core == 0, sides[0], sides[1]) * (rows // 2)


def chosen_rows(x, column, blocks):
    for ref, base in blocks:
        hit = column - base == iota((column.shape[0], ref.shape[0]), 1)
        x = x + dot(jnp.where(hit, 1.0, 0.0).astype(BF16), ref[...])
    return x


def prepare(
    length, tables, rows, cap, size, where_from, info, d_oth, ids_col, ids_row, *refs
):
    parts = refs[: len(where_from)]
    (rate, w_out, d_own, gain,
    g, ga, dest, meta, emb, falling, rising, rate_row, gain_row, w_here, d_here, rates, sems) = refs[len(where_from) :]
    pairs = ((rate, rates), (d_own, d_here), (w_out, w_here), (gain, gain_row))
    copies = [pltpu.make_async_copy(a, b, sems.at[n]) for n, (a, b) in enumerate(pairs)]
    for copy in copies:
        copy.start()
    mine, core, z = info[0], info[1], info[2]
    half = g.shape[2]
    blocks = list(held_rows(where_from, parts, info, rows))
    numbers = []
    for j in range(2):
        column = ids_col[j]
        row = ids_row[j : j + 1, :]
        owner_row = row // rows
        local_row = row - owner_row * rows
        order = iota((length, length), 0) < iota((length, length), 1)
        same = jnp.where((column // rows == owner_row) & order, 1.0, 0.0)
        slot = jnp.sum(same, axis=0, keepdims=True).astype(jnp.int32)
        where_to = (owner_row ^ mine) * cap + slot
        dest[j : j + 1, :] = where_to
        x = chosen_rows(jnp.zeros((length, emb.shape[2]), F32), column, blocks)
        emb[j] = x.astype(BF16)
        high = local_row // 32
        line = iota((16, length), 0) - 2 * j
        coded = jnp.where(line == 0, high + 1, jnp.where(line == 1, local_row - high * 32, 0))
        numbers.append((coded.astype(F32).astype(BF16), where_to))
    for m in range(tables):
        total = jnp.zeros((16, cap), F32)
        for coded, where_to in numbers:
            hit = iota((cap, length), 0) + m * cap == where_to
            total = total + dot_nt(coded, jnp.where(hit, 1.0, 0.0).astype(BF16))
        meta[m] = total.astype(BF16)
    for copy in copies:
        copy.wait()
    head = head_of((1, half), 1, size) + core * (half // size)
    chosen = jnp.zeros((1, half), F32)
    for h in range(rates.shape[1]):
        chosen = jnp.where(head == h, rates[0:1, h : h + 1], chosen)
    rate_row[...] = chosen
    own_rows = pl.ds(pl.multiple_of(core * half, half), half)
    for j, d_ref in enumerate((d_here, d_oth)):
        side = core if j == 0 else 1 - core
        valid = valid_col(info, (2 * z + side) * length, length)
        down, up = decay(chosen, side * length, length, 2 * length)
        falling[j], rising[j] = down, up
        grads = (dot_nt(d_ref[...], w_here[own_rows, :]) * valid).astype(BF16)
        g[j] = grads
        ga[j] = (grads.astype(F32) * down).astype(BF16)


def same_heads(half, size):
    return head_of((half, half), 0, size) == head_of((half, half), 1, size)


def project(
    length, where_from, rows, size, chips, info, ids_col, gain, w_q, w_k, w_v, g, falling, rising, emb_own, *refs
):
    parts, outs = refs[: len(where_from)], refs[len(where_from) :]
    emb, v_out, qa_out, kb_out, vb_out, qn_out, kn_out, qs_out, ks_out, rstd_out, states = outs[:11]
    sends = outs[11:]
    mine, core, z = info[0], info[1], info[2]
    half = w_q.shape[1] // 2
    mine_at = pl.ds(pl.multiple_of(core * half, half), half)
    blocks = list(held_rows(where_from, parts, info, rows))
    same_head = same_heads(half, size)
    mean_of = jnp.where(same_head, 1.0 / size, 0.0).astype(BF16)
    totals = [0.0, 0.0]
    for j in range(2):
        side = core if j == 0 else 1 - core
        column = ids_col[j]
        x = chosen_rows(emb_own[j].astype(F32), column, blocks)
        emb[j] = x.astype(BF16)
        rstd = lax.rsqrt(jnp.mean(x * x, axis=1, keepdims=True) + EPS)
        rstd_out[j] = rstd
        normed = (x * rstd * gain[...]).astype(BF16)
        valid = valid_col(info, (2 * z + side) * length, length)
        qr = dot(normed, w_q[:, mine_at])
        kr = dot(normed, w_k[:, mine_at])
        v = dot(normed, w_v[:, mine_at]) * valid
        q_rms = lax.rsqrt(dot((qr * qr).astype(BF16), mean_of) + EPS)
        k_rms = lax.rsqrt(dot((kr * kr).astype(BF16), mean_of) + EPS)
        qn = qr * q_rms
        kn = kr * k_rms * valid
        qa = (qn * falling[j] / size).astype(BF16)
        kb = (kn * rising[j] / math.sqrt(size)).astype(BF16)
        vb_out[j] = (v * rising[j]).astype(BF16)
        v = v.astype(BF16)
        v_out[j] = v
        qa_out[j] = qa
        kb_out[j] = kb
        qn_out[j] = qn.astype(BF16)
        kn_out[j] = kn.astype(BF16)
        qs_out[j] = q_rms / size
        ks_out[j] = k_rms * (valid / math.sqrt(size))
        for n, full in enumerate((dot_tn(kb, v), dot_tn(qa, g[j]))):
            full = jnp.where(same_head, full, 0.0)
            states[n, j] = full.astype(BF16)
            totals[n] = totals[n] + full

    def packed(full):
        return sum(full[h * size : (h + 1) * size, :] for h in range(half // size))

    carried, adjoint = packed(totals[0]), packed(totals[1])
    for bit, ref in enumerate(sends):
        low = ((z >> bit) & 1) == 0
        ref[...] = jnp.where(low, carried, adjoint).astype(BF16)


class Pairs:
    def __init__(self, length, half, size):
        self.length, self.count = length, half // size
        self.lane_head = head_of((length, half), 1, size)
        self.lanes = [
            jnp.where(self.lane_head == h, 1.0, 0.0).astype(BF16) for h in range(self.count)
        ]
        ahead = iota((length, length), 0) - iota((length, length), 1)
        self.causal = jnp.where(ahead >= 0, 1.0, 0.0).astype(BF16)
        self.anti = jnp.where(ahead <= 0, 1.0, 0.0).astype(BF16)

    def __call__(self, left, right, mask, value):
        length = self.length
        every = jnp.concatenate([left * only for only in self.lanes], 0)
        scores = dot_nt(every, right).astype(BF16)
        scores = [scores[h * length : (h + 1) * length] * mask for h in range(self.count)]
        values = jnp.concatenate([value * only for only in self.lanes], 0)
        total = dot(jnp.concatenate(scores, 1), values)
        return total


def attend(length, size, info, qa_in, kb_in, v_in, vb_in, g_in, ga_in, states, gq, gk, gv):
    core = info[1]
    pairs = Pairs(length, qa_in.shape[2], size)
    for j in range(2):
        qa, kb, v, vb, g, ga = qa_in[j], kb_in[j], v_in[j], vb_in[j], g_in[j], ga_in[j]
        later = (core if j == 0 else 1 - core).astype(F32)
        grad_q = pairs(ga, v, pairs.causal, kb) + later * dot_nt(ga, states[0, 1 - j])
        grad_k = pairs(vb, g, pairs.anti, qa) + (1.0 - later) * dot_nt(vb, states[1, 1 - j])
        grad_v = pairs(kb, qa, pairs.anti, g) + (1.0 - later) * dot(kb, states[1, 1 - j])
        gq[j], gk[j], gv[j] = grad_q.astype(BF16), grad_k.astype(BF16), grad_v.astype(BF16)


def finish(
    length, size, chips, info, rate, kb, vb, ga, qn_in, kn_in, qs, ks, rstd_in, gq, gk, gv,
    emb, gain, w_q, w_k, w_v, d_own, d_oth, *refs
):
    came, (before_out, row_keep, row_send) = refs[: chips - 1], refs[chips - 1 :]
    core, z = info[1], info[2]
    half = kb.shape[2]
    same_head = same_heads(half, size)
    mean_of = jnp.where(same_head, 1.0 / size, 0.0).astype(BF16)
    state = jnp.zeros((size, half), F32)
    back = jnp.zeros((size, half), F32)
    for m in range(1, chips):
        peer = z ^ m
        apart = jnp.abs(peer - z).astype(F32) * (2.0 * length)
        piece = came[m - 1][...].astype(F32) * jnp.exp(-rate[...] * apart)
        before = peer < z
        state = state + jnp.where(before, piece, 0.0)
        back = back + jnp.where(before, 0.0, piece)

    def spread(packed):
        return jnp.where(same_head, jnp.concatenate([packed] * (half // size), 0), 0.0).astype(BF16)

    state, back = spread(state), spread(back)
    before_out[...] = state
    keep_at = pl.multiple_of(core * half, half)
    mine_at = pl.ds(keep_at, half)
    send_at = pl.multiple_of((1 - core) * half, half)
    for j, d_ref in enumerate((d_own, d_oth)):
        side = core if j == 0 else 1 - core
        valid = valid_col(info, (2 * z + side) * length, length)
        grad_q = gq[j].astype(F32) + dot_nt(ga[j], state)
        grad_k = gk[j].astype(F32) + dot_nt(vb[j], back)
        grad_v = gv[j].astype(F32) + dot(kb[j], back)
        qn, kn = qn_in[j].astype(F32), kn_in[j].astype(F32)
        d_q = qs[j] * (grad_q - qn * dot((qn * grad_q).astype(BF16), mean_of))
        d_k = ks[j] * (grad_k - kn * dot((kn * grad_k).astype(BF16), mean_of))
        d_q, d_k, d_v = d_q.astype(BF16), d_k.astype(BF16), (grad_v * valid).astype(BF16)
        rstd = rstd_in[j]
        scaled = []
        total = jnp.zeros((length, 1), F32)
        for at in (keep_at, send_at):
            rows = pl.ds(at, half)
            d_normed = (
                dot_nt(d_q, w_q[rows, mine_at])
                + dot_nt(d_k, w_k[rows, mine_at])
                + dot_nt(d_v, w_v[rows, mine_at])
            )
            d_normed = d_normed * gain[:, rows]
            part = emb[j, :, rows].astype(F32)
            scaled.append((d_normed, part))
            total = total + jnp.sum(d_normed * part, axis=1, keepdims=True)
        pull = total * (rstd * rstd / (2 * half))
        kept = rstd * (scaled[0][0] - scaled[0][1] * pull)
        row_keep[j] = kept + d_ref[:, pl.ds(keep_at, half)].astype(F32) * valid
        row_send[1 - j] = (rstd * (scaled[1][0] - scaled[1][1] * pull)).astype(BF16)


def outward(length, size, info, qa_in, kb_in, v_in, states, before, att_own, att_oth):
    core = info[1]
    pairs = Pairs(length, qa_in.shape[2], size)
    for j, out in enumerate((att_own, att_oth)):
        qa = qa_in[j]
        later = (core if j == 0 else 1 - core).astype(F32)
        whole = pairs(qa, kb_in[j], pairs.causal, v_in[j]) + dot(qa, before[...])
        out[...] = (whole + later * dot(qa, states[0, 1 - j])).astype(BF16)


def compact(length, tables, cap, info, row_keep, row_came, dest, meta, *outs):
    for j in range(2):
        grads = (row_keep[j] + row_came[j].astype(F32)).astype(BF16)
        where_to = dest[j : j + 1, :]
        for m in range(tables):
            hit = iota((cap, length), 0) + m * cap == where_to
            hit = jnp.where(hit, 1.0, 0.0).astype(BF16)
            outs[m][j * cap : (j + 1) * cap, :] = dot(hit, grads).astype(BF16)
    for m in range(tables):
        outs[m][2 * cap : 2 * cap + 16, :] = jnp.zeros((16, outs[m].shape[1]), BF16)
        outs[m][2 * cap : 2 * cap + 16, 0:cap] = meta[m]


def result(info, emb, att_own, att_came, w_out, out):
    core = info[1]
    half = att_own.shape[1]
    own = pl.ds(pl.multiple_of(core * half, half), half)
    other = pl.ds(pl.multiple_of((1 - core) * half, half), half)
    total = dot(att_own[...], w_out[own, :]) + dot(att_came[...], w_out[other, :])
    out[...] = (emb[0].astype(F32) + total).astype(BF16)


def row_sums(rows, cap, refs):
    total = None
    for ref in refs:
        coded = ref[2 * cap : 2 * cap + 16, 0:cap].astype(F32)
        hits = []
        for j in range(2):
            high, low = coded[2 * j : 2 * j + 1, :], coded[2 * j + 1 : 2 * j + 2, :]
            number = ((high - 1.0) * 32.0 + low).astype(jnp.int32)
            hits.append(jnp.where(iota((rows, cap), 0) == number, 1.0, 0.0).astype(BF16))
        if cap % 128 == 0:
            parts = [dot(jnp.concatenate(hits, 1), ref[: 2 * cap, :])]
        else:
            parts = [dot(hit, ref[j * cap : (j + 1) * cap, :]) for j, hit in enumerate(hits)]
        for part in parts:
            total = part if total is None else total + part
    return total


def early_sum(rows, cap, info, *refs):
    refs[-1][...] = row_sums(rows, cap, refs[:-1])


def owner_sum(rows, cap, chips, count, info, early, *refs):
    came, outs, acc = refs[:count], refs[count : count + chips], refs[count + chips]
    z = info[2]
    acc[...] = early[...] + row_sums(rows, cap, came)
    share = rows // chips
    for m in range(chips):
        at = pl.multiple_of((z ^ m) * share, share)
        outs[m][...] = acc[pl.ds(at, share), :].astype(BF16)


def add_up(chips, info, *refs):
    total = refs[0][...].astype(F32)
    for m in range(1, chips):
        total = total + refs[m][...].astype(F32)
    refs[chips][...] = total.astype(BF16)


def assemble(chips, share, half, info, *refs):
    own, other, (out, held, sems) = refs[:chips], refs[chips : 2 * chips], refs[2 * chips :]
    core, z = info[1], info[2]
    copies = []
    for m in range(chips):
        rows = pl.ds(pl.multiple_of((z ^ m) * share, share), share)
        for ref, side in ((own[m], core), (other[m], 1 - core)):
            held[m, :, pl.ds(pl.multiple_of(side * half, half), half)] = ref[...]
        copies.append(pltpu.make_async_copy(held.at[m], out.at[rows, :], sems.at[m]))
        copies[-1].start()
    for copy in copies:
        copy.wait()


def local(
    item_local, item_owner, hist_len, table, gain, w_query, w_key, w_value, w_out, rate, d_out
):
    tables = lax.axis_size("table")
    count = lax.axis_size("ctx")
    length = item_local.shape[1]
    rows, width = table.shape
    heads = rate.shape[0]
    size = width // heads
    half = width // 2
    chips = count // 2
    cap = 2 * length // tables
    mine = lax.axis_index("table")
    block = lax.axis_index("ctx")
    core = block % 2
    z = block // 2

    def over_table(x, m):
        return lax.ppermute(x, "table", [(i, i ^ m) for i in range(tables)])

    def over_z(x, m):
        return lax.ppermute(x, "ctx", [(i, i ^ (2 * m)) for i in range(count)])

    def swap(x):
        return lax.ppermute(x, "ctx", [(i, i ^ 1) for i in range(count)])

    def array(shape, dtype):
        return jax.ShapeDtypeStruct(shape, dtype)

    info = jnp.stack([mine, core, z, hist_len[0]]).astype(jnp.int32)
    part = rows // 2
    first, second = pl.pallas_call(
        functools.partial(pick, part),
        in_specs=[pl.BlockSpec(memory_space=pl.ANY)],
        out_specs=[pl.BlockSpec(memory_space=pltpu.VMEM)] * 2,
        out_shape=[pltpu.VMEM((part, width), BF16)] * 2,
        scratch_shapes=[pltpu.SemaphoreType.DMA((2,))],
        name="pick",
    )(table)

    def from_mask(x, masks):
        return lax.ppermute(
            x,
            ("table", "ctx"),
            [
                (t * count + c, (t ^ masks[c % 2]) * count + c)
                for t in range(tables)
                for c in range(count)
            ],
        )

    ids = item_owner[:, :, 0] * rows + item_local
    ids_row = jnp.concatenate([ids, swap(ids)], 0)
    ids_col = ids_row[:, :, None]
    if tables == 4:
        near = from_mask(first, (1, 2))
        rest = from_mask(second, (1, 2))
        far = from_mask(lax.optimization_barrier((near, ids_row))[0], (2, 1))
        fetched = [(near, (1, 2), (0, 1)), (rest, (1, 2), (1, 0)), (far, (3, 3), (0, 1))]
        early = fetched[:1]
    else:
        fetched = [(over_table(first, m), (m, m), (0, 1)) for m in range(1, tables)]
        early = []
    late = fetched[len(early) :]
    early = [(first, (0, 0), (0, 1)), (second, (0, 0), (1, 0)), *early]

    d_own = d_out[0]
    d_oth = swap(d_own)
    g, ga, dest, meta, emb_own, falling, rising, rate_row, gain_row, w_here, d_here = call(
        functools.partial(prepare, length, tables, rows, cap, size, [x[1:] for x in early]),
        info,
        (d_oth, ids_col, ids_row, *[x[0] for x in early]),
        [
            array((2, length, half), BF16),
            array((2, length, half), BF16),
            array((2, length), jnp.int32),
            array((tables, 16, cap), BF16),
            array((2, length, width), BF16),
            array((2, length, half), F32),
            array((2, length, half), F32),
            array((1, half), F32),
            array((1, width), F32),
            array((width, width), BF16),
            array((length, width), BF16),
        ],
        4 * length * width * half,
        "prepare",
        away=(rate[None, :], w_out, d_own, gain[None, :]),
        scratch=[pltpu.VMEM((1, heads), F32), pltpu.SemaphoreType.DMA((4,))],
    )
    others = [swap(fetched[0][0])]
    others += [swap(lax.optimization_barrier((x, meta))[0]) for x, _, _ in fetched[1:]]
    late += [(x, m[::-1], h[::-1]) for x, (_, m, h) in zip(others, fetched)]
    bits = max(chips - 1, 1).bit_length() if chips > 1 else 0
    emb, v, qa, kb, vb, qn, kn, qs, ks, rstd, states, *sends = call(
        functools.partial(project, length, [x[1:] for x in late], rows, size, chips),
        info,
        (ids_col, gain_row, w_query, w_key, w_value, g, falling, rising, emb_own, *[x[0] for x in late]),
        [array((2, length, width), BF16)]
        + [array((2, length, half), BF16)] * 6
        + [array((2, length, half), F32)] * 2
        + [array((2, length, 1), F32), array((2, 2, half, half), BF16)]
        + [array((size, half), BF16)] * bits,
        4 * length * tables * rows * width,
        "project",
    )
    came = [over_z(sends[m.bit_length() - 1], m) for m in range(1, chips)]
    gq, gk, gv = call(
        functools.partial(attend, length, size),
        info,
        (qa, kb, v, vb, g, ga, states),
        [array((2, length, half), BF16)] * 3,
        24 * length * length * half,
        "attend",
    )
    before, row_keep, row_send = call(
        functools.partial(finish, length, size, chips),
        info,
        (rate_row, kb, vb, ga, qn, kn, qs, ks, rstd, gq, gk, gv, emb, gain_row, w_query, w_key, w_value,
         d_here, d_oth, *came),
        [
            array((half, half), BF16),
            array((2, length, half), F32),
            array((2, length, half), BF16),
        ],
        12 * length * width * half,
        "finish",
    )
    row_came = swap(row_send)
    outgoing = call(
        functools.partial(compact, length, tables, cap),
        info,
        (row_keep, row_came, dest, meta),
        [array((2 * cap + 16, half), BF16)] * tables,
        4 * length * 2 * length * half,
        "compact",
    )
    arrived = [over_table(outgoing[m], m) for m in range(1, tables)]
    arrived[0], before = lax.optimization_barrier((arrived[0], before))
    (early,) = call(
        functools.partial(early_sum, rows, cap),
        info,
        (outgoing[0], arrived[0]),
        [array((rows, half), F32)],
        8 * rows * length * half,
        "early_sum",
    )
    att_own, att_oth = call(
        functools.partial(outward, length, size),
        info,
        (qa, kb, v, states, before),
        [array((length, half), BF16)] * 2,
        8 * length * length * half,
        "outward",
    )
    share = rows // chips
    early, att_oth = lax.optimization_barrier((early, att_oth))
    att_came = swap(att_oth)
    everything = call(
        functools.partial(owner_sum, rows, cap, chips, tables - 2),
        info,
        (early, *arrived[1:]),
        [array((share, half), BF16)] * chips,
        8 * rows * length * (tables - 2) * half,
        "owner_sum",
        None,
        [pltpu.VMEM((rows, half), F32)],
    )
    pieces = [over_z(everything[m], m) for m in (*range(chips - 1, chips), *range(1, chips - 1)) if m]
    if pieces:
        pieces[0], att_came = lax.optimization_barrier((pieces[0], att_came))
    (output,) = call(
        result,
        info,
        (emb, att_own, att_came, w_here),
        [array((length, width), BF16)],
        2 * length * width * width,
        "result",
        pltpu.VMEM,
    )
    pieces, output = lax.optimization_barrier((pieces, output))
    pieces = [everything[0]] + pieces
    (summed,) = call(
        functools.partial(add_up, chips),
        info,
        pieces,
        [array((share, half), BF16)],
        chips * share * half,
        "add_up",
    )
    own = [summed] + [over_z(summed, m) for m in range(1, chips)]
    other = [swap(x) for x in own]
    (table_grad,) = call(
        functools.partial(assemble, chips, share, half),
        info,
        [*own, *other],
        [array((rows, width), BF16)],
        rows * width,
        "assemble",
        pl.ANY,
        [pltpu.VMEM((chips, share, width), BF16), pltpu.SemaphoreType.DMA((chips,))],
    )
    return (output[None], table_grad)


def solution(mesh):
    return jax.shard_map(
        local,
        mesh=mesh,
        in_specs=(
            P("table", "ctx"),
            P("table", "ctx", None),
            P("table"),
            P("table", None),
            P(),
            P(),
            P(),
            P(),
            P(),
            P(),
            P("table", "ctx", None),
        ),
        out_specs=(P("table", "ctx", None), P("table", None)),
        check_vma=False,
    )
```

```python
import functools
import math

import jax
import jax.numpy as jnp
from jax import lax
from jax.experimental import pallas as pl
from jax.experimental.pallas import tpu as pltpu
from jax.sharding import PartitionSpec as P

EPS = 1e-06
F32 = jnp.float32
BF16 = jnp.bfloat16
MIB = 1 << 20


def dot(left, right, ways=(1, 0)):
    return lax.dot_general(
        left, right, (((ways[0],), (ways[1],)), ((), ())), preferred_element_type=F32
    )


def dot_nt(left, right):
    return dot(left, right, (1, 1))


def dot_tn(left, right):
    return dot(left, right, (0, 0))


def call(body, info, operands, outs, flops, name, final=None, scratch=(), away=()):
    moved = sum(math.prod(x.shape) * x.dtype.itemsize for x in (*operands, *outs))
    here = pl.BlockSpec(memory_space=pltpu.VMEM)
    operands = [pltpu.with_memory_space_constraint(x, pltpu.VMEM) for x in operands]
    return pl.pallas_call(
        body,
        in_specs=[pl.BlockSpec(memory_space=pltpu.SMEM)]
        + [here] * len(operands)
        + [pl.BlockSpec(memory_space=pl.ANY)] * len(away),
        out_specs=[pl.BlockSpec(memory_space=final) if final else here] * len(outs),
        out_shape=outs if final else [pltpu.VMEM(o.shape, o.dtype) for o in outs],
        scratch_shapes=scratch,
        compiler_params=pltpu.CompilerParams(vmem_limit_bytes=32 * MIB),
        cost_estimate=pl.CostEstimate(flops=flops, bytes_accessed=moved, transcendentals=0),
        name=name,
    )(info, *operands, *away)


def iota(shape, dim):
    return lax.broadcasted_iota(jnp.int32, shape, dim)


def head_of(shape, dim, size):
    return iota(shape, dim) // size


def valid_col(info, offset, length):
    position = offset + iota((length, 1), 0)
    return (position < info[3]).astype(F32)


def decay(rate, offset, length, chip):
    centre = (chip - 1) / 2.0
    moment = (offset + iota((length, rate.shape[1]), 0)).astype(F32) - centre
    return jnp.exp(-rate * moment), jnp.exp(rate * moment)


def pick(part, table, first, second, sems):
    core = lax.axis_index("ctx") & 1
    copies = []
    for n, (side, out) in enumerate(((core, first), (1 - core, second))):
        at = pl.multiple_of(side * part, part)
        copies.append(pltpu.make_async_copy(table.at[pl.ds(at, part), :], out, sems.at[n]))
    for copy in copies:
        copy.start()
    for copy in copies:
        copy.wait()


def held_rows(where_from, refs, info, rows):
    mine, core = info[0], info[1]
    for ref, (masks, sides) in zip(refs, where_from):
        owner = mine ^ jnp.where(core == 0, masks[0], masks[1])
        yield ref, owner * rows + jnp.where(core == 0, sides[0], sides[1]) * (rows // 2)


def chosen_rows(column, blocks):
    hits = []
    for ref, base in blocks:
        hit = column - base == iota((column.shape[0], ref.shape[0]), 1)
        hits.append(jnp.where(hit, 1.0, 0.0).astype(BF16))
    return dot(jnp.concatenate(hits, 1), jnp.concatenate([ref[...] for ref, _ in blocks], 0))


def both(ref):
    return jnp.concatenate([ref[0], ref[1]], 0)


def valid_both(info, length):
    core, z = info[1], info[2]
    return jnp.concatenate(
        [valid_col(info, (2 * z + side) * length, length) for side in (core, 1 - core)], 0
    )


def prepare(
    length, tables, rows, cap, size, where_from, info, d_oth, ids_col, ids_row, *refs
):
    parts = refs[: len(where_from)]
    (rate, w_out, d_own, gain,
    g, ga, dest, meta, emb, falling, rising, rate_row, gain_row, w_here, d_here, rates, sems) = refs[len(where_from) :]
    pairs = ((rate, rates), (d_own, d_here), (w_out, w_here), (gain, gain_row))
    copies = [pltpu.make_async_copy(a, b, sems.at[n]) for n, (a, b) in enumerate(pairs)]
    for copy in copies:
        copy.start()
    mine, core, z = info[0], info[1], info[2]
    half = g.shape[2]
    blocks = list(held_rows(where_from, parts, info, rows))
    numbers = []
    for j in range(2):
        column = ids_col[j]
        row = ids_row[j : j + 1, :]
        owner_row = row // rows
        local_row = row - owner_row * rows
        order = iota((length, length), 0) < iota((length, length), 1)
        same = jnp.where((column // rows == owner_row) & order, 1.0, 0.0)
        slot = jnp.sum(same, axis=0, keepdims=True).astype(jnp.int32)
        where_to = (owner_row ^ mine) * cap + slot
        dest[j : j + 1, :] = where_to
        x = chosen_rows(column, blocks)
        emb[j] = x.astype(BF16)
        high = local_row // 32
        line = iota((16, length), 0) - 2 * j
        coded = jnp.where(line == 0, high + 1, jnp.where(line == 1, local_row - high * 32, 0))
        numbers.append((coded.astype(F32).astype(BF16), where_to))
    for m in range(tables):
        total = jnp.zeros((16, cap), F32)
        for coded, where_to in numbers:
            hit = iota((cap, length), 0) + m * cap == where_to
            total = total + dot_nt(coded, jnp.where(hit, 1.0, 0.0).astype(BF16))
        meta[m] = total.astype(BF16)
    for copy in copies:
        copy.wait()
    head = head_of((1, half), 1, size) + core * (half // size)
    chosen = jnp.zeros((1, half), F32)
    for h in range(rates.shape[1]):
        chosen = jnp.where(head == h, rates[0:1, h : h + 1], chosen)
    rate_row[...] = chosen
    own_rows = pl.ds(pl.multiple_of(core * half, half), half)
    for j, d_ref in enumerate((d_here, d_oth)):
        side = core if j == 0 else 1 - core
        valid = valid_col(info, (2 * z + side) * length, length)
        down, up = decay(chosen, side * length, length, 2 * length)
        falling[j], rising[j] = down, up
        grads = (dot_nt(d_ref[...], w_here[own_rows, :]) * valid).astype(BF16)
        g[j] = grads
        ga[j] = (grads.astype(F32) * down).astype(BF16)


def same_heads(half, size):
    return head_of((half, half), 0, size) == head_of((half, half), 1, size)


def project(
    length, where_from, rows, size, chips, info, ids_col, gain, w_q, w_k, w_v, g, falling, rising, emb_own, *refs
):
    parts, outs = refs[: len(where_from)], refs[len(where_from) :]
    emb, v_out, qa_out, kb_out, vb_out, qn_out, kn_out, qs_out, ks_out, rstd_out, states = outs[:11]
    sends = outs[11:]
    mine, core, z = info[0], info[1], info[2]
    half = w_q.shape[1] // 2
    mine_at = pl.ds(pl.multiple_of(core * half, half), half)
    blocks = list(held_rows(where_from, parts, info, rows))
    same_head = same_heads(half, size)
    mean_of = jnp.where(same_head, 1.0 / size, 0.0).astype(BF16)
    x = both(emb_own).astype(F32) + chosen_rows(both(ids_col), blocks)
    rstd = lax.rsqrt(jnp.mean(x * x, axis=1, keepdims=True) + EPS)
    normed = (x * rstd * gain[...]).astype(BF16)
    valid = valid_both(info, length)
    qr = dot(normed, w_q[:, mine_at])
    kr = dot(normed, w_k[:, mine_at])
    v = dot(normed, w_v[:, mine_at]) * valid
    q_rms = lax.rsqrt(dot((qr * qr).astype(BF16), mean_of) + EPS)
    k_rms = lax.rsqrt(dot((kr * kr).astype(BF16), mean_of) + EPS)
    qn = qr * q_rms
    kn = kr * k_rms * valid
    up = both(rising)
    qa = (qn * both(falling) / size).astype(BF16)
    kb = (kn * up / math.sqrt(size)).astype(BF16)
    vb = (v * up).astype(BF16)
    v = v.astype(BF16)
    qs, ks = q_rms / size, k_rms * (valid / math.sqrt(size))
    totals = [0.0, 0.0]
    for j in range(2):
        at = slice(j * length, (j + 1) * length)
        for n, full in enumerate((dot_tn(kb[at], v[at]), dot_tn(qa[at], g[j]))):
            full = jnp.where(same_head, full, 0.0)
            states[n, j] = full.astype(BF16)
            totals[n] = totals[n] + full
        for out, value in (
            (emb, x), (rstd_out, rstd), (v_out, v), (qa_out, qa), (kb_out, kb), (vb_out, vb),
            (qn_out, qn), (kn_out, kn), (qs_out, qs), (ks_out, ks),
        ):
            out[j] = value[at].astype(out.dtype)

    def packed(full):
        return sum(full[h * size : (h + 1) * size, :] for h in range(half // size))

    carried, adjoint = packed(totals[0]), packed(totals[1])
    for bit, ref in enumerate(sends):
        low = ((z >> bit) & 1) == 0
        ref[...] = jnp.where(low, carried, adjoint).astype(BF16)


class Pairs:
    def __init__(self, length, half, size):
        self.length, self.count = length, half // size
        self.lane_head = head_of((length, half), 1, size)
        self.lanes = [
            jnp.where(self.lane_head == h, 1.0, 0.0).astype(BF16) for h in range(self.count)
        ]
        ahead = iota((length, length), 0) - iota((length, length), 1)
        self.causal = jnp.where(ahead >= 0, 1.0, 0.0).astype(BF16)
        self.anti = jnp.where(ahead <= 0, 1.0, 0.0).astype(BF16)

    def __call__(self, left, right, mask, value):
        length = self.length
        every = jnp.concatenate([left * only for only in self.lanes], 0)
        scores = dot_nt(every, right).astype(BF16)
        scores = [scores[h * length : (h + 1) * length] * mask for h in range(self.count)]
        values = jnp.concatenate([value * only for only in self.lanes], 0)
        total = dot(jnp.concatenate(scores, 1), values)
        return total


def attend(length, size, info, qa_in, kb_in, v_in, vb_in, g_in, ga_in, states, gq, gk, gv):
    core = info[1]
    pairs = Pairs(length, qa_in.shape[2], size)
    for j in range(2):
        qa, kb, v, vb, g, ga = qa_in[j], kb_in[j], v_in[j], vb_in[j], g_in[j], ga_in[j]
        later = (core if j == 0 else 1 - core).astype(F32)
        grad_q = pairs(ga, v, pairs.causal, kb) + later * dot_nt(ga, states[0, 1 - j])
        grad_k = pairs(vb, g, pairs.anti, qa) + (1.0 - later) * dot_nt(vb, states[1, 1 - j])
        grad_v = pairs(kb, qa, pairs.anti, g) + (1.0 - later) * dot(kb, states[1, 1 - j])
        gq[j], gk[j], gv[j] = grad_q.astype(BF16), grad_k.astype(BF16), grad_v.astype(BF16)


def finish(
    length, size, chips, info, rate, kb, vb, ga, qn_in, kn_in, qs, ks, rstd_in, gq, gk, gv,
    emb, gain, w_q, w_k, w_v, d_own, d_oth, *refs
):
    came, (before_out, row_keep, row_send) = refs[: chips - 1], refs[chips - 1 :]
    core, z = info[1], info[2]
    half = kb.shape[2]
    same_head = same_heads(half, size)
    mean_of = jnp.where(same_head, 1.0 / size, 0.0).astype(BF16)
    state = jnp.zeros((size, half), F32)
    back = jnp.zeros((size, half), F32)
    for m in range(1, chips):
        peer = z ^ m
        apart = jnp.abs(peer - z).astype(F32) * (2.0 * length)
        piece = came[m - 1][...].astype(F32) * jnp.exp(-rate[...] * apart)
        before = peer < z
        state = state + jnp.where(before, piece, 0.0)
        back = back + jnp.where(before, 0.0, piece)

    def spread(packed):
        return jnp.where(same_head, jnp.concatenate([packed] * (half // size), 0), 0.0).astype(BF16)

    state, back = spread(state), spread(back)
    before_out[...] = state
    keep_at = pl.multiple_of(core * half, half)
    mine_at = pl.ds(keep_at, half)
    send_at = pl.multiple_of((1 - core) * half, half)
    for j, d_ref in enumerate((d_own, d_oth)):
        side = core if j == 0 else 1 - core
        valid = valid_col(info, (2 * z + side) * length, length)
        grad_q = gq[j].astype(F32) + dot_nt(ga[j], state)
        grad_k = gk[j].astype(F32) + dot_nt(vb[j], back)
        grad_v = gv[j].astype(F32) + dot(kb[j], back)
        qn, kn = qn_in[j].astype(F32), kn_in[j].astype(F32)
        d_q = qs[j] * (grad_q - qn * dot((qn * grad_q).astype(BF16), mean_of))
        d_k = ks[j] * (grad_k - kn * dot((kn * grad_k).astype(BF16), mean_of))
        d_q, d_k, d_v = d_q.astype(BF16), d_k.astype(BF16), (grad_v * valid).astype(BF16)
        rstd = rstd_in[j]
        scaled = []
        total = jnp.zeros((length, 1), F32)
        for at in (keep_at, send_at):
            rows = pl.ds(at, half)
            weights = jnp.concatenate([w[rows, mine_at] for w in (w_q, w_k, w_v)], 1)
            d_normed = dot_nt(jnp.concatenate([d_q, d_k, d_v], 1), weights) * gain[:, rows]
            part = emb[j, :, rows].astype(F32)
            scaled.append((d_normed, part))
            total = total + jnp.sum(d_normed * part, axis=1, keepdims=True)
        pull = total * (rstd * rstd / (2 * half))
        kept = rstd * (scaled[0][0] - scaled[0][1] * pull)
        row_keep[j] = kept + d_ref[:, pl.ds(keep_at, half)].astype(F32) * valid
        row_send[1 - j] = (rstd * (scaled[1][0] - scaled[1][1] * pull)).astype(BF16)


def outward(length, size, info, qa_in, kb_in, v_in, states, before, att_own, att_oth):
    core = info[1]
    pairs = Pairs(length, qa_in.shape[2], size)
    for j, out in enumerate((att_own, att_oth)):
        qa = qa_in[j]
        later = (core if j == 0 else 1 - core).astype(F32)
        whole = pairs(qa, kb_in[j], pairs.causal, v_in[j]) + dot(qa, before[...])
        out[...] = (whole + later * dot(qa, states[0, 1 - j])).astype(BF16)


def compact(length, tables, cap, info, row_keep, row_came, dest, meta, *outs):
    for j in range(2):
        grads = (row_keep[j] + row_came[j].astype(F32)).astype(BF16)
        where_to = dest[j : j + 1, :]
        for m in range(tables):
            hit = iota((cap, length), 0) + m * cap == where_to
            hit = jnp.where(hit, 1.0, 0.0).astype(BF16)
            outs[m][j * cap : (j + 1) * cap, :] = dot(hit, grads).astype(BF16)
    for m in range(tables):
        outs[m][2 * cap : 2 * cap + 16, :] = jnp.zeros((16, outs[m].shape[1]), BF16)
        outs[m][2 * cap : 2 * cap + 16, 0:cap] = meta[m]


def result(info, emb, att_own, att_came, w_out, out):
    core = info[1]
    half = att_own.shape[1]
    own = pl.ds(pl.multiple_of(core * half, half), half)
    other = pl.ds(pl.multiple_of((1 - core) * half, half), half)
    total = dot(att_own[...], w_out[own, :]) + dot(att_came[...], w_out[other, :])
    out[...] = (emb[0].astype(F32) + total).astype(BF16)


def row_sums(rows, cap, refs):
    total = None
    for ref in refs:
        coded = ref[2 * cap : 2 * cap + 16, 0:cap].astype(F32)
        hits = []
        for j in range(2):
            high, low = coded[2 * j : 2 * j + 1, :], coded[2 * j + 1 : 2 * j + 2, :]
            number = ((high - 1.0) * 32.0 + low).astype(jnp.int32)
            hits.append(jnp.where(iota((rows, cap), 0) == number, 1.0, 0.0).astype(BF16))
        if cap % 128 == 0:
            parts = [dot(jnp.concatenate(hits, 1), ref[: 2 * cap, :])]
        else:
            parts = [dot(hit, ref[j * cap : (j + 1) * cap, :]) for j, hit in enumerate(hits)]
        for part in parts:
            total = part if total is None else total + part
    return total


def early_sum(rows, cap, info, *refs):
    refs[-1][...] = row_sums(rows, cap, refs[:-1])


def owner_sum(rows, cap, chips, count, info, early, *refs):
    came, outs, acc = refs[:count], refs[count : count + chips], refs[count + chips]
    z = info[2]
    acc[...] = early[...] + row_sums(rows, cap, came)
    share = rows // chips
    for m in range(chips):
        at = pl.multiple_of((z ^ m) * share, share)
        outs[m][...] = acc[pl.ds(at, share), :].astype(BF16)


def add_up(chips, info, *refs):
    total = refs[0][...].astype(F32)
    for m in range(1, chips):
        total = total + refs[m][...].astype(F32)
    refs[chips][...] = total.astype(BF16)


def assemble(chips, share, half, info, *refs):
    own, other, (out, held, sems) = refs[:chips], refs[chips : 2 * chips], refs[2 * chips :]
    core, z = info[1], info[2]
    copies = []
    for m in range(chips):
        rows = pl.ds(pl.multiple_of((z ^ m) * share, share), share)
        for ref, side in ((own[m], core), (other[m], 1 - core)):
            held[m, :, pl.ds(pl.multiple_of(side * half, half), half)] = ref[...]
        copies.append(pltpu.make_async_copy(held.at[m], out.at[rows, :], sems.at[m]))
        copies[-1].start()
    for copy in copies:
        copy.wait()


def local(
    item_local, item_owner, hist_len, table, gain, w_query, w_key, w_value, w_out, rate, d_out
):
    tables = lax.axis_size("table")
    count = lax.axis_size("ctx")
    length = item_local.shape[1]
    rows, width = table.shape
    heads = rate.shape[0]
    size = width // heads
    half = width // 2
    chips = count // 2
    cap = 2 * length // tables
    mine = lax.axis_index("table")
    block = lax.axis_index("ctx")
    core = block % 2
    z = block // 2

    def over_table(x, m):
        return lax.ppermute(x, "table", [(i, i ^ m) for i in range(tables)])

    def over_z(x, m):
        return lax.ppermute(x, "ctx", [(i, i ^ (2 * m)) for i in range(count)])

    def swap(x):
        return lax.ppermute(x, "ctx", [(i, i ^ 1) for i in range(count)])

    def array(shape, dtype):
        return jax.ShapeDtypeStruct(shape, dtype)

    info = jnp.stack([mine, core, z, hist_len[0]]).astype(jnp.int32)
    part = rows // 2
    first, second = pl.pallas_call(
        functools.partial(pick, part),
        in_specs=[pl.BlockSpec(memory_space=pl.ANY)],
        out_specs=[pl.BlockSpec(memory_space=pltpu.VMEM)] * 2,
        out_shape=[pltpu.VMEM((part, width), BF16)] * 2,
        scratch_shapes=[pltpu.SemaphoreType.DMA((2,))],
        name="pick",
    )(table)

    def from_mask(x, masks):
        return lax.ppermute(
            x,
            ("table", "ctx"),
            [
                (t * count + c, (t ^ masks[c % 2]) * count + c)
                for t in range(tables)
                for c in range(count)
            ],
        )

    ids = item_owner[:, :, 0] * rows + item_local
    ids_row = jnp.concatenate([ids, swap(ids)], 0)
    ids_col = ids_row[:, :, None]
    if tables == 4:
        near = from_mask(first, (1, 2))
        rest = from_mask(second, (1, 2))
        far = from_mask(lax.optimization_barrier((near, ids_row))[0], (2, 1))
        fetched = [(near, (1, 2), (0, 1)), (rest, (1, 2), (1, 0)), (far, (3, 3), (0, 1))]
        early = fetched[:1]
    else:
        fetched = [(over_table(first, m), (m, m), (0, 1)) for m in range(1, tables)]
        early = []
    late = fetched[len(early) :]
    early = [(first, (0, 0), (0, 1)), (second, (0, 0), (1, 0)), *early]

    d_own = d_out[0]
    d_oth = swap(d_own)
    g, ga, dest, meta, emb_own, falling, rising, rate_row, gain_row, w_here, d_here = call(
        functools.partial(prepare, length, tables, rows, cap, size, [x[1:] for x in early]),
        info,
        (d_oth, ids_col, ids_row, *[x[0] for x in early]),
        [
            array((2, length, half), BF16),
            array((2, length, half), BF16),
            array((2, length), jnp.int32),
            array((tables, 16, cap), BF16),
            array((2, length, width), BF16),
            array((2, length, half), F32),
            array((2, length, half), F32),
            array((1, half), F32),
            array((1, width), F32),
            array((width, width), BF16),
            array((length, width), BF16),
        ],
        4 * length * width * half,
        "prepare",
        away=(rate[None, :], w_out, d_own, gain[None, :]),
        scratch=[pltpu.VMEM((1, heads), F32), pltpu.SemaphoreType.DMA((4,))],
    )
    others = [swap(fetched[0][0])]
    others += [swap(lax.optimization_barrier((x, meta))[0]) for x, _, _ in fetched[1:]]
    late += [(x, m[::-1], h[::-1]) for x, (_, m, h) in zip(others, fetched)]
    bits = max(chips - 1, 1).bit_length() if chips > 1 else 0
    emb, v, qa, kb, vb, qn, kn, qs, ks, rstd, states, *sends = call(
        functools.partial(project, length, [x[1:] for x in late], rows, size, chips),
        info,
        (ids_col, gain_row, w_query, w_key, w_value, g, falling, rising, emb_own, *[x[0] for x in late]),
        [array((2, length, width), BF16)]
        + [array((2, length, half), BF16)] * 6
        + [array((2, length, half), F32)] * 2
        + [array((2, length, 1), F32), array((2, 2, half, half), BF16)]
        + [array((size, half), BF16)] * bits,
        4 * length * tables * rows * width,
        "project",
    )
    came = [over_z(sends[m.bit_length() - 1], m) for m in range(1, chips)]
    gq, gk, gv = call(
        functools.partial(attend, length, size),
        info,
        (qa, kb, v, vb, g, ga, states),
        [array((2, length, half), BF16)] * 3,
        24 * length * length * half,
        "attend",
    )
    before, row_keep, row_send = call(
        functools.partial(finish, length, size, chips),
        info,
        (rate_row, kb, vb, ga, qn, kn, qs, ks, rstd, gq, gk, gv, emb, gain_row, w_query, w_key, w_value,
         d_here, d_oth, *came),
        [
            array((half, half), BF16),
            array((2, length, half), F32),
            array((2, length, half), BF16),
        ],
        12 * length * width * half,
        "finish",
    )
    row_came = swap(row_send)
    outgoing = call(
        functools.partial(compact, length, tables, cap),
        info,
        (row_keep, row_came, dest, meta),
        [array((2 * cap + 16, half), BF16)] * tables,
        4 * length * 2 * length * half,
        "compact",
    )
    arrived = [over_table(outgoing[m], m) for m in range(1, tables)]
    arrived[0], before = lax.optimization_barrier((arrived[0], before))
    (early,) = call(
        functools.partial(early_sum, rows, cap),
        info,
        (outgoing[0], arrived[0]),
        [array((rows, half), F32)],
        8 * rows * length * half,
        "early_sum",
    )
    att_own, att_oth = call(
        functools.partial(outward, length, size),
        info,
        (qa, kb, v, states, before),
        [array((length, half), BF16)] * 2,
        8 * length * length * half,
        "outward",
    )
    share = rows // chips
    early, att_oth = lax.optimization_barrier((early, att_oth))
    att_came = swap(att_oth)
    everything = call(
        functools.partial(owner_sum, rows, cap, chips, tables - 2),
        info,
        (early, *arrived[1:]),
        [array((share, half), BF16)] * chips,
        8 * rows * length * (tables - 2) * half,
        "owner_sum",
        None,
        [pltpu.VMEM((rows, half), F32)],
    )
    pieces = [over_z(everything[m], m) for m in (*range(chips - 1, chips), *range(1, chips - 1)) if m]
    if pieces:
        pieces[0], att_came = lax.optimization_barrier((pieces[0], att_came))
    (output,) = call(
        result,
        info,
        (emb, att_own, att_came, w_here),
        [array((length, width), BF16)],
        2 * length * width * width,
        "result",
        pltpu.VMEM,
    )
    pieces, output = lax.optimization_barrier((pieces, output))
    pieces = [everything[0]] + pieces
    (summed,) = call(
        functools.partial(add_up, chips),
        info,
        pieces,
        [array((share, half), BF16)],
        chips * share * half,
        "add_up",
    )
    own = [summed] + [over_z(summed, m) for m in range(1, chips)]
    other = [swap(x) for x in own]
    (table_grad,) = call(
        functools.partial(assemble, chips, share, half),
        info,
        [*own, *other],
        [array((rows, width), BF16)],
        rows * width,
        "assemble",
        pl.ANY,
        [pltpu.VMEM((chips, share, width), BF16), pltpu.SemaphoreType.DMA((chips,))],
    )
    return (output[None], table_grad)


def solution(mesh):
    return jax.shard_map(
        local,
        mesh=mesh,
        in_specs=(
            P("table", "ctx"),
            P("table", "ctx", None),
            P("table"),
            P("table", None),
            P(),
            P(),
            P(),
            P(),
            P(),
            P(),
            P("table", "ctx", None),
        ),
        out_specs=(P("table", "ctx", None), P("table", None)),
        check_vma=False,
    )
```

```python
import functools
import math

import jax
import jax.numpy as jnp
from jax import lax
from jax.experimental import pallas as pl
from jax.experimental.pallas import tpu as pltpu
from jax.sharding import PartitionSpec as P

EPS = 1e-06
F32 = jnp.float32
BF16 = jnp.bfloat16
MIB = 1 << 20


def dot(left, right, ways=(1, 0)):
    return lax.dot_general(
        left, right, (((ways[0],), (ways[1],)), ((), ())), preferred_element_type=F32
    )


def dot_nt(left, right):
    return dot(left, right, (1, 1))


def dot_tn(left, right):
    return dot(left, right, (0, 0))


def call(body, info, operands, outs, flops, name, final=None, scratch=(), away=()):
    moved = sum(math.prod(x.shape) * x.dtype.itemsize for x in (*operands, *outs))
    here = pl.BlockSpec(memory_space=pltpu.VMEM)
    operands = [pltpu.with_memory_space_constraint(x, pltpu.VMEM) for x in operands]
    return pl.pallas_call(
        body,
        in_specs=[pl.BlockSpec(memory_space=pltpu.SMEM)]
        + [here] * len(operands)
        + [pl.BlockSpec(memory_space=pl.ANY)] * len(away),
        out_specs=[pl.BlockSpec(memory_space=final) if final else here] * len(outs),
        out_shape=outs if final else [pltpu.VMEM(o.shape, o.dtype) for o in outs],
        scratch_shapes=scratch,
        compiler_params=pltpu.CompilerParams(vmem_limit_bytes=32 * MIB),
        cost_estimate=pl.CostEstimate(flops=flops, bytes_accessed=moved, transcendentals=0),
        name=name,
    )(info, *operands, *away)


def iota(shape, dim):
    return lax.broadcasted_iota(jnp.int32, shape, dim)


def head_of(shape, dim, size):
    return iota(shape, dim) // size


def valid_col(info, offset, length):
    position = offset + iota((length, 1), 0)
    return (position < info[3]).astype(F32)


def decay(rate, offset, length, chip):
    centre = (chip - 1) / 2.0
    moment = (offset + iota((length, rate.shape[1]), 0)).astype(F32) - centre
    return jnp.exp(-rate * moment), jnp.exp(rate * moment)


def pick(part, table, first, second, sems):
    core = lax.axis_index("ctx") & 1
    copies = []
    for n, (side, out) in enumerate(((core, first), (1 - core, second))):
        at = pl.multiple_of(side * part, part)
        copies.append(pltpu.make_async_copy(table.at[pl.ds(at, part), :], out, sems.at[n]))
    for copy in copies:
        copy.start()
    for copy in copies:
        copy.wait()


def held_rows(where_from, refs, info, rows):
    mine, core = info[0], info[1]
    for ref, (masks, sides) in zip(refs, where_from):
        owner = mine ^ jnp.where(core == 0, masks[0], masks[1])
        yield ref, owner * rows + jnp.where(core == 0, sides[0], sides[1]) * (rows // 2)


def chosen_rows(column, blocks):
    hits = []
    for ref, base in blocks:
        hit = column - base == iota((column.shape[0], ref.shape[0]), 1)
        hits.append(jnp.where(hit, 1.0, 0.0).astype(BF16))
    return dot(jnp.concatenate(hits, 1), jnp.concatenate([ref[...] for ref, _ in blocks], 0))


def both(ref):
    return jnp.concatenate([ref[0], ref[1]], 0)


def valid_both(info, length):
    core, z = info[1], info[2]
    return jnp.concatenate(
        [valid_col(info, (2 * z + side) * length, length) for side in (core, 1 - core)], 0
    )


def prepare(
    length, tables, rows, cap, size, where_from, info, d_oth, ids_col, ids_row, *refs
):
    parts = refs[: len(where_from)]
    (rate, w_out, d_own, gain,
    g, ga, dest, meta, emb, falling, rising, rate_row, gain_row, w_here, d_here, rates, sems) = refs[len(where_from) :]
    pairs = ((rate, rates), (d_own, d_here), (w_out, w_here), (gain, gain_row))
    copies = [pltpu.make_async_copy(a, b, sems.at[n]) for n, (a, b) in enumerate(pairs)]
    for copy in copies:
        copy.start()
    mine, core, z = info[0], info[1], info[2]
    half = g.shape[2]
    blocks = list(held_rows(where_from, parts, info, rows))
    numbers = []
    for j in range(2):
        column = ids_col[j]
        row = ids_row[j : j + 1, :]
        owner_row = row // rows
        local_row = row - owner_row * rows
        order = iota((length, length), 0) < iota((length, length), 1)
        same = jnp.where((column // rows == owner_row) & order, 1.0, 0.0)
        slot = jnp.sum(same, axis=0, keepdims=True).astype(jnp.int32)
        where_to = (owner_row ^ mine) * cap + slot
        dest[j : j + 1, :] = where_to
        x = chosen_rows(column, blocks)
        emb[j] = x.astype(BF16)
        high = local_row // 32
        line = iota((16, length), 0) - 2 * j
        coded = jnp.where(line == 0, high + 1, jnp.where(line == 1, local_row - high * 32, 0))
        numbers.append((coded.astype(F32).astype(BF16), where_to))
    for m in range(tables):
        total = jnp.zeros((16, cap), F32)
        for coded, where_to in numbers:
            hit = iota((cap, length), 0) + m * cap == where_to
            total = total + dot_nt(coded, jnp.where(hit, 1.0, 0.0).astype(BF16))
        meta[m] = total.astype(BF16)
    for copy in copies:
        copy.wait()
    head = head_of((1, half), 1, size) + core * (half // size)
    chosen = jnp.zeros((1, half), F32)
    for h in range(rates.shape[1]):
        chosen = jnp.where(head == h, rates[0:1, h : h + 1], chosen)
    rate_row[...] = chosen
    own_rows = pl.ds(pl.multiple_of(core * half, half), half)
    for j, d_ref in enumerate((d_here, d_oth)):
        side = core if j == 0 else 1 - core
        valid = valid_col(info, (2 * z + side) * length, length)
        down, up = decay(chosen, side * length, length, 2 * length)
        falling[j], rising[j] = down, up
        grads = (dot_nt(d_ref[...], w_here[own_rows, :]) * valid).astype(BF16)
        g[j] = grads
        ga[j] = (grads.astype(F32) * down).astype(BF16)


def same_heads(half, size):
    return head_of((half, half), 0, size) == head_of((half, half), 1, size)


def project(
    length, where_from, rows, size, chips, info, ids_col, gain, w_q, w_k, w_v, g, falling, rising, emb_own, *refs
):
    parts, outs = refs[: len(where_from)], refs[len(where_from) :]
    emb, v_out, qa_out, kb_out, vb_out, qn_out, kn_out, qs_out, ks_out, rstd_out, states = outs[:11]
    sends = outs[11:]
    mine, core, z = info[0], info[1], info[2]
    half = w_q.shape[1] // 2
    mine_at = pl.ds(pl.multiple_of(core * half, half), half)
    blocks = list(held_rows(where_from, parts, info, rows))
    same_head = same_heads(half, size)
    mean_of = jnp.where(same_head, 1.0 / size, 0.0).astype(BF16)
    x = both(emb_own).astype(F32) + chosen_rows(both(ids_col), blocks)
    rstd = lax.rsqrt(jnp.mean(x * x, axis=1, keepdims=True) + EPS)
    normed = (x * rstd * gain[...]).astype(BF16)
    valid = valid_both(info, length)
    qr = dot(normed, w_q[:, mine_at])
    kr = dot(normed, w_k[:, mine_at])
    v = dot(normed, w_v[:, mine_at]) * valid
    q_rms = lax.rsqrt(dot((qr * qr).astype(BF16), mean_of) + EPS)
    k_rms = lax.rsqrt(dot((kr * kr).astype(BF16), mean_of) + EPS)
    qn = qr * q_rms
    kn = kr * k_rms * valid
    up = both(rising)
    qa = (qn * both(falling) / size).astype(BF16)
    kb = (kn * up / math.sqrt(size)).astype(BF16)
    vb = (v * up).astype(BF16)
    v = v.astype(BF16)
    qs, ks = q_rms / size, k_rms * (valid / math.sqrt(size))
    totals = [0.0, 0.0]
    for j in range(2):
        at = slice(j * length, (j + 1) * length)
        for n, full in enumerate((dot_tn(kb[at], v[at]), dot_tn(qa[at], g[j]))):
            full = jnp.where(same_head, full, 0.0)
            states[n, j] = full.astype(BF16)
            totals[n] = totals[n] + full
        for out, value in (
            (emb, x), (rstd_out, rstd), (v_out, v), (qa_out, qa), (kb_out, kb), (vb_out, vb),
            (qn_out, qn), (kn_out, kn), (qs_out, qs), (ks_out, ks),
        ):
            out[j] = value[at].astype(out.dtype)

    def packed(full):
        return sum(full[h * size : (h + 1) * size, :] for h in range(half // size))

    carried, adjoint = packed(totals[0]), packed(totals[1])
    for bit, ref in enumerate(sends):
        low = ((z >> bit) & 1) == 0
        ref[...] = jnp.where(low, carried, adjoint).astype(BF16)


class Pairs:
    def __init__(self, length, half, size):
        self.length, self.count = length, half // size
        self.lane_head = head_of((length, half), 1, size)
        self.lanes = [
            jnp.where(self.lane_head == h, 1.0, 0.0).astype(BF16) for h in range(self.count)
        ]
        ahead = iota((length, length), 0) - iota((length, length), 1)
        self.causal = jnp.where(ahead >= 0, 1.0, 0.0).astype(BF16)
        self.anti = jnp.where(ahead <= 0, 1.0, 0.0).astype(BF16)

    def __call__(self, left, right, mask, value):
        length = self.length
        every = jnp.concatenate([left * only for only in self.lanes], 0)
        scores = dot_nt(every, right).astype(BF16)
        scores = [scores[h * length : (h + 1) * length] * mask for h in range(self.count)]
        values = jnp.concatenate([value * only for only in self.lanes], 0)
        total = dot(jnp.concatenate(scores, 1), values)
        return total


def attend(length, size, info, qa_in, kb_in, v_in, vb_in, g_in, ga_in, states, gq, gk, gv):
    core = info[1]
    pairs = Pairs(length, qa_in.shape[2], size)
    for j in range(2):
        qa, kb, v, vb, g, ga = qa_in[j], kb_in[j], v_in[j], vb_in[j], g_in[j], ga_in[j]
        later = (core if j == 0 else 1 - core).astype(F32)
        grad_q = pairs(ga, v, pairs.causal, kb) + later * dot_nt(ga, states[0, 1 - j])
        grad_k = pairs(vb, g, pairs.anti, qa) + (1.0 - later) * dot_nt(vb, states[1, 1 - j])
        grad_v = pairs(kb, qa, pairs.anti, g) + (1.0 - later) * dot(kb, states[1, 1 - j])
        gq[j], gk[j], gv[j] = grad_q.astype(BF16), grad_k.astype(BF16), grad_v.astype(BF16)


def finish(
    length, size, chips, info, rate, kb, vb, ga, qn_in, kn_in, qs, ks, rstd_in, gq, gk, gv,
    emb, gain, w_q, w_k, w_v, d_own, d_oth, *refs
):
    came, (before_out, row_keep, row_send) = refs[: chips - 1], refs[chips - 1 :]
    core, z = info[1], info[2]
    half = kb.shape[2]
    same_head = same_heads(half, size)
    mean_of = jnp.where(same_head, 1.0 / size, 0.0).astype(BF16)
    mean_all = jnp.full((half, half), 0.5 / half, BF16)
    state = jnp.zeros((size, half), F32)
    back = jnp.zeros((size, half), F32)
    for m in range(1, chips):
        peer = z ^ m
        apart = jnp.abs(peer - z).astype(F32) * (2.0 * length)
        piece = came[m - 1][...].astype(F32) * jnp.exp(-rate[...] * apart)
        before = peer < z
        state = state + jnp.where(before, piece, 0.0)
        back = back + jnp.where(before, 0.0, piece)

    def spread(packed):
        return jnp.where(same_head, jnp.concatenate([packed] * (half // size), 0), 0.0).astype(BF16)

    state, back = spread(state), spread(back)
    before_out[...] = state
    keep_at = pl.multiple_of(core * half, half)
    mine_at = pl.ds(keep_at, half)
    send_at = pl.multiple_of((1 - core) * half, half)
    for j, d_ref in enumerate((d_own, d_oth)):
        side = core if j == 0 else 1 - core
        valid = valid_col(info, (2 * z + side) * length, length)
        grad_q = gq[j].astype(F32) + dot_nt(ga[j], state)
        grad_k = gk[j].astype(F32) + dot_nt(vb[j], back)
        grad_v = gv[j].astype(F32) + dot(kb[j], back)
        qn, kn = qn_in[j].astype(F32), kn_in[j].astype(F32)
        d_q = qs[j] * (grad_q - qn * dot((qn * grad_q).astype(BF16), mean_of))
        d_k = ks[j] * (grad_k - kn * dot((kn * grad_k).astype(BF16), mean_of))
        d_q, d_k, d_v = d_q.astype(BF16), d_k.astype(BF16), (grad_v * valid).astype(BF16)
        rstd = rstd_in[j]
        scaled = []
        total = 0.0
        for at in (keep_at, send_at):
            rows = pl.ds(at, half)
            weights = jnp.concatenate([w[rows, mine_at] for w in (w_q, w_k, w_v)], 1)
            d_normed = dot_nt(jnp.concatenate([d_q, d_k, d_v], 1), weights) * gain[:, rows]
            part = emb[j, :, rows].astype(F32)
            scaled.append((d_normed, part))
            total = total + d_normed * part
        pull = dot(total.astype(BF16), mean_all) * (rstd * rstd)
        kept = rstd * (scaled[0][0] - scaled[0][1] * pull)
        row_keep[j] = kept + d_ref[:, pl.ds(keep_at, half)].astype(F32) * valid
        row_send[1 - j] = (rstd * (scaled[1][0] - scaled[1][1] * pull)).astype(BF16)


def outward(length, size, info, qa_in, kb_in, v_in, states, before, att_own, att_oth):
    core = info[1]
    pairs = Pairs(length, qa_in.shape[2], size)
    for j, out in enumerate((att_own, att_oth)):
        qa = qa_in[j]
        later = (core if j == 0 else 1 - core).astype(F32)
        whole = pairs(qa, kb_in[j], pairs.causal, v_in[j]) + dot(qa, before[...])
        out[...] = (whole + later * dot(qa, states[0, 1 - j])).astype(BF16)


def compact(length, tables, cap, info, row_keep, row_came, dest, meta, *outs):
    for j in range(2):
        grads = (row_keep[j] + row_came[j].astype(F32)).astype(BF16)
        where_to = dest[j : j + 1, :]
        for m in range(tables):
            hit = iota((cap, length), 0) + m * cap == where_to
            hit = jnp.where(hit, 1.0, 0.0).astype(BF16)
            outs[m][j * cap : (j + 1) * cap, :] = dot(hit, grads).astype(BF16)
    for m in range(tables):
        outs[m][2 * cap : 2 * cap + 16, :] = jnp.zeros((16, outs[m].shape[1]), BF16)
        outs[m][2 * cap : 2 * cap + 16, 0:cap] = meta[m]


def result(info, emb, att_own, att_came, w_out, out):
    core = info[1]
    half = att_own.shape[1]
    own = pl.ds(pl.multiple_of(core * half, half), half)
    other = pl.ds(pl.multiple_of((1 - core) * half, half), half)
    total = dot(att_own[...], w_out[own, :]) + dot(att_came[...], w_out[other, :])
    out[...] = (emb[0].astype(F32) + total).astype(BF16)


def row_sums(rows, cap, refs):
    total = None
    for ref in refs:
        coded = ref[2 * cap : 2 * cap + 16, 0:cap].astype(F32)
        hits = []
        for j in range(2):
            high, low = coded[2 * j : 2 * j + 1, :], coded[2 * j + 1 : 2 * j + 2, :]
            number = ((high - 1.0) * 32.0 + low).astype(jnp.int32)
            hits.append(jnp.where(iota((rows, cap), 0) == number, 1.0, 0.0).astype(BF16))
        if cap % 128 == 0:
            parts = [dot(jnp.concatenate(hits, 1), ref[: 2 * cap, :])]
        else:
            parts = [dot(hit, ref[j * cap : (j + 1) * cap, :]) for j, hit in enumerate(hits)]
        for part in parts:
            total = part if total is None else total + part
    return total


def early_sum(rows, cap, info, *refs):
    refs[-1][...] = row_sums(rows, cap, refs[:-1])


def peer(z, core, masks):
    return z ^ jnp.where(core == 0, masks[0], masks[1])


def owner_sum(rows, cap, masks, count, info, early, *refs):
    came, outs, acc = refs[:count], refs[count:-1], refs[-1]
    core, z = info[1], info[2]
    acc[...] = early[...] + row_sums(rows, cap, came)
    share = rows // len(masks)
    for m, pair in enumerate(masks):
        at = pl.multiple_of(peer(z, core, pair) * share, share)
        outs[m][...] = acc[pl.ds(at, share), :].astype(BF16)


def add_up(chips, info, *refs):
    total = refs[0][...].astype(F32)
    for m in range(1, chips):
        total = total + refs[m][...].astype(F32)
    refs[chips][...] = total.astype(BF16)


def assemble(masks, share, half, info, *refs):
    chips = len(masks)
    own, other, (out, sems) = refs[:chips], refs[chips : 2 * chips], refs[2 * chips :]
    core, z = info[1], info[2]
    copies = []
    for m, pair in enumerate(masks):
        for n, (ref, side) in enumerate(((own[m], core), (other[m], 1 - core))):
            rows = pl.ds(pl.multiple_of(peer(z, side, pair) * share, share), share)
            columns = pl.ds(pl.multiple_of(side * half, half), half)
            copies.append(pltpu.make_async_copy(ref, out.at[rows, columns], sems.at[2 * m + n]))
            copies[-1].start()
    for copy in copies:
        copy.wait()


def local(
    item_local, item_owner, hist_len, table, gain, w_query, w_key, w_value, w_out, rate, d_out
):
    tables = lax.axis_size("table")
    count = lax.axis_size("ctx")
    length = item_local.shape[1]
    rows, width = table.shape
    heads = rate.shape[0]
    size = width // heads
    half = width // 2
    chips = count // 2
    cap = 2 * length // tables
    mine = lax.axis_index("table")
    block = lax.axis_index("ctx")
    core = block % 2
    z = block // 2

    def over_table(x, m):
        return lax.ppermute(x, "table", [(i, i ^ m) for i in range(tables)])

    def over_z(x, m):
        return lax.ppermute(x, "ctx", [(i, i ^ (2 * m)) for i in range(count)])

    def swap(x):
        return lax.ppermute(x, "ctx", [(i, i ^ 1) for i in range(count)])

    def array(shape, dtype):
        return jax.ShapeDtypeStruct(shape, dtype)

    info = jnp.stack([mine, core, z, hist_len[0]]).astype(jnp.int32)
    part = rows // 2
    first, second = pl.pallas_call(
        functools.partial(pick, part),
        in_specs=[pl.BlockSpec(memory_space=pl.ANY)],
        out_specs=[pl.BlockSpec(memory_space=pltpu.VMEM)] * 2,
        out_shape=[pltpu.VMEM((part, width), BF16)] * 2,
        scratch_shapes=[pltpu.SemaphoreType.DMA((2,))],
        name="pick",
    )(table)

    def from_mask(x, masks):
        return lax.ppermute(
            x,
            ("table", "ctx"),
            [
                (t * count + c, (t ^ masks[c % 2]) * count + c)
                for t in range(tables)
                for c in range(count)
            ],
        )

    ids = item_owner[:, :, 0] * rows + item_local
    ids_row = jnp.concatenate([ids, swap(ids)], 0)
    ids_col = ids_row[:, :, None]
    if tables == 4:
        near = from_mask(first, (1, 2))
        rest = from_mask(second, (1, 2))
        far = from_mask(lax.optimization_barrier((near, ids_row))[0], (2, 1))
        fetched = [(near, (1, 2), (0, 1)), (rest, (1, 2), (1, 0)), (far, (3, 3), (0, 1))]
        early = fetched[:1]
    else:
        fetched = [(over_table(first, m), (m, m), (0, 1)) for m in range(1, tables)]
        early = []
    late = fetched[len(early) :]
    early = [(first, (0, 0), (0, 1)), (second, (0, 0), (1, 0)), *early]

    d_own = d_out[0]
    d_oth = swap(d_own)
    g, ga, dest, meta, emb_own, falling, rising, rate_row, gain_row, w_here, d_here = call(
        functools.partial(prepare, length, tables, rows, cap, size, [x[1:] for x in early]),
        info,
        (d_oth, ids_col, ids_row, *[x[0] for x in early]),
        [
            array((2, length, half), BF16),
            array((2, length, half), BF16),
            array((2, length), jnp.int32),
            array((tables, 16, cap), BF16),
            array((2, length, width), BF16),
            array((2, length, half), F32),
            array((2, length, half), F32),
            array((1, half), F32),
            array((1, width), F32),
            array((width, width), BF16),
            array((length, width), BF16),
        ],
        4 * length * width * half,
        "prepare",
        away=(rate[None, :], w_out, d_own, gain[None, :]),
        scratch=[pltpu.VMEM((1, heads), F32), pltpu.SemaphoreType.DMA((4,))],
    )
    others = [swap(fetched[0][0])]
    others += [swap(lax.optimization_barrier((x, meta))[0]) for x, _, _ in fetched[1:]]
    late += [(x, m[::-1], h[::-1]) for x, (_, m, h) in zip(others, fetched)]
    bits = max(chips - 1, 1).bit_length() if chips > 1 else 0
    emb, v, qa, kb, vb, qn, kn, qs, ks, rstd, states, *sends = call(
        functools.partial(project, length, [x[1:] for x in late], rows, size, chips),
        info,
        (ids_col, gain_row, w_query, w_key, w_value, g, falling, rising, emb_own, *[x[0] for x in late]),
        [array((2, length, width), BF16)]
        + [array((2, length, half), BF16)] * 6
        + [array((2, length, half), F32)] * 2
        + [array((2, length, 1), F32), array((2, 2, half, half), BF16)]
        + [array((size, half), BF16)] * bits,
        4 * length * tables * rows * width,
        "project",
    )
    came = [over_z(sends[m.bit_length() - 1], m) for m in range(1, chips)]
    gq, gk, gv = call(
        functools.partial(attend, length, size),
        info,
        (qa, kb, v, vb, g, ga, states),
        [array((2, length, half), BF16)] * 3,
        24 * length * length * half,
        "attend",
    )
    before, row_keep, row_send = call(
        functools.partial(finish, length, size, chips),
        info,
        (rate_row, kb, vb, ga, qn, kn, qs, ks, rstd, gq, gk, gv, emb, gain_row, w_query, w_key, w_value,
         d_here, d_oth, *came),
        [
            array((half, half), BF16),
            array((2, length, half), F32),
            array((2, length, half), BF16),
        ],
        12 * length * width * half,
        "finish",
    )
    row_came = swap(row_send)
    outgoing = call(
        functools.partial(compact, length, tables, cap),
        info,
        (row_keep, row_came, dest, meta),
        [array((2 * cap + 16, half), BF16)] * tables,
        4 * length * 2 * length * half,
        "compact",
    )
    arrived = [over_table(outgoing[m], m) for m in range(1, tables)]
    arrived[0], before = lax.optimization_barrier((arrived[0], before))
    (early,) = call(
        functools.partial(early_sum, rows, cap),
        info,
        (outgoing[0], arrived[0]),
        [array((rows, half), F32)],
        8 * rows * length * half,
        "early_sum",
    )
    att_own, att_oth = call(
        functools.partial(outward, length, size),
        info,
        (qa, kb, v, states, before),
        [array((length, half), BF16)] * 2,
        8 * length * length * half,
        "outward",
    )
    share = rows // chips
    each = list(range(1, chips))
    adding = [(0, 0)] + ([(3, 3), (1, 1), (2, 2)] if chips == 4 else list(zip(each, each)))
    giving = [(0, 0)] + ([(1, 3), (2, 1), (3, 2)] if chips == 4 else list(zip(each, each)))

    def by_core(x, masks):
        return lax.ppermute(x, "ctx", [(c, c ^ (2 * masks[c % 2])) for c in range(count)])

    early, att_oth = lax.optimization_barrier((early, att_oth))
    att_came = swap(att_oth)
    everything = call(
        functools.partial(owner_sum, rows, cap, adding, tables - 2),
        info,
        (early, *arrived[1:]),
        [array((share, half), BF16)] * chips,
        8 * rows * length * (tables - 2) * half,
        "owner_sum",
        None,
        [pltpu.VMEM((rows, half), F32)],
    )
    pieces = [by_core(x, pair) for x, pair in zip(everything[1:], adding[1:])]
    if pieces:
        pieces[0], att_came = lax.optimization_barrier((pieces[0], att_came))
    (output,) = call(
        result,
        info,
        (emb, att_own, att_came, w_here),
        [array((length, width), BF16)],
        2 * length * width * width,
        "result",
        pltpu.VMEM,
    )
    pieces, output = lax.optimization_barrier((pieces, output))
    pieces = [everything[0]] + pieces
    (summed,) = call(
        functools.partial(add_up, chips),
        info,
        pieces,
        [array((share, half), BF16)],
        chips * share * half,
        "add_up",
    )
    own = [summed] + [by_core(summed, pair) for pair in giving[1:]]
    other = [swap(x) for x in own]
    (table_grad,) = call(
        functools.partial(assemble, giving, share, half),
        info,
        [*own, *other],
        [array((rows, width), BF16)],
        rows * width,
        "assemble",
        pl.ANY,
        [pltpu.SemaphoreType.DMA((2 * chips,))],
    )
    return (output[None], table_grad)


def solution(mesh):
    return jax.shard_map(
        local,
        mesh=mesh,
        in_specs=(
            P("table", "ctx"),
            P("table", "ctx", None),
            P("table"),
            P("table", None),
            P(),
            P(),
            P(),
            P(),
            P(),
            P(),
            P("table", "ctx", None),
        ),
        out_specs=(P("table", "ctx", None), P("table", None)),
        check_vma=False,
    )
```

```python
import functools
import math

import jax
import jax.numpy as jnp
from jax import lax
from jax.experimental import pallas as pl
from jax.experimental.pallas import tpu as pltpu
from jax.sharding import PartitionSpec as P

EPS = 1e-06
F32 = jnp.float32
BF16 = jnp.bfloat16
MIB = 1 << 20


def dot(left, right, ways=(1, 0)):
    return lax.dot_general(
        left, right, (((ways[0],), (ways[1],)), ((), ())), preferred_element_type=F32
    )


def dot_nt(left, right):
    return dot(left, right, (1, 1))


def dot_tn(left, right):
    return dot(left, right, (0, 0))


def call(body, info, operands, outs, flops, name, final=None, scratch=(), away=()):
    moved = sum(math.prod(x.shape) * x.dtype.itemsize for x in (*operands, *outs))
    here = pl.BlockSpec(memory_space=pltpu.VMEM)
    operands = [pltpu.with_memory_space_constraint(x, pltpu.VMEM) for x in operands]
    return pl.pallas_call(
        body,
        in_specs=[pl.BlockSpec(memory_space=pltpu.SMEM)]
        + [here] * len(operands)
        + [pl.BlockSpec(memory_space=pl.ANY)] * len(away),
        out_specs=[pl.BlockSpec(memory_space=final) if final else here] * len(outs),
        out_shape=outs if final else [pltpu.VMEM(o.shape, o.dtype) for o in outs],
        scratch_shapes=scratch,
        compiler_params=pltpu.CompilerParams(vmem_limit_bytes=16 * MIB),
        cost_estimate=pl.CostEstimate(flops=flops, bytes_accessed=moved, transcendentals=0),
        name=name,
    )(info, *operands, *away)


def iota(shape, dim):
    return lax.broadcasted_iota(jnp.int32, shape, dim)


def head_of(shape, dim, size):
    return iota(shape, dim) // size


def valid_col(info, offset, length):
    position = offset + iota((length, 1), 0)
    return (position < info[3]).astype(F32)


def decay(rate, offset, length, chip):
    centre = (chip - 1) / 2.0
    moment = (offset + iota((length, rate.shape[1]), 0)).astype(F32) - centre
    return jnp.exp(-rate * moment), jnp.exp(rate * moment)


def pick(part, table, first, second, sems):
    core = lax.axis_index("ctx") & 1
    copies = []
    for n, (side, out) in enumerate(((core, first), (1 - core, second))):
        at = pl.multiple_of(side * part, part)
        copies.append(pltpu.make_async_copy(table.at[pl.ds(at, part), :], out, sems.at[n]))
    for copy in copies:
        copy.start()
    for copy in copies:
        copy.wait()


def held_rows(where_from, refs, info, rows):
    mine, core = info[0], info[1]
    for ref, (masks, sides) in zip(refs, where_from):
        owner = mine ^ jnp.where(core == 0, masks[0], masks[1])
        yield ref, owner * rows + jnp.where(core == 0, sides[0], sides[1]) * (rows // 2)


def chosen_rows(column, blocks):
    hits = []
    for ref, base in blocks:
        hit = column - base == iota((column.shape[0], ref.shape[0]), 1)
        hits.append(jnp.where(hit, 1.0, 0.0).astype(BF16))
    return dot(jnp.concatenate(hits, 1), jnp.concatenate([ref[...] for ref, _ in blocks], 0))


def both(ref):
    return jnp.concatenate([ref[0], ref[1]], 0)


def valid_both(info, length):
    core, z = info[1], info[2]
    return jnp.concatenate(
        [valid_col(info, (2 * z + side) * length, length) for side in (core, 1 - core)], 0
    )


def prepare(
    length, tables, rows, cap, size, where_from, info, d_oth, ids_col, ids_row, *refs
):
    parts = refs[: len(where_from)]
    (rate, w_out, d_own, gain,
    g, ga, dest, meta, emb, falling, rising, rate_row, gain_row, w_here, d_here, rates, sems) = refs[len(where_from) :]
    pairs = ((rate, rates), (d_own, d_here), (w_out, w_here), (gain, gain_row))
    copies = [pltpu.make_async_copy(a, b, sems.at[n]) for n, (a, b) in enumerate(pairs)]
    for copy in copies:
        copy.start()
    mine, core, z = info[0], info[1], info[2]
    half = g.shape[2]
    blocks = list(held_rows(where_from, parts, info, rows))
    numbers = []
    for j in range(2):
        column = ids_col[j]
        row = ids_row[j : j + 1, :]
        owner_row = row // rows
        local_row = row - owner_row * rows
        order = iota((length, length), 0) < iota((length, length), 1)
        same = jnp.where((column // rows == owner_row) & order, 1.0, 0.0)
        slot = jnp.sum(same, axis=0, keepdims=True).astype(jnp.int32)
        where_to = (owner_row ^ mine) * cap + slot
        dest[j : j + 1, :] = where_to
        x = chosen_rows(column, blocks)
        emb[j] = x.astype(BF16)
        high = local_row // 32
        line = iota((16, length), 0) - 2 * j
        coded = jnp.where(line == 0, high + 1, jnp.where(line == 1, local_row - high * 32, 0))
        numbers.append((coded.astype(F32).astype(BF16), where_to))
    for m in range(tables):
        total = jnp.zeros((16, cap), F32)
        for coded, where_to in numbers:
            hit = iota((cap, length), 0) + m * cap == where_to
            total = total + dot_nt(coded, jnp.where(hit, 1.0, 0.0).astype(BF16))
        meta[m] = total.astype(BF16)
    for copy in copies:
        copy.wait()
    head = head_of((1, half), 1, size) + core * (half // size)
    chosen = jnp.zeros((1, half), F32)
    for h in range(rates.shape[1]):
        chosen = jnp.where(head == h, rates[0:1, h : h + 1], chosen)
    rate_row[...] = chosen
    own_rows = pl.ds(pl.multiple_of(core * half, half), half)
    for j, d_ref in enumerate((d_here, d_oth)):
        side = core if j == 0 else 1 - core
        valid = valid_col(info, (2 * z + side) * length, length)
        down, up = decay(chosen, side * length, length, 2 * length)
        falling[j], rising[j] = down, up
        grads = (dot_nt(d_ref[...], w_here[own_rows, :]) * valid).astype(BF16)
        g[j] = grads
        ga[j] = (grads.astype(F32) * down).astype(BF16)


def same_heads(half, size):
    return head_of((half, half), 0, size) == head_of((half, half), 1, size)


def project(
    length, where_from, rows, size, chips, info, ids_col, gain, w_q, w_k, w_v, g, falling, rising, emb_own, *refs
):
    parts, outs = refs[: len(where_from)], refs[len(where_from) :]
    emb, v_out, qa_out, kb_out, vb_out, qn_out, kn_out, qs_out, ks_out, rstd_out, states = outs[:11]
    sends = outs[11:]
    mine, core, z = info[0], info[1], info[2]
    half = w_q.shape[1] // 2
    mine_at = pl.ds(pl.multiple_of(core * half, half), half)
    blocks = list(held_rows(where_from, parts, info, rows))
    same_head = same_heads(half, size)
    mean_of = jnp.where(same_head, 1.0 / size, 0.0).astype(BF16)
    x = both(emb_own).astype(F32) + chosen_rows(both(ids_col), blocks)
    rstd = lax.rsqrt(jnp.mean(x * x, axis=1, keepdims=True) + EPS)
    normed = (x * rstd * gain[...]).astype(BF16)
    valid = valid_both(info, length)
    qr = dot(normed, w_q[:, mine_at])
    kr = dot(normed, w_k[:, mine_at])
    v = dot(normed, w_v[:, mine_at]) * valid
    q_rms = lax.rsqrt(dot((qr * qr).astype(BF16), mean_of) + EPS)
    k_rms = lax.rsqrt(dot((kr * kr).astype(BF16), mean_of) + EPS)
    qn = qr * q_rms
    kn = kr * k_rms * valid
    up = both(rising)
    qa = (qn * both(falling) / size).astype(BF16)
    kb = (kn * up / math.sqrt(size)).astype(BF16)
    vb = (v * up).astype(BF16)
    v = v.astype(BF16)
    qs, ks = q_rms / size, k_rms * (valid / math.sqrt(size))
    totals = [0.0, 0.0]
    for j in range(2):
        at = slice(j * length, (j + 1) * length)
        for n, full in enumerate((dot_tn(kb[at], v[at]), dot_tn(qa[at], g[j]))):
            full = jnp.where(same_head, full, 0.0)
            states[n, j] = full.astype(BF16)
            totals[n] = totals[n] + full
        for out, value in (
            (emb, x), (rstd_out, rstd), (v_out, v), (qa_out, qa), (kb_out, kb), (vb_out, vb),
            (qn_out, qn), (kn_out, kn), (qs_out, qs), (ks_out, ks),
        ):
            out[j] = value[at].astype(out.dtype)

    def packed(full):
        return sum(full[h * size : (h + 1) * size, :] for h in range(half // size))

    carried, adjoint = packed(totals[0]), packed(totals[1])
    for bit, ref in enumerate(sends):
        low = ((z >> bit) & 1) == 0
        ref[...] = jnp.where(low, carried, adjoint).astype(BF16)


class Pairs:
    def __init__(self, length, half, size):
        self.length, self.count = length, half // size
        self.lane_head = head_of((length, half), 1, size)
        self.lanes = [
            jnp.where(self.lane_head == h, 1.0, 0.0).astype(BF16) for h in range(self.count)
        ]
        ahead = iota((length, length), 0) - iota((length, length), 1)
        self.causal = jnp.where(ahead >= 0, 1.0, 0.0).astype(BF16)
        self.anti = jnp.where(ahead <= 0, 1.0, 0.0).astype(BF16)

    def __call__(self, left, right, mask, value):
        length = self.length
        every = jnp.concatenate([left * only for only in self.lanes], 0)
        scores = dot_nt(every, right).astype(BF16)
        scores = [scores[h * length : (h + 1) * length] * mask for h in range(self.count)]
        values = jnp.concatenate([value * only for only in self.lanes], 0)
        total = dot(jnp.concatenate(scores, 1), values)
        return total


def attend(length, size, info, qa_in, kb_in, v_in, vb_in, g_in, ga_in, states, gq, gk, gv):
    core = info[1]
    pairs = Pairs(length, qa_in.shape[2], size)
    for j in range(2):
        qa, kb, v, vb, g, ga = qa_in[j], kb_in[j], v_in[j], vb_in[j], g_in[j], ga_in[j]
        later = (core if j == 0 else 1 - core).astype(F32)
        grad_q = pairs(ga, v, pairs.causal, kb) + later * dot_nt(ga, states[0, 1 - j])
        grad_k = pairs(vb, g, pairs.anti, qa) + (1.0 - later) * dot_nt(vb, states[1, 1 - j])
        grad_v = pairs(kb, qa, pairs.anti, g) + (1.0 - later) * dot(kb, states[1, 1 - j])
        gq[j], gk[j], gv[j] = grad_q.astype(BF16), grad_k.astype(BF16), grad_v.astype(BF16)


def finish(
    length, size, chips, info, rate, kb, vb, ga, qn_in, kn_in, qs, ks, rstd_in, gq, gk, gv,
    emb, gain, w_q, w_k, w_v, d_own, d_oth, *refs
):
    came, (before_out, row_keep, row_send) = refs[: chips - 1], refs[chips - 1 :]
    core, z = info[1], info[2]
    half = kb.shape[2]
    same_head = same_heads(half, size)
    mean_of = jnp.where(same_head, 1.0 / size, 0.0).astype(BF16)
    state = jnp.zeros((size, half), F32)
    back = jnp.zeros((size, half), F32)
    for m in range(1, chips):
        peer = z ^ m
        apart = jnp.abs(peer - z).astype(F32) * (2.0 * length)
        piece = came[m - 1][...].astype(F32) * jnp.exp(-rate[...] * apart)
        before = peer < z
        state = state + jnp.where(before, piece, 0.0)
        back = back + jnp.where(before, 0.0, piece)

    def spread(packed):
        return jnp.where(same_head, jnp.concatenate([packed] * (half // size), 0), 0.0).astype(BF16)

    state, back = spread(state), spread(back)
    before_out[...] = state
    keep_at = pl.multiple_of(core * half, half)
    mine_at = pl.ds(keep_at, half)
    send_at = pl.multiple_of((1 - core) * half, half)
    for j, d_ref in enumerate((d_own, d_oth)):
        side = core if j == 0 else 1 - core
        valid = valid_col(info, (2 * z + side) * length, length)
        grad_q = gq[j].astype(F32) + dot_nt(ga[j], state)
        grad_k = gk[j].astype(F32) + dot_nt(vb[j], back)
        grad_v = gv[j].astype(F32) + dot(kb[j], back)
        qn, kn = qn_in[j].astype(F32), kn_in[j].astype(F32)
        d_q = qs[j] * (grad_q - qn * dot((qn * grad_q).astype(BF16), mean_of))
        d_k = ks[j] * (grad_k - kn * dot((kn * grad_k).astype(BF16), mean_of))
        d_q, d_k, d_v = d_q.astype(BF16), d_k.astype(BF16), (grad_v * valid).astype(BF16)
        rstd = rstd_in[j]
        scaled = []
        total = jnp.zeros((length, 1), F32)
        for at in (keep_at, send_at):
            rows = pl.ds(at, half)
            weights = jnp.concatenate([w[rows, mine_at] for w in (w_q, w_k, w_v)], 1)
            d_normed = dot_nt(jnp.concatenate([d_q, d_k, d_v], 1), weights) * gain[:, rows]
            part = emb[j, :, rows].astype(F32)
            scaled.append((d_normed, part))
            total = total + jnp.sum(d_normed * part, axis=1, keepdims=True)
        pull = total * (rstd * rstd / (2 * half))
        kept = rstd * (scaled[0][0] - scaled[0][1] * pull)
        row_keep[j] = kept + d_ref[:, pl.ds(keep_at, half)].astype(F32) * valid
        row_send[1 - j] = (rstd * (scaled[1][0] - scaled[1][1] * pull)).astype(BF16)


def outward(length, size, info, qa_in, kb_in, v_in, states, before, att_own, att_oth):
    core = info[1]
    pairs = Pairs(length, qa_in.shape[2], size)
    for j, out in enumerate((att_own, att_oth)):
        qa = qa_in[j]
        later = (core if j == 0 else 1 - core).astype(F32)
        whole = pairs(qa, kb_in[j], pairs.causal, v_in[j]) + dot(qa, before[...])
        out[...] = (whole + later * dot(qa, states[0, 1 - j])).astype(BF16)


def compact(length, tables, cap, info, row_keep, row_came, dest, meta, *outs):
    for j in range(2):
        grads = (row_keep[j] + row_came[j].astype(F32)).astype(BF16)
        where_to = dest[j : j + 1, :]
        for m in range(tables):
            hit = iota((cap, length), 0) + m * cap == where_to
            hit = jnp.where(hit, 1.0, 0.0).astype(BF16)
            outs[m][j * cap : (j + 1) * cap, :] = dot(hit, grads).astype(BF16)
    for m in range(tables):
        outs[m][2 * cap : 2 * cap + 16, :] = jnp.zeros((16, outs[m].shape[1]), BF16)
        outs[m][2 * cap : 2 * cap + 16, 0:cap] = meta[m]


def result(info, emb, att_own, att_came, w_out, out):
    core = info[1]
    half = att_own.shape[1]
    own = pl.ds(pl.multiple_of(core * half, half), half)
    other = pl.ds(pl.multiple_of((1 - core) * half, half), half)
    total = dot(att_own[...], w_out[own, :]) + dot(att_came[...], w_out[other, :])
    out[...] = (emb[0].astype(F32) + total).astype(BF16)


def row_sums(rows, cap, refs):
    total = None
    for ref in refs:
        coded = ref[2 * cap : 2 * cap + 16, 0:cap].astype(F32)
        hits = []
        for j in range(2):
            high, low = coded[2 * j : 2 * j + 1, :], coded[2 * j + 1 : 2 * j + 2, :]
            number = ((high - 1.0) * 32.0 + low).astype(jnp.int32)
            hits.append(jnp.where(iota((rows, cap), 0) == number, 1.0, 0.0).astype(BF16))
        if cap % 128 == 0:
            parts = [dot(jnp.concatenate(hits, 1), ref[: 2 * cap, :])]
        else:
            parts = [dot(hit, ref[j * cap : (j + 1) * cap, :]) for j, hit in enumerate(hits)]
        for part in parts:
            total = part if total is None else total + part
    return total


def early_sum(rows, cap, info, *refs):
    refs[-1][...] = row_sums(rows, cap, refs[:-1])


def owner_sum(rows, cap, chips, count, info, early, *refs):
    came, outs, acc = refs[:count], refs[count : count + chips], refs[count + chips]
    z = info[2]
    acc[...] = early[...] + row_sums(rows, cap, came)
    share = rows // chips
    for m in range(chips):
        at = pl.multiple_of((z ^ m) * share, share)
        outs[m][...] = acc[pl.ds(at, share), :].astype(BF16)


def add_up(chips, info, *refs):
    total = refs[0][...].astype(F32)
    for m in range(1, chips):
        total = total + refs[m][...].astype(F32)
    refs[chips][...] = total.astype(BF16)


def assemble(chips, share, half, info, *refs):
    own, other, (out, held, sems) = refs[:chips], refs[chips : 2 * chips], refs[2 * chips :]
    core, z = info[1], info[2]
    copies = []
    for m in range(chips):
        rows = pl.ds(pl.multiple_of((z ^ m) * share, share), share)
        for ref, side in ((own[m], core), (other[m], 1 - core)):
            held[m, :, pl.ds(pl.multiple_of(side * half, half), half)] = ref[...]
        copies.append(pltpu.make_async_copy(held.at[m], out.at[rows, :], sems.at[m]))
        copies[-1].start()
    for copy in copies:
        copy.wait()


def local(
    item_local, item_owner, hist_len, table, gain, w_query, w_key, w_value, w_out, rate, d_out
):
    tables = lax.axis_size("table")
    count = lax.axis_size("ctx")
    length = item_local.shape[1]
    rows, width = table.shape
    heads = rate.shape[0]
    size = width // heads
    half = width // 2
    chips = count // 2
    cap = 2 * length // tables
    mine = lax.axis_index("table")
    block = lax.axis_index("ctx")
    core = block % 2
    z = block // 2

    def over_table(x, m):
        return lax.ppermute(x, "table", [(i, i ^ m) for i in range(tables)])

    def over_z(x, m):
        return lax.ppermute(x, "ctx", [(i, i ^ (2 * m)) for i in range(count)])

    def swap(x):
        return lax.ppermute(x, "ctx", [(i, i ^ 1) for i in range(count)])

    def array(shape, dtype):
        return jax.ShapeDtypeStruct(shape, dtype)

    info = jnp.stack([mine, core, z, hist_len[0]]).astype(jnp.int32)
    part = rows // 2
    first, second = pl.pallas_call(
        functools.partial(pick, part),
        in_specs=[pl.BlockSpec(memory_space=pl.ANY)],
        out_specs=[pl.BlockSpec(memory_space=pltpu.VMEM)] * 2,
        out_shape=[pltpu.VMEM((part, width), BF16)] * 2,
        scratch_shapes=[pltpu.SemaphoreType.DMA((2,))],
        name="pick",
    )(table)

    def from_mask(x, masks):
        return lax.ppermute(
            x,
            ("table", "ctx"),
            [
                (t * count + c, (t ^ masks[c % 2]) * count + c)
                for t in range(tables)
                for c in range(count)
            ],
        )

    ids = item_owner[:, :, 0] * rows + item_local
    ids_row = jnp.concatenate([ids, swap(ids)], 0)
    ids_col = ids_row[:, :, None]
    if tables == 4:
        near = from_mask(first, (1, 2))
        rest = from_mask(second, (1, 2))
        far = from_mask(lax.optimization_barrier((near, ids_row))[0], (2, 1))
        fetched = [(near, (1, 2), (0, 1)), (rest, (1, 2), (1, 0)), (far, (3, 3), (0, 1))]
        early = fetched[:1]
    else:
        fetched = [(over_table(first, m), (m, m), (0, 1)) for m in range(1, tables)]
        early = []
    late = fetched[len(early) :]
    early = [(first, (0, 0), (0, 1)), (second, (0, 0), (1, 0)), *early]

    d_own = d_out[0]
    d_oth = swap(d_own)
    g, ga, dest, meta, emb_own, falling, rising, rate_row, gain_row, w_here, d_here = call(
        functools.partial(prepare, length, tables, rows, cap, size, [x[1:] for x in early]),
        info,
        (d_oth, ids_col, ids_row, *[x[0] for x in early]),
        [
            array((2, length, half), BF16),
            array((2, length, half), BF16),
            array((2, length), jnp.int32),
            array((tables, 16, cap), BF16),
            array((2, length, width), BF16),
            array((2, length, half), F32),
            array((2, length, half), F32),
            array((1, half), F32),
            array((1, width), F32),
            array((width, width), BF16),
            array((length, width), BF16),
        ],
        4 * length * width * half,
        "prepare",
        away=(rate[None, :], w_out, d_own, gain[None, :]),
        scratch=[pltpu.VMEM((1, heads), F32), pltpu.SemaphoreType.DMA((4,))],
    )
    others = [swap(fetched[0][0])]
    others += [swap(lax.optimization_barrier((x, meta))[0]) for x, _, _ in fetched[1:]]
    late += [(x, m[::-1], h[::-1]) for x, (_, m, h) in zip(others, fetched)]
    bits = max(chips - 1, 1).bit_length() if chips > 1 else 0
    emb, v, qa, kb, vb, qn, kn, qs, ks, rstd, states, *sends = call(
        functools.partial(project, length, [x[1:] for x in late], rows, size, chips),
        info,
        (ids_col, gain_row, w_query, w_key, w_value, g, falling, rising, emb_own, *[x[0] for x in late]),
        [array((2, length, width), BF16)]
        + [array((2, length, half), BF16)] * 6
        + [array((2, length, half), F32)] * 2
        + [array((2, length, 1), F32), array((2, 2, half, half), BF16)]
        + [array((size, half), BF16)] * bits,
        4 * length * tables * rows * width,
        "project",
    )
    came = [over_z(sends[m.bit_length() - 1], m) for m in range(1, chips)]
    gq, gk, gv = call(
        functools.partial(attend, length, size),
        info,
        (qa, kb, v, vb, g, ga, states),
        [array((2, length, half), BF16)] * 3,
        24 * length * length * half,
        "attend",
    )
    before, row_keep, row_send = call(
        functools.partial(finish, length, size, chips),
        info,
        (rate_row, kb, vb, ga, qn, kn, qs, ks, rstd, gq, gk, gv, emb, gain_row, w_query, w_key, w_value,
         d_here, d_oth, *came),
        [
            array((half, half), BF16),
            array((2, length, half), F32),
            array((2, length, half), BF16),
        ],
        12 * length * width * half,
        "finish",
    )
    row_came = swap(row_send)
    outgoing = call(
        functools.partial(compact, length, tables, cap),
        info,
        (row_keep, row_came, dest, meta),
        [array((2 * cap + 16, half), BF16)] * tables,
        4 * length * 2 * length * half,
        "compact",
    )
    arrived = [over_table(outgoing[m], m) for m in range(1, tables)]
    arrived[0], before = lax.optimization_barrier((arrived[0], before))
    (early,) = call(
        functools.partial(early_sum, rows, cap),
        info,
        (outgoing[0], arrived[0]),
        [array((rows, half), F32)],
        8 * rows * length * half,
        "early_sum",
    )
    att_own, att_oth = call(
        functools.partial(outward, length, size),
        info,
        (qa, kb, v, states, before),
        [array((length, half), BF16)] * 2,
        8 * length * length * half,
        "outward",
    )
    share = rows // chips
    early, att_oth = lax.optimization_barrier((early, att_oth))
    att_came = swap(att_oth)
    everything = call(
        functools.partial(owner_sum, rows, cap, chips, tables - 2),
        info,
        (early, *arrived[1:]),
        [array((share, half), BF16)] * chips,
        8 * rows * length * (tables - 2) * half,
        "owner_sum",
        None,
        [pltpu.VMEM((rows, half), F32)],
    )
    pieces = [over_z(everything[m], m) for m in (*range(chips - 1, chips), *range(1, chips - 1)) if m]
    if pieces:
        pieces[0], att_came = lax.optimization_barrier((pieces[0], att_came))
    (output,) = call(
        result,
        info,
        (emb, att_own, att_came, w_here),
        [array((length, width), BF16)],
        2 * length * width * width,
        "result",
        pltpu.VMEM,
    )
    pieces, output = lax.optimization_barrier((pieces, output))
    pieces = [everything[0]] + pieces
    (summed,) = call(
        functools.partial(add_up, chips),
        info,
        pieces,
        [array((share, half), BF16)],
        chips * share * half,
        "add_up",
    )
    own = [summed] + [over_z(summed, m) for m in range(1, chips)]
    other = [swap(x) for x in own]
    (table_grad,) = call(
        functools.partial(assemble, chips, share, half),
        info,
        [*own, *other],
        [array((rows, width), BF16)],
        rows * width,
        "assemble",
        pl.ANY,
        [pltpu.VMEM((chips, share, width), BF16), pltpu.SemaphoreType.DMA((chips,))],
    )
    return (output[None], table_grad)


def solution(mesh):
    return jax.shard_map(
        local,
        mesh=mesh,
        in_specs=(
            P("table", "ctx"),
            P("table", "ctx", None),
            P("table"),
            P("table", None),
            P(),
            P(),
            P(),
            P(),
            P(),
            P(),
            P("table", "ctx", None),
        ),
        out_specs=(P("table", "ctx", None), P("table", None)),
        check_vma=False,
    )
```
